512 devices in a mesh: leaf: 512 (over y, x, z, core).
Axes of the slice: x: 4, y: 4, z: 16, core: 2. Of those that a mesh axis runs over, the one named last changes fastest.
Arguments:
- vectors: float32 [512, 512, 128], P('leaf'), may hold values from -6 to 6
- points: float32 [512, 3, 512], P('leaf')
- leaf_basis: float32 [512, 512, 128], P('leaf'), may hold values from -0.25 to 0.25
- transfer_leaf: float32 [512, 128, 128], P('leaf'), may hold values from -0.5 to 0.5
- transfer_pair: float32 [32768, 128], P('leaf'), may hold values from -0.5 to 0.5
- transfer_quad: float32 [16384, 128], P('leaf'), may hold values from -0.5 to 0.5
- skel_leaf: float32 [512, 3, 128], P('leaf')
- skel_pair: float32 [256, 3, 128], replicated
- skel_quad: float32 [128, 3, 128], replicated
- skel_top: float32 [64, 3, 128], replicated
- near_list: int32 [512, 16], P('leaf'), may hold values from -1 to 511, as said below
- far_leaf: int32 [512, 8], P('leaf'), may hold values from -1 to 511, as said below
- far_pair: int32 [256, 8], replicated, may hold values from -1 to 255, as said below
- far_quad: int32 [128, 8], replicated, may hold values from -1 to 127, as said below
- far_top: int32 [64, 8], replicated, may hold values from -1 to 63, as said below
Outputs:
- product: float32 [512, 512, 128], P('leaf')
The draws below stay inside these ranges and needn't reach their ends.
Inputs may be any that keep to these rules, and one draw needn't show every extreme that they name: `near_list`: entry 0 of row l is l; the other entries are distinct leaves within 8 of l, or -1 for an unused slot. `far_leaf`: distinct leaves within 8 of the row's leaf, none of them in that leaf's row of near_list, or -1 for an unused slot. `far_pair`: distinct clusters within 4 of the row's cluster and other than it, or -1 for an unused slot. `far_quad`: distinct clusters within 4 of the row's cluster and other than it, or -1 for an unused slot. `far_top`: distinct top clusters other than the row's cluster, or -1 for an unused slot.
All inputs are finite; a program needn't handle non-finite values.
Results may differ from the reference program's by a relative error of at most 0.0003.
Values sent between devices are 32-bit elements; how exact they have to be, the bound alone decides.
A program may use at most 64 MiB of HBM per device.

```python
import jax
import jax.numpy as jnp
from jax import lax

LEAF = 512
RANK = 128
NVEC = 128
NEAR = 16
FAR = 8
REACH = 8
FAR_REACH = 4
LEAVES = 512


def corner_of(leaf_ids):
    first = jnp.zeros(leaf_ids.shape, jnp.float32)
    second = jnp.zeros(leaf_ids.shape, jnp.float32)
    third = jnp.zeros(leaf_ids.shape, jnp.float32)
    for bit_index in range(15):
        digit = (leaf_ids // 2 ** bit_index % 2).astype(jnp.float32) * float(2 ** (bit_index // 3))
        if bit_index % 3 == 0:
            first = first + digit
        elif bit_index % 3 == 1:
            second = second + digit
        else:
            third = third + digit
    return jnp.stack([first, second, third], axis=-2)


def draw_points(key, part):
    corners = corner_of(jnp.arange(LEAVES)[:, None])
    return corners + jax.random.uniform(key, (LEAVES, 3, LEAF), jnp.float32)


def skeleton_draw(key, level):
    clusters = LEAVES // 2 ** level
    first_key, second_key = jax.random.split(jax.random.fold_in(key, 31 + level))
    common = 8.0 * jax.random.uniform(first_key, (1, 3, RANK), jnp.float32)
    jitter = 0.15 * jax.random.uniform(second_key, (clusters, 3, RANK), jnp.float32)
    return common + jitter


def draw_skel_leaf(key, part):
    return skeleton_draw(key, 0)


def draw_skel_pair(key, part):
    return skeleton_draw(key, 1)


def draw_skel_quad(key, part):
    return skeleton_draw(key, 2)


def draw_skel_top(key, part):
    return skeleton_draw(key, 3)


def shuffled_offsets(key, rows, reach):
    offsets = jnp.concatenate([jnp.arange(-reach, 0), jnp.arange(1, reach + 1)]).astype(jnp.int32)
    scores = jax.random.randint(key, (rows, 2 * reach), 0, 1 << 20) * (2 * reach) + jnp.arange(2 * reach)[None, :]
    return offsets[jnp.argsort(scores, axis=1)]


def leaf_lists(key):
    first_key, second_key = jax.random.split(jax.random.fold_in(key, 11))
    chosen = shuffled_offsets(first_key, LEAVES, REACH)
    leaf_ids = jnp.arange(LEAVES).astype(jnp.int32)
    near_count = jax.random.randint(second_key, (LEAVES,), 1, NEAR + 1)
    near_count = jnp.where(leaf_ids % 5 == 0, NEAR, jnp.where(leaf_ids % 5 == 1, 1, near_count))
    targets = leaf_ids[:, None] + chosen
    inside = (targets >= 0) & (targets < LEAVES)
    slot_ids = jnp.arange(2 * REACH)[None, :]
    near_rest = jnp.where((slot_ids < near_count[:, None] - 1) & inside, targets, -1)[:, :NEAR - 1]
    near_rows = jnp.concatenate([leaf_ids[:, None], near_rest], axis=1)
    source = near_count[:, None] - 1 + jnp.arange(FAR)[None, :]
    bounded = jnp.minimum(source, 2 * REACH - 1)
    picked = jnp.take_along_axis(targets, bounded, axis=1)
    picked_inside = jnp.take_along_axis(inside, bounded, axis=1)
    far_rows = jnp.where((source < 2 * REACH) & picked_inside, picked, -1)
    return (near_rows.astype(jnp.int32), far_rows.astype(jnp.int32))


def draw_near_list(key, part):
    return leaf_lists(key)[0]


def draw_far_leaf(key, part):
    return leaf_lists(key)[1]


def cluster_lists(key, level):
    clusters = LEAVES // 2 ** level
    first_key, second_key = jax.random.split(jax.random.fold_in(key, 51 + level))
    chosen = shuffled_offsets(first_key, clusters, FAR_REACH)[:, :FAR]
    cluster_ids = jnp.arange(clusters).astype(jnp.int32)
    counts = jax.random.randint(second_key, (clusters,), 1, FAR + 1)
    counts = jnp.where(cluster_ids % 5 == 0, FAR, counts)
    targets = cluster_ids[:, None] + chosen
    inside = (targets >= 0) & (targets < clusters)
    slot_ids = jnp.arange(FAR)[None, :]
    return jnp.where((slot_ids < counts[:, None]) & inside, targets, -1).astype(jnp.int32)


def draw_far_pair(key, part):
    return cluster_lists(key, 1)


def draw_far_quad(key, part):
    return cluster_lists(key, 2)


def draw_far_top(key, part):
    clusters = LEAVES // 8
    most = min(FAR, clusters - 1)
    first_key, second_key = jax.random.split(jax.random.fold_in(key, 77))
    offsets = jnp.arange(1, clusters).astype(jnp.int32)
    scores = jax.random.randint(first_key, (clusters, clusters - 1), 0, 1 << 20) * clusters + jnp.arange(clusters - 1)[None, :]
    chosen = offsets[jnp.argsort(scores, axis=1)][:, :most]
    cluster_ids = jnp.arange(clusters).astype(jnp.int32)
    counts = jax.random.randint(second_key, (clusters,), 1, most + 1)
    counts = jnp.where(cluster_ids % 5 == 0, most, counts)
    slot_ids = jnp.arange(most)[None, :]
    entries = jnp.where(slot_ids < counts[:, None], (cluster_ids[:, None] + chosen) % clusters, -1)
    padding = jnp.full((clusters, FAR - most), -1, jnp.int32)
    return jnp.concatenate([entries.astype(jnp.int32), padding], axis=1)


def level_of(rng, shape, shards, smallest, largest):
    def one(axis_at, shards_of):
        draws = jax.random.uniform(jax.random.fold_in(jax.random.fold_in(rng, 6), axis_at), (shards_of,), jnp.float32, smallest / len(shards), largest / len(shards))
        return jnp.repeat(jnp.exp(draws), shape[axis_at] // shards_of).reshape((-1,) + (1,) * (len(shape) - axis_at - 1))

    loudness = one(*shards[0])
    for cut in shards[1:]:
        loudness = loudness * one(*cut)
    return loudness


def gaussian(rng, dims, scale, bound, shards=(), kind=jnp.bfloat16):
    values = scale * jax.random.normal(rng, dims, jnp.float32)
    if shards:
        values = values * level_of(rng, dims, shards, -0.22, 0.18)
    return jnp.clip(values, -bound, bound).astype(kind)


def setup_inputs(seed: int = 0) -> dict:
    arg_keys = jax.random.split(jax.random.key(seed), 16)
    return {
        "vectors": gaussian(arg_keys[0], (LEAVES, LEAF, NVEC), 1.0, 6.0, ((0, 512),), jnp.float32),
        "points": draw_points(jax.random.fold_in(arg_keys[15], 71), 0),
        "leaf_basis": gaussian(arg_keys[2], (LEAVES, LEAF, RANK), LEAF ** -0.5, 0.25, ((0, 512),), jnp.float32),
        "transfer_leaf": gaussian(arg_keys[3], (LEAVES, RANK, RANK), RANK ** -0.5, 0.5, ((0, 512),), jnp.float32),
        "transfer_pair": gaussian(arg_keys[4], (LEAVES // 2 * RANK, RANK), RANK ** -0.5, 0.5, ((0, 512),), jnp.float32),
        "transfer_quad": gaussian(arg_keys[5], (LEAVES // 4 * RANK, RANK), RANK ** -0.5, 0.5, ((0, 512),), jnp.float32),
        "skel_leaf": draw_skel_leaf(jax.random.fold_in(arg_keys[15], 71), 0),
        "skel_pair": draw_skel_pair(jax.random.fold_in(arg_keys[15], 71), 0),
        "skel_quad": draw_skel_quad(jax.random.fold_in(arg_keys[15], 71), 0),
        "skel_top": draw_skel_top(jax.random.fold_in(arg_keys[15], 71), 0),
        "near_list": draw_near_list(jax.random.fold_in(arg_keys[15], 71), 0),
        "far_leaf": draw_far_leaf(jax.random.fold_in(arg_keys[15], 71), 0),
        "far_pair": draw_far_pair(jax.random.fold_in(arg_keys[15], 71), 0),
        "far_quad": draw_far_quad(jax.random.fold_in(arg_keys[15], 71), 0),
        "far_top": draw_far_top(jax.random.fold_in(arg_keys[15], 71), 0),
    }


INV_FOUR_PI = 0.07957747154594767
DELTA_SQ = 0.01
HIGHEST = lax.Precision.HIGHEST

def kernel_block(left_pts, right_pts):
    distance = jnp.zeros((left_pts.shape[1], right_pts.shape[1]), jnp.float32)
    for axis_id in range(3):
        offset_gap = left_pts[axis_id][:, None] - right_pts[axis_id][None, :]
        distance = distance + offset_gap * offset_gap
    return INV_FOUR_PI * lax.rsqrt(distance + DELTA_SQ)

def listed_sum(own_coords, entries, coords_all, values_all, width):

    def advance(running, partner):
        chosen = jnp.maximum(partner, 0)
        contrib = jnp.dot(kernel_block(own_coords, coords_all[chosen]), values_all[chosen], precision=HIGHEST)
        return (running + jnp.where(partner >= 0, contrib, 0.0), None)
    start_value = jnp.zeros((own_coords.shape[1], width), jnp.float32)
    result, _ = lax.scan(advance, start_value, entries)
    return result

def far_level(skeletons, lists, coefs):
    width = coefs.shape[2]

    def single(cluster):
        return listed_sum(skeletons[cluster], lists[cluster], skeletons, coefs, width)
    return lax.map(single, jnp.arange(skeletons.shape[0]))

def reference(vectors, points, leaf_basis, transfer_leaf, transfer_pair, transfer_quad, skel_leaf, skel_pair, skel_quad, skel_top, near_list, far_leaf, far_pair, far_quad, far_top):
    width = vectors.shape[2]

    def near_single(leaf_id):
        return listed_sum(points[leaf_id], near_list[leaf_id], points, vectors, width)
    near_field = lax.map(near_single, jnp.arange(vectors.shape[0]))
    pair_mats = transfer_pair.reshape(-1, RANK, RANK)
    quad_mats = transfer_quad.reshape(-1, RANK, RANK)
    coef_leaf = jnp.einsum('lpr,lpv->lrv', leaf_basis, vectors, precision=HIGHEST)
    coef_pair = jnp.einsum('lrs,lrv->lsv', transfer_leaf, coef_leaf, precision=HIGHEST).reshape(-1, 2, RANK, width).sum(axis=1)
    coef_quad = jnp.einsum('crs,crv->csv', pair_mats, coef_pair, precision=HIGHEST).reshape(-1, 2, RANK, width).sum(axis=1)
    coef_top = jnp.einsum('crs,crv->csv', quad_mats, coef_quad, precision=HIGHEST).reshape(-1, 2, RANK, width).sum(axis=1)
    local_top = far_level(skel_top, far_top, coef_top)
    local_quad = far_level(skel_quad, far_quad, coef_quad) + jnp.einsum('crs,csv->crv', quad_mats, jnp.repeat(local_top, 2, axis=0), precision=HIGHEST)
    local_pair = far_level(skel_pair, far_pair, coef_pair) + jnp.einsum('crs,csv->crv', pair_mats, jnp.repeat(local_quad, 2, axis=0), precision=HIGHEST)
    local_leaf = far_level(skel_leaf, far_leaf, coef_leaf) + jnp.einsum('crs,csv->crv', transfer_leaf, jnp.repeat(local_pair, 2, axis=0), precision=HIGHEST)
    return near_field + jnp.einsum('lpr,lrv->lpv', leaf_basis, local_leaf, precision=HIGHEST)
```

```python
import jax
import jax.numpy as jnp
from jax import lax
from jax.sharding import Mesh
from jax.sharding import PartitionSpec as P

REACH = 8
FAR_REACH = 4


INV_FOUR_PI = 0.07957747154594767
DELTA_SQ = 0.01
HIGHEST = lax.Precision.HIGHEST

AX = ("cl", "q", "p", "c")
MEMBERS = ("q", "p", "c")


def from_partner(value, axis, bit):
    mask = 2**bit
    pairs = [(source, source ^ mask) for source in range(lax.axis_size(axis))]
    return lax.ppermute(value, axis, pairs)


def from_behind(block, axis, distance):
    devices = range(lax.axis_size(axis))
    route = [(i - distance, i) for i in devices if i - distance in devices]
    return lax.ppermute(block, axis, route)


def kernel_block(left_pts, right_pts):
    distance = jnp.zeros((left_pts.shape[1], right_pts.shape[1]), jnp.float32)
    for axis_id in range(3):
        offset_gap = left_pts[axis_id][:, None] - right_pts[axis_id][None, :]
        distance = distance + offset_gap * offset_gap
    return INV_FOUR_PI * lax.rsqrt(distance + DELTA_SQ)


def transposed_dot(matrix, values):
    return lax.dot_general(matrix, values, (((0,), (0,)), ((), ())), precision=HIGHEST)


def listed_sum(own_coords, entries, fetcher, width):

    def advance(running, partner):
        coords, values = fetcher(jnp.maximum(partner, 0))
        contrib = jnp.dot(kernel_block(own_coords, coords), values, precision=HIGHEST)
        return (running + jnp.where(partner >= 0, contrib, 0.0), None)

    start_value = jnp.zeros((own_coords.shape[1], width), jnp.float32)
    result, _ = lax.scan(advance, start_value, entries)
    return result


def batched_far(own_coords, coords, values, valid):
    count, _, span = coords.shape
    right = jnp.transpose(coords, (1, 0, 2)).reshape(3, count * span)
    masked = jnp.where(valid[:, None, None], values, 0.0)
    flat = masked.reshape(count * span, values.shape[2])
    return jnp.dot(kernel_block(own_coords, right), flat, precision=HIGHEST)


def pair_total(partial_value, levels):
    for bit_index in range(levels):
        partial_value = partial_value + from_partner(partial_value, AX, bit_index)
    return partial_value


def join_rows(block, levels, device):
    for bit_index in range(levels):
        other = from_partner(block, AX, bit_index)
        upper = device // 2**bit_index % 2
        block = jnp.where(
            upper == 0, jnp.concatenate([block, other], 0), jnp.concatenate([other, block], 0)
        )
    return block


def window(shipped):
    gathered = []
    for distance in range(-REACH, REACH + 1):
        if distance == 0:
            gathered.append(shipped)
        else:
            gathered.append(from_behind(shipped, AX, -distance))
    return jnp.stack(gathered)


def partner_stack(coefs, stride):
    gathered = []
    for offset in list(range(-FAR_REACH, 0)) + list(range(1, FAR_REACH + 1)):
        gathered.append(from_behind(coefs, AX, -offset * stride))
    stacked = jnp.stack(gathered)

    def slot_of(distance):
        return distance + FAR_REACH - (distance > 0).astype(jnp.int32)

    return (stacked, slot_of)


def middle_level(coefs, skeletons, lists, transfer_rows, above, stride, device):
    rank_rows = coefs.shape[0] // stride
    cluster = device // stride
    member = device % stride
    own_full = lax.dynamic_index_in_dim(skeletons, cluster, 0, keepdims=False)
    own_coords = lax.dynamic_slice_in_dim(own_full, member * rank_rows, rank_rows, 1)
    stacked, slot_of = partner_stack(coefs, stride)
    entries = lax.dynamic_index_in_dim(lists, cluster, 0, keepdims=False)
    chosen = jnp.maximum(entries, 0)
    coords = jnp.take(skeletons, chosen, axis=0)
    slots = jnp.clip(slot_of(chosen - cluster), 0, stacked.shape[0] - 1)
    values = jnp.take(stacked, slots, axis=0)
    rows_here = batched_far(own_coords, coords, values, entries >= 0) + jnp.dot(
        transfer_rows, above, precision=HIGHEST
    )
    return join_rows(rows_here, stride.bit_length() - 1, device)


def per_device(
    vectors,
    points,
    leaf_basis,
    transfer_leaf,
    transfer_pair,
    transfer_quad,
    skel_leaf,
    skel_pair,
    skel_quad,
    skel_top,
    near_list,
    far_leaf,
    far_pair,
    far_quad,
    far_top,
):
    leaf_points = vectors.shape[1]
    width = vectors.shape[2]
    rank = leaf_basis.shape[2]
    device = lax.axis_index(AX)
    own_points = points[0]
    shipped = jnp.concatenate(
        [vectors[0], own_points.reshape(3 * leaf_points // width, width)], axis=0
    )
    near_rim = window(shipped)

    def near_fetch(partner):
        position = jnp.clip(partner - device + REACH, 0, 2 * REACH)
        block = lax.dynamic_index_in_dim(near_rim, position, 0, keepdims=False)
        return (block[leaf_points:].reshape(3, leaf_points), block[:leaf_points])

    near_field = listed_sum(own_points, near_list[0], near_fetch, width)
    coef_leaf = transposed_dot(leaf_basis[0], vectors[0])
    coef_pair = pair_total(transposed_dot(transfer_leaf[0], coef_leaf), 1)
    pair_rows = lax.dynamic_slice_in_dim(coef_pair, device % 2 * (rank // 2), rank // 2, 0)
    coef_quad = pair_total(transposed_dot(transfer_pair, pair_rows), 2)
    quad_rows = lax.dynamic_slice_in_dim(coef_quad, device % 4 * (rank // 4), rank // 4, 0)
    coef_top = pair_total(transposed_dot(transfer_quad, quad_rows), 3)
    top_cluster = device // 8
    top_member = device % 8
    share = width // 8
    top_cols_own = lax.dynamic_slice_in_dim(coef_top, top_member * share, share, 1)
    all_top = lax.all_gather(top_cols_own, "cl", axis=0)
    top_coords = lax.dynamic_index_in_dim(skel_top, top_cluster, 0, keepdims=False)
    top_entries = lax.dynamic_index_in_dim(far_top, top_cluster, 0, keepdims=False)
    top_chosen = jnp.maximum(top_entries, 0)
    top_cols = batched_far(
        top_coords,
        jnp.take(skel_top, top_chosen, axis=0),
        jnp.take(all_top, top_chosen, axis=0),
        top_entries >= 0,
    )
    local_top = lax.all_gather(top_cols, MEMBERS, axis=1, tiled=True)
    local_quad = middle_level(coef_quad, skel_quad, far_quad, transfer_quad, local_top, 4, device)
    local_pair = middle_level(coef_pair, skel_pair, far_pair, transfer_pair, local_quad, 2, device)
    leaf_ship = jnp.concatenate([coef_leaf, skel_leaf[0]], axis=0)
    leaf_rim = window(leaf_ship)
    leaf_entries = far_leaf[0]
    positions = jnp.clip(jnp.maximum(leaf_entries, 0) - device + REACH, 0, 2 * REACH)
    leaf_blocks = jnp.take(leaf_rim, positions, axis=0)
    local_leaf = batched_far(
        skel_leaf[0], leaf_blocks[:, rank:], leaf_blocks[:, :rank], leaf_entries >= 0
    ) + jnp.dot(transfer_leaf[0], local_pair, precision=HIGHEST)
    product = near_field + jnp.dot(leaf_basis[0], local_leaf, precision=HIGHEST)
    return product[None]


def solution(mesh):
    count = mesh.devices.size
    grid = Mesh(mesh.devices.reshape(count // 8, 2, 2, 2), AX)
    spread = P(AX, None, None)
    rows = P(AX, None)
    placed = (
        spread,
        spread,
        spread,
        spread,
        rows,
        rows,
        spread,
        P(),
        P(),
        P(),
        rows,
        rows,
        P(),
        P(),
        P(),
    )
    return jax.shard_map(per_device, mesh=grid, in_specs=placed, out_specs=spread, check_vma=False)
```

```python
import jax
import jax.numpy as jnp
from jax import lax
from jax.sharding import Mesh
from jax.sharding import PartitionSpec as P

REACH = 8
FAR_REACH = 4


INV_FOUR_PI = 0.07957747154594767
DELTA_SQ = 0.01
HIGHEST = lax.Precision.HIGHEST

AX = ("cl", "q", "p", "c")
MEMBERS = ("q", "p", "c")


def from_partner(value, axis, bit):
    mask = 2**bit
    pairs = [(source, source ^ mask) for source in range(lax.axis_size(axis))]
    return lax.ppermute(value, axis, pairs)


def from_behind(block, axis, distance):
    devices = range(lax.axis_size(axis))
    route = [(i - distance, i) for i in devices if i - distance in devices]
    return lax.ppermute(block, axis, route)


def kernel_block(left_pts, right_pts):
    distance = jnp.zeros((left_pts.shape[1], right_pts.shape[1]), jnp.float32)
    for axis_id in range(3):
        offset_gap = left_pts[axis_id][:, None] - right_pts[axis_id][None, :]
        distance = distance + offset_gap * offset_gap
    return INV_FOUR_PI * lax.rsqrt(distance + DELTA_SQ)


def transposed_dot(matrix, values):
    return lax.dot_general(matrix, values, (((0,), (0,)), ((), ())), precision=HIGHEST)


def listed_sum(own_coords, entries, fetcher, width):

    def advance(running, partner):
        coords, values = fetcher(jnp.maximum(partner, 0))
        contrib = jnp.dot(kernel_block(own_coords, coords), values, precision=HIGHEST)
        return (running + jnp.where(partner >= 0, contrib, 0.0), None)

    start_value = jnp.zeros((own_coords.shape[1], width), jnp.float32)
    result, _ = lax.scan(advance, start_value, entries)
    return result


def batched_far(own_coords, coords, values, valid):
    count, _, span = coords.shape
    right = jnp.transpose(coords, (1, 0, 2)).reshape(3, count * span)
    masked = jnp.where(valid[:, None, None], values, 0.0)
    flat = masked.reshape(count * span, values.shape[2])
    return jnp.dot(kernel_block(own_coords, right), flat, precision=HIGHEST)


def pair_total(partial_value, levels):
    for bit_index in range(levels):
        partial_value = partial_value + from_partner(partial_value, AX, bit_index)
    return partial_value


def join_rows(block, levels, device):
    for bit_index in range(levels):
        other = from_partner(block, AX, bit_index)
        upper = device // 2**bit_index % 2
        block = jnp.where(
            upper == 0, jnp.concatenate([block, other], 0), jnp.concatenate([other, block], 0)
        )
    return block


def window(shipped):
    gathered = []
    for distance in range(-REACH, REACH + 1):
        if distance == 0:
            gathered.append(shipped)
        else:
            gathered.append(from_behind(shipped, AX, -distance))
    return jnp.stack(gathered)


def partner_stack(coefs, stride):
    gathered = []
    for offset in list(range(-FAR_REACH, 0)) + list(range(1, FAR_REACH + 1)):
        gathered.append(from_behind(coefs, AX, -offset * stride))
    stacked = jnp.stack(gathered)

    def slot_of(distance):
        return distance + FAR_REACH - (distance > 0).astype(jnp.int32)

    return (stacked, slot_of)


def middle_level(coefs, skeletons, lists, transfer_rows, above, stride, device):
    rank_rows = coefs.shape[0] // stride
    cluster = device // stride
    member = device % stride
    own_full = lax.dynamic_index_in_dim(skeletons, cluster, 0, keepdims=False)
    own_coords = lax.dynamic_slice_in_dim(own_full, member * rank_rows, rank_rows, 1)
    stacked, slot_of = partner_stack(coefs, stride)
    entries = lax.dynamic_index_in_dim(lists, cluster, 0, keepdims=False)
    chosen = jnp.maximum(entries, 0)
    coords = jnp.take(skeletons, chosen, axis=0)
    slots = jnp.clip(slot_of(chosen - cluster), 0, stacked.shape[0] - 1)
    values = jnp.take(stacked, slots, axis=0)
    rows_here = batched_far(own_coords, coords, values, entries >= 0) + jnp.dot(
        transfer_rows, above, precision=HIGHEST
    )
    return join_rows(rows_here, stride.bit_length() - 1, device)


def cluster_gather(block, device, clusters):
    gathered = block[None]
    for level in range(clusters.bit_length() - 1):
        bit_index = 3 + level
        other = from_partner(gathered, AX, bit_index)
        upper = device // 2**bit_index % 2
        gathered = jnp.where(
            upper == 0,
            jnp.concatenate([gathered, other], 0),
            jnp.concatenate([other, gathered], 0),
        )
    return gathered


def near_sum(own_points, near_entries, shipped, device):
    leaf_points = own_points.shape[1]
    total = None
    for distance in range(-REACH, REACH + 1):
        block = shipped if distance == 0 else from_behind(shipped, AX, -distance)
        listed = jnp.any(near_entries == device + distance)
        coords = block[leaf_points:].reshape(3, leaf_points)
        contrib = jnp.dot(kernel_block(own_points, coords), block[:leaf_points], precision=HIGHEST)
        contrib = jnp.where(listed, contrib, 0.0)
        total = contrib if total is None else total + contrib
    return total


def per_device(
    vectors,
    points,
    leaf_basis,
    transfer_leaf,
    transfer_pair,
    transfer_quad,
    skel_leaf,
    skel_pair,
    skel_quad,
    skel_top,
    near_list,
    far_leaf,
    far_pair,
    far_quad,
    far_top,
):
    leaf_points = vectors.shape[1]
    width = vectors.shape[2]
    rank = leaf_basis.shape[2]
    device = lax.axis_index(AX)
    own_points = points[0]
    shipped = jnp.concatenate(
        [vectors[0], own_points.reshape(3 * leaf_points // width, width)], axis=0
    )
    near_field = near_sum(own_points, near_list[0], shipped, device)
    coef_leaf = transposed_dot(leaf_basis[0], vectors[0])
    coef_pair = pair_total(transposed_dot(transfer_leaf[0], coef_leaf), 1)
    pair_rows = lax.dynamic_slice_in_dim(coef_pair, device % 2 * (rank // 2), rank // 2, 0)
    coef_quad = pair_total(transposed_dot(transfer_pair, pair_rows), 2)
    quad_rows = lax.dynamic_slice_in_dim(coef_quad, device % 4 * (rank // 4), rank // 4, 0)
    coef_top = pair_total(transposed_dot(transfer_quad, quad_rows), 3)
    top_cluster = device // 8
    top_member = device % 8
    share = width // 8
    top_cols_own = lax.dynamic_slice_in_dim(coef_top, top_member * share, share, 1)
    all_top = cluster_gather(top_cols_own, device, lax.axis_size("cl"))
    top_coords = lax.dynamic_index_in_dim(skel_top, top_cluster, 0, keepdims=False)
    top_entries = lax.dynamic_index_in_dim(far_top, top_cluster, 0, keepdims=False)
    top_chosen = jnp.maximum(top_entries, 0)
    top_cols = batched_far(
        top_coords,
        jnp.take(skel_top, top_chosen, axis=0),
        jnp.take(all_top, top_chosen, axis=0),
        top_entries >= 0,
    )
    local_top = lax.all_gather(top_cols, MEMBERS, axis=1, tiled=True)
    local_quad = middle_level(coef_quad, skel_quad, far_quad, transfer_quad, local_top, 4, device)
    local_pair = middle_level(coef_pair, skel_pair, far_pair, transfer_pair, local_quad, 2, device)
    leaf_ship = jnp.concatenate([coef_leaf, skel_leaf[0]], axis=0)
    leaf_rim = window(leaf_ship)
    leaf_entries = far_leaf[0]
    positions = jnp.clip(jnp.maximum(leaf_entries, 0) - device + REACH, 0, 2 * REACH)
    leaf_blocks = jnp.take(leaf_rim, positions, axis=0)
    local_leaf = batched_far(
        skel_leaf[0], leaf_blocks[:, rank:], leaf_blocks[:, :rank], leaf_entries >= 0
    ) + jnp.dot(transfer_leaf[0], local_pair, precision=HIGHEST)
    product = near_field + jnp.dot(leaf_basis[0], local_leaf, precision=HIGHEST)
    return product[None]


def solution(mesh):
    count = mesh.devices.size
    grid = Mesh(mesh.devices.reshape(count // 8, 2, 2, 2), AX)
    spread = P(AX, None, None)
    rows = P(AX, None)
    placed = (
        spread,
        spread,
        spread,
        spread,
        rows,
        rows,
        spread,
        P(),
        P(),
        P(),
        rows,
        rows,
        P(),
        P(),
        P(),
    )
    return jax.shard_map(per_device, mesh=grid, in_specs=placed, out_specs=spread, check_vma=False)
```

```python
import jax
import jax.numpy as jnp
from jax import lax
from jax.sharding import Mesh
from jax.sharding import PartitionSpec as P

REACH = 8
FAR_REACH = 4


INV_FOUR_PI = 0.07957747154594767
DELTA_SQ = 0.01
HIGHEST = lax.Precision.HIGHEST

AX = ("cl", "q", "p", "c")
MEMBERS = ("q", "p", "c")


def from_partner(value, axis, bit):
    mask = 2**bit
    pairs = [(source, source ^ mask) for source in range(lax.axis_size(axis))]
    return lax.ppermute(value, axis, pairs)


def from_behind(block, axis, distance):
    devices = range(lax.axis_size(axis))
    route = [(i - distance, i) for i in devices if i - distance in devices]
    return lax.ppermute(block, axis, route)


def kernel_block(left_pts, right_pts):
    distance = jnp.zeros((left_pts.shape[1], right_pts.shape[1]), jnp.float32)
    for axis_id in range(3):
        offset_gap = left_pts[axis_id][:, None] - right_pts[axis_id][None, :]
        distance = distance + offset_gap * offset_gap
    return INV_FOUR_PI * lax.rsqrt(distance + DELTA_SQ)


def transposed_dot(matrix, values):
    return lax.dot_general(matrix, values, (((0,), (0,)), ((), ())), precision=HIGHEST)


def listed_sum(own_coords, entries, fetcher, width):

    def advance(running, partner):
        coords, values = fetcher(jnp.maximum(partner, 0))
        contrib = jnp.dot(kernel_block(own_coords, coords), values, precision=HIGHEST)
        return (running + jnp.where(partner >= 0, contrib, 0.0), None)

    start_value = jnp.zeros((own_coords.shape[1], width), jnp.float32)
    result, _ = lax.scan(advance, start_value, entries)
    return result


def batched_far(own_coords, coords, values, valid):
    count, _, span = coords.shape
    right = jnp.transpose(coords, (1, 0, 2)).reshape(3, count * span)
    masked = jnp.where(valid[:, None, None], values, 0.0)
    flat = masked.reshape(count * span, values.shape[2])
    return jnp.dot(kernel_block(own_coords, right), flat, precision=HIGHEST)


def pair_total(partial_value, levels):
    for bit_index in range(levels):
        partial_value = partial_value + from_partner(partial_value, AX, bit_index)
    return partial_value


def join_rows(block, levels, device):
    for bit_index in range(levels):
        other = from_partner(block, AX, bit_index)
        upper = device // 2**bit_index % 2
        block = jnp.where(
            upper == 0, jnp.concatenate([block, other], 0), jnp.concatenate([other, block], 0)
        )
    return block


def window(shipped):
    gathered = []
    for distance in range(-REACH, REACH + 1):
        if distance == 0:
            gathered.append(shipped)
        else:
            gathered.append(from_behind(shipped, AX, -distance))
    return jnp.stack(gathered)


def partner_stack(coefs, stride):
    gathered = []
    for offset in list(range(-FAR_REACH, 0)) + list(range(1, FAR_REACH + 1)):
        gathered.append(from_behind(coefs, AX, -offset * stride))
    stacked = jnp.stack(gathered)

    def slot_of(distance):
        return distance + FAR_REACH - (distance > 0).astype(jnp.int32)

    return (stacked, slot_of)


def middle_level(coefs, skeletons, lists, transfer_rows, above, stride, device):
    rank_rows = coefs.shape[0] // stride
    cluster = device // stride
    member = device % stride
    own_full = lax.dynamic_index_in_dim(skeletons, cluster, 0, keepdims=False)
    own_coords = lax.dynamic_slice_in_dim(own_full, member * rank_rows, rank_rows, 1)
    stacked, slot_of = partner_stack(coefs, stride)
    entries = lax.dynamic_index_in_dim(lists, cluster, 0, keepdims=False)
    chosen = jnp.maximum(entries, 0)
    coords = jnp.take(skeletons, chosen, axis=0)
    slots = jnp.clip(slot_of(chosen - cluster), 0, stacked.shape[0] - 1)
    values = jnp.take(stacked, slots, axis=0)
    rows_here = batched_far(own_coords, coords, values, entries >= 0) + jnp.dot(
        transfer_rows, above, precision=HIGHEST
    )
    return join_rows(rows_here, stride.bit_length() - 1, device)


def cluster_gather(block, device, clusters):
    gathered = block[None]
    for level in range(clusters.bit_length() - 1):
        bit_index = 3 + level
        other = from_partner(gathered, AX, bit_index)
        upper = device // 2**bit_index % 2
        gathered = jnp.where(
            upper == 0,
            jnp.concatenate([gathered, other], 0),
            jnp.concatenate([other, gathered], 0),
        )
    return gathered


def near_sum(own_points, near_entries, shipped, device):
    leaf_points = own_points.shape[1]

    def contribution(block, distance):
        listed = jnp.any(near_entries == device + distance)
        coords = block[leaf_points:].reshape(3, leaf_points)
        contrib = jnp.dot(kernel_block(own_points, coords), block[:leaf_points], precision=HIGHEST)
        return jnp.where(listed, contrib, 0.0)

    total = contribution(shipped, 0)
    ahead = shipped
    behind = shipped
    for step in range(1, REACH + 1):
        ahead = from_behind(ahead, AX, 1)
        behind = from_behind(behind, AX, -1)
        total = total + contribution(ahead, -step) + contribution(behind, step)
    return total


def middle_full(coefs, skeletons, lists, transfer, above, stride, device):
    cluster = device // stride
    own_coords = lax.dynamic_index_in_dim(skeletons, cluster, 0, keepdims=False)
    stacked, slot_of = partner_stack(coefs, stride)
    entries = lax.dynamic_index_in_dim(lists, cluster, 0, keepdims=False)
    chosen = jnp.maximum(entries, 0)
    coords = jnp.take(skeletons, chosen, axis=0)
    slots = jnp.clip(slot_of(chosen - cluster), 0, stacked.shape[0] - 1)
    values = jnp.take(stacked, slots, axis=0)
    return batched_far(own_coords, coords, values, entries >= 0) + jnp.dot(
        transfer, above, precision=HIGHEST
    )


def per_device(
    vectors,
    points,
    leaf_basis,
    transfer_leaf,
    transfer_pair,
    transfer_quad,
    skel_leaf,
    skel_pair,
    skel_quad,
    skel_top,
    near_list,
    far_leaf,
    far_pair,
    far_quad,
    far_top,
):
    leaf_points = vectors.shape[1]
    width = vectors.shape[2]
    rank = leaf_basis.shape[2]
    device = lax.axis_index(AX)
    own_points = points[0]
    shipped = jnp.concatenate(
        [vectors[0], own_points.reshape(3 * leaf_points // width, width)], axis=0
    )
    near_field = near_sum(own_points, near_list[0], shipped, device)
    coef_leaf = transposed_dot(leaf_basis[0], vectors[0])
    pair_matrix = join_rows(transfer_pair, 1, device)
    quad_matrix = join_rows(transfer_quad, 2, device)
    up_pair = transposed_dot(transfer_leaf[0], coef_leaf)
    up_quad = transposed_dot(pair_matrix, up_pair)
    up_top = transposed_dot(quad_matrix, up_quad)
    first = jnp.stack([up_pair, up_quad, up_top])
    first = first + from_partner(first, AX, 0)
    coef_pair = first[0]
    second = first[1:] + from_partner(first[1:], AX, 1)
    coef_quad = second[0]
    coef_top = second[1] + from_partner(second[1], AX, 2)
    top_cluster = device // 8
    top_member = device % 8
    share = width // 8
    top_cols_own = lax.dynamic_slice_in_dim(coef_top, top_member * share, share, 1)
    all_top = cluster_gather(top_cols_own, device, lax.axis_size("cl"))
    top_coords = lax.dynamic_index_in_dim(skel_top, top_cluster, 0, keepdims=False)
    top_entries = lax.dynamic_index_in_dim(far_top, top_cluster, 0, keepdims=False)
    top_chosen = jnp.maximum(top_entries, 0)
    top_cols = batched_far(
        top_coords,
        jnp.take(skel_top, top_chosen, axis=0),
        jnp.take(all_top, top_chosen, axis=0),
        top_entries >= 0,
    )
    local_top = lax.all_gather(top_cols, MEMBERS, axis=1, tiled=True)
    local_quad = middle_full(coef_quad, skel_quad, far_quad, quad_matrix, local_top, 4, device)
    local_pair = middle_full(coef_pair, skel_pair, far_pair, pair_matrix, local_quad, 2, device)
    leaf_ship = jnp.concatenate([coef_leaf, skel_leaf[0]], axis=0)
    leaf_rim = window(leaf_ship)
    leaf_entries = far_leaf[0]
    positions = jnp.clip(jnp.maximum(leaf_entries, 0) - device + REACH, 0, 2 * REACH)
    leaf_blocks = jnp.take(leaf_rim, positions, axis=0)
    local_leaf = batched_far(
        skel_leaf[0], leaf_blocks[:, rank:], leaf_blocks[:, :rank], leaf_entries >= 0
    ) + jnp.dot(transfer_leaf[0], local_pair, precision=HIGHEST)
    product = near_field + jnp.dot(leaf_basis[0], local_leaf, precision=HIGHEST)
    return product[None]


def solution(mesh):
    count = mesh.devices.size
    grid = Mesh(mesh.devices.reshape(count // 8, 2, 2, 2), AX)
    spread = P(AX, None, None)
    rows = P(AX, None)
    placed = (
        spread,
        spread,
        spread,
        spread,
        rows,
        rows,
        spread,
        P(),
        P(),
        P(),
        rows,
        rows,
        P(),
        P(),
        P(),
    )
    return jax.shard_map(per_device, mesh=grid, in_specs=placed, out_specs=spread, check_vma=False)
```

```python
import functools

import jax
import jax.numpy as jnp
from jax import lax
from jax.experimental import pallas as pl
from jax.experimental.pallas import tpu as pltpu
from jax.sharding import Mesh
from jax.sharding import PartitionSpec as P

REACH = 8
FAR_REACH = 4


INV_FOUR_PI = 0.07957747154594767
DELTA_SQ = 0.01
HIGHEST = lax.Precision.HIGHEST

AX = ("cl", "q", "p", "c")
MEMBERS = ("q", "p", "c")


def from_partner(value, axis, bit):
    mask = 2**bit
    pairs = [(source, source ^ mask) for source in range(lax.axis_size(axis))]
    return lax.ppermute(value, axis, pairs)


def from_behind(block, axis, distance):
    devices = range(lax.axis_size(axis))
    route = [(i - distance, i) for i in devices if i - distance in devices]
    return lax.ppermute(block, axis, route)


def kernel_block(left_pts, right_pts):
    distance = jnp.zeros((left_pts.shape[1], right_pts.shape[1]), jnp.float32)
    for axis_id in range(3):
        offset_gap = left_pts[axis_id][:, None] - right_pts[axis_id][None, :]
        distance = distance + offset_gap * offset_gap
    return INV_FOUR_PI * lax.rsqrt(distance + DELTA_SQ)


def transposed_dot(matrix, values):
    return lax.dot_general(matrix, values, (((0,), (0,)), ((), ())), precision=HIGHEST)


def listed_sum(own_coords, entries, fetcher, width):

    def advance(running, partner):
        coords, values = fetcher(jnp.maximum(partner, 0))
        contrib = jnp.dot(kernel_block(own_coords, coords), values, precision=HIGHEST)
        return (running + jnp.where(partner >= 0, contrib, 0.0), None)

    start_value = jnp.zeros((own_coords.shape[1], width), jnp.float32)
    result, _ = lax.scan(advance, start_value, entries)
    return result


def batched_far(own_coords, coords, values, valid):
    count, _, span = coords.shape
    right = jnp.transpose(coords, (1, 0, 2)).reshape(3, count * span)
    masked = jnp.where(valid[:, None, None], values, 0.0)
    flat = masked.reshape(count * span, values.shape[2])
    return jnp.dot(kernel_block(own_coords, right), flat, precision=HIGHEST)


def pair_total(partial_value, levels):
    for bit_index in range(levels):
        partial_value = partial_value + from_partner(partial_value, AX, bit_index)
    return partial_value


def join_rows(block, levels, device):
    for bit_index in range(levels):
        other = from_partner(block, AX, bit_index)
        upper = device // 2**bit_index % 2
        block = jnp.where(
            upper == 0, jnp.concatenate([block, other], 0), jnp.concatenate([other, block], 0)
        )
    return block


def window(shipped):
    gathered = []
    for distance in range(-REACH, REACH + 1):
        if distance == 0:
            gathered.append(shipped)
        else:
            gathered.append(from_behind(shipped, AX, -distance))
    return jnp.stack(gathered)


def partner_stack(coefs, stride):
    gathered = []
    for offset in list(range(-FAR_REACH, 0)) + list(range(1, FAR_REACH + 1)):
        gathered.append(from_behind(coefs, AX, -offset * stride))
    stacked = jnp.stack(gathered)

    def slot_of(distance):
        return distance + FAR_REACH - (distance > 0).astype(jnp.int32)

    return (stacked, slot_of)


def middle_level(coefs, skeletons, lists, transfer_rows, above, stride, device):
    rank_rows = coefs.shape[0] // stride
    cluster = device // stride
    member = device % stride
    own_full = lax.dynamic_index_in_dim(skeletons, cluster, 0, keepdims=False)
    own_coords = lax.dynamic_slice_in_dim(own_full, member * rank_rows, rank_rows, 1)
    stacked, slot_of = partner_stack(coefs, stride)
    entries = lax.dynamic_index_in_dim(lists, cluster, 0, keepdims=False)
    chosen = jnp.maximum(entries, 0)
    coords = jnp.take(skeletons, chosen, axis=0)
    slots = jnp.clip(slot_of(chosen - cluster), 0, stacked.shape[0] - 1)
    values = jnp.take(stacked, slots, axis=0)
    rows_here = batched_far(own_coords, coords, values, entries >= 0) + jnp.dot(
        transfer_rows, above, precision=HIGHEST
    )
    return join_rows(rows_here, stride.bit_length() - 1, device)


def cluster_gather(block, device, clusters):
    gathered = block[None]
    for level in range(clusters.bit_length() - 1):
        bit_index = 3 + level
        other = from_partner(gathered, AX, bit_index)
        upper = device // 2**bit_index % 2
        gathered = jnp.where(
            upper == 0,
            jnp.concatenate([gathered, other], 0),
            jnp.concatenate([other, gathered], 0),
        )
    return gathered


def near_sum(own_points, near_entries, shipped, device):
    leaf_points = own_points.shape[1]

    def contribution(block, distance):
        listed = jnp.any(near_entries == device + distance)
        coords = block[leaf_points:].reshape(3, leaf_points)
        contrib = jnp.dot(kernel_block(own_points, coords), block[:leaf_points], precision=HIGHEST)
        return jnp.where(listed, contrib, 0.0)

    total = contribution(shipped, 0)
    ahead = shipped
    behind = shipped
    for step in range(1, REACH + 1):
        ahead = from_behind(ahead, AX, 1)
        behind = from_behind(behind, AX, -1)
        total = total + contribution(ahead, -step) + contribution(behind, step)
    return total


def middle_full(coefs, skeletons, lists, transfer, above, stride, device):
    cluster = device // stride
    own_coords = lax.dynamic_index_in_dim(skeletons, cluster, 0, keepdims=False)
    stacked, slot_of = partner_stack(coefs, stride)
    entries = lax.dynamic_index_in_dim(lists, cluster, 0, keepdims=False)
    chosen = jnp.maximum(entries, 0)
    coords = jnp.take(skeletons, chosen, axis=0)
    slots = jnp.clip(slot_of(chosen - cluster), 0, stacked.shape[0] - 1)
    values = jnp.take(stacked, slots, axis=0)
    return batched_far(own_coords, coords, values, entries >= 0) + jnp.dot(
        transfer, above, precision=HIGHEST
    )


def gather_kernel(clusters, block_ref, out_ref, landing, send_sem, recv_sem):
    me = lax.axis_index("cl")
    mesh_id = pl.DeviceIdType.MESH
    barrier = pltpu.get_barrier_semaphore()

    def greet(step, carry):
        peer = lax.rem(me + step, clusters)
        pl.semaphore_signal(barrier, inc=1, device_id={"cl": peer}, device_id_type=mesh_id)
        return carry

    lax.fori_loop(1, clusters, greet, 0)
    pl.semaphore_wait(barrier, clusters - 1)

    def outgoing(step):
        peer = lax.rem(me + step, clusters)
        return pltpu.make_async_remote_copy(
            src_ref=block_ref,
            dst_ref=landing.at[me],
            send_sem=send_sem.at[step],
            recv_sem=recv_sem.at[me],
            device_id={"cl": peer},
            device_id_type=mesh_id,
        )

    def incoming(step):
        source = lax.rem(me - step + clusters, clusters)
        return pltpu.make_async_remote_copy(
            src_ref=block_ref,
            dst_ref=landing.at[source],
            send_sem=send_sem.at[step],
            recv_sem=recv_sem.at[source],
            device_id={"cl": source},
            device_id_type=mesh_id,
        )

    def send(step, carry):
        outgoing(step).start()
        return carry

    lax.fori_loop(1, clusters, send, 0)
    landing[me] = block_ref[...]

    def finish(step, carry):
        outgoing(step).wait_send()
        incoming(step).wait_recv()
        return carry

    lax.fori_loop(1, clusters, finish, 0)
    out_ref[...] = landing[...]


def cluster_gather_kernel(block):
    clusters = lax.axis_size("cl")
    rows, cols = block.shape
    return pl.pallas_call(
        functools.partial(gather_kernel, clusters),
        out_shape=jax.ShapeDtypeStruct((clusters, rows, cols), jnp.float32),
        in_specs=[pl.BlockSpec(memory_space=pltpu.VMEM)],
        out_specs=pl.BlockSpec(memory_space=pltpu.VMEM),
        scratch_shapes=[
            pltpu.VMEM((clusters, rows, cols), jnp.float32),
            pltpu.SemaphoreType.DMA((clusters,)),
            pltpu.SemaphoreType.DMA((clusters,)),
        ],
        compiler_params=pltpu.CompilerParams(collective_id=0, has_side_effects=True),
    )(block)


def per_device(
    vectors,
    points,
    leaf_basis,
    transfer_leaf,
    transfer_pair,
    transfer_quad,
    skel_leaf,
    skel_pair,
    skel_quad,
    skel_top,
    near_list,
    far_leaf,
    far_pair,
    far_quad,
    far_top,
):
    leaf_points = vectors.shape[1]
    width = vectors.shape[2]
    rank = leaf_basis.shape[2]
    device = lax.axis_index(AX)
    own_points = points[0]
    shipped = jnp.concatenate(
        [vectors[0], own_points.reshape(3 * leaf_points // width, width)], axis=0
    )
    near_field = near_sum(own_points, near_list[0], shipped, device)
    coef_leaf = transposed_dot(leaf_basis[0], vectors[0])
    pair_matrix = join_rows(transfer_pair, 1, device)
    quad_matrix = join_rows(transfer_quad, 2, device)
    up_pair = transposed_dot(transfer_leaf[0], coef_leaf)
    up_quad = transposed_dot(pair_matrix, up_pair)
    up_top = transposed_dot(quad_matrix, up_quad)
    first = jnp.stack([up_pair, up_quad, up_top])
    first = first + from_partner(first, AX, 0)
    coef_pair = first[0]
    second = first[1:] + from_partner(first[1:], AX, 1)
    coef_quad = second[0]
    coef_top = second[1] + from_partner(second[1], AX, 2)
    top_cluster = device // 8
    top_member = device % 8
    share = width // 8
    top_cols_own = lax.dynamic_slice_in_dim(coef_top.T, top_member * share, share, 0)
    all_top = jnp.swapaxes(cluster_gather_kernel(top_cols_own), 1, 2)
    top_coords = lax.dynamic_index_in_dim(skel_top, top_cluster, 0, keepdims=False)
    top_entries = lax.dynamic_index_in_dim(far_top, top_cluster, 0, keepdims=False)
    top_chosen = jnp.maximum(top_entries, 0)
    top_cols = batched_far(
        top_coords,
        jnp.take(skel_top, top_chosen, axis=0),
        jnp.take(all_top, top_chosen, axis=0),
        top_entries >= 0,
    )
    local_top = lax.all_gather(top_cols, MEMBERS, axis=1, tiled=True)
    local_quad = middle_full(coef_quad, skel_quad, far_quad, quad_matrix, local_top, 4, device)
    local_pair = middle_full(coef_pair, skel_pair, far_pair, pair_matrix, local_quad, 2, device)
    leaf_ship = jnp.concatenate([coef_leaf, skel_leaf[0]], axis=0)
    leaf_rim = window(leaf_ship)
    leaf_entries = far_leaf[0]
    positions = jnp.clip(jnp.maximum(leaf_entries, 0) - device + REACH, 0, 2 * REACH)
    leaf_blocks = jnp.take(leaf_rim, positions, axis=0)
    local_leaf = batched_far(
        skel_leaf[0], leaf_blocks[:, rank:], leaf_blocks[:, :rank], leaf_entries >= 0
    ) + jnp.dot(transfer_leaf[0], local_pair, precision=HIGHEST)
    product = near_field + jnp.dot(leaf_basis[0], local_leaf, precision=HIGHEST)
    return product[None]


def solution(mesh):
    count = mesh.devices.size
    grid = Mesh(mesh.devices.reshape(count // 8, 2, 2, 2), AX)
    spread = P(AX, None, None)
    rows = P(AX, None)
    placed = (
        spread,
        spread,
        spread,
        spread,
        rows,
        rows,
        spread,
        P(),
        P(),
        P(),
        rows,
        rows,
        P(),
        P(),
        P(),
    )
    return jax.shard_map(per_device, mesh=grid, in_specs=placed, out_specs=spread, check_vma=False)
```

```python
import functools

import jax
import jax.numpy as jnp
from jax import lax
from jax.experimental import pallas as pl
from jax.experimental.pallas import tpu as pltpu
from jax.sharding import Mesh
from jax.sharding import PartitionSpec as P

REACH = 8
FAR_REACH = 4


INV_FOUR_PI = 0.07957747154594767
DELTA_SQ = 0.01
HIGHEST = lax.Precision.HIGHEST

AX = ("cl", "q", "p", "c")
MEMBERS = ("q", "p", "c")


def from_partner(value, axis, bit):
    mask = 2**bit
    pairs = [(source, source ^ mask) for source in range(lax.axis_size(axis))]
    return lax.ppermute(value, axis, pairs)


def from_behind(block, axis, distance):
    devices = range(lax.axis_size(axis))
    route = [(i - distance, i) for i in devices if i - distance in devices]
    return lax.ppermute(block, axis, route)


def kernel_block(left_pts, right_pts):
    distance = jnp.zeros((left_pts.shape[1], right_pts.shape[1]), jnp.float32)
    for axis_id in range(3):
        offset_gap = left_pts[axis_id][:, None] - right_pts[axis_id][None, :]
        distance = distance + offset_gap * offset_gap
    return INV_FOUR_PI * lax.rsqrt(distance + DELTA_SQ)


def transposed_dot(matrix, values):
    return lax.dot_general(matrix, values, (((0,), (0,)), ((), ())), precision=HIGHEST)


def listed_sum(own_coords, entries, fetcher, width):

    def advance(running, partner):
        coords, values = fetcher(jnp.maximum(partner, 0))
        contrib = jnp.dot(kernel_block(own_coords, coords), values, precision=HIGHEST)
        return (running + jnp.where(partner >= 0, contrib, 0.0), None)

    start_value = jnp.zeros((own_coords.shape[1], width), jnp.float32)
    result, _ = lax.scan(advance, start_value, entries)
    return result


def batched_far(own_coords, coords, values, valid):
    count, _, span = coords.shape
    right = jnp.transpose(coords, (1, 0, 2)).reshape(3, count * span)
    masked = jnp.where(valid[:, None, None], values, 0.0)
    flat = masked.reshape(count * span, values.shape[2])
    return jnp.dot(kernel_block(own_coords, right), flat, precision=HIGHEST)


def pair_total(partial_value, levels):
    for bit_index in range(levels):
        partial_value = partial_value + from_partner(partial_value, AX, bit_index)
    return partial_value


def join_rows(block, levels, device):
    for bit_index in range(levels):
        other = from_partner(block, AX, bit_index)
        upper = device // 2**bit_index % 2
        block = jnp.where(
            upper == 0, jnp.concatenate([block, other], 0), jnp.concatenate([other, block], 0)
        )
    return block


def window(shipped):
    gathered = []
    for distance in range(-REACH, REACH + 1):
        if distance == 0:
            gathered.append(shipped)
        else:
            gathered.append(from_behind(shipped, AX, -distance))
    return jnp.stack(gathered)


def partner_stack(coefs, stride):
    gathered = []
    for offset in list(range(-FAR_REACH, 0)) + list(range(1, FAR_REACH + 1)):
        gathered.append(from_behind(coefs, AX, -offset * stride))
    stacked = jnp.stack(gathered)

    def slot_of(distance):
        return distance + FAR_REACH - (distance > 0).astype(jnp.int32)

    return (stacked, slot_of)


def middle_level(coefs, skeletons, lists, transfer_rows, above, stride, device):
    rank_rows = coefs.shape[0] // stride
    cluster = device // stride
    member = device % stride
    own_full = lax.dynamic_index_in_dim(skeletons, cluster, 0, keepdims=False)
    own_coords = lax.dynamic_slice_in_dim(own_full, member * rank_rows, rank_rows, 1)
    stacked, slot_of = partner_stack(coefs, stride)
    entries = lax.dynamic_index_in_dim(lists, cluster, 0, keepdims=False)
    chosen = jnp.maximum(entries, 0)
    coords = jnp.take(skeletons, chosen, axis=0)
    slots = jnp.clip(slot_of(chosen - cluster), 0, stacked.shape[0] - 1)
    values = jnp.take(stacked, slots, axis=0)
    rows_here = batched_far(own_coords, coords, values, entries >= 0) + jnp.dot(
        transfer_rows, above, precision=HIGHEST
    )
    return join_rows(rows_here, stride.bit_length() - 1, device)


def cluster_gather(block, device, clusters):
    gathered = block[None]
    for level in range(clusters.bit_length() - 1):
        bit_index = 3 + level
        other = from_partner(gathered, AX, bit_index)
        upper = device // 2**bit_index % 2
        gathered = jnp.where(
            upper == 0,
            jnp.concatenate([gathered, other], 0),
            jnp.concatenate([other, gathered], 0),
        )
    return gathered


def near_sum(own_points, near_entries, shipped, device):
    leaf_points = own_points.shape[1]

    def contribution(block, distance):
        listed = jnp.any(near_entries == device + distance)
        coords = block[leaf_points:].reshape(3, leaf_points)
        contrib = jnp.dot(kernel_block(own_points, coords), block[:leaf_points], precision=HIGHEST)
        return jnp.where(listed, contrib, 0.0)

    total = contribution(shipped, 0)
    ahead = shipped
    behind = shipped
    for step in range(1, REACH + 1):
        ahead = from_behind(ahead, AX, 1)
        behind = from_behind(behind, AX, -1)
        total = total + contribution(ahead, -step) + contribution(behind, step)
    return total


def middle_full(coefs, skeletons, lists, transfer, above, stride, device):
    cluster = device // stride
    own_coords = lax.dynamic_index_in_dim(skeletons, cluster, 0, keepdims=False)
    stacked, slot_of = partner_stack(coefs, stride)
    entries = lax.dynamic_index_in_dim(lists, cluster, 0, keepdims=False)
    chosen = jnp.maximum(entries, 0)
    coords = jnp.take(skeletons, chosen, axis=0)
    slots = jnp.clip(slot_of(chosen - cluster), 0, stacked.shape[0] - 1)
    values = jnp.take(stacked, slots, axis=0)
    return batched_far(own_coords, coords, values, entries >= 0) + jnp.dot(
        transfer, above, precision=HIGHEST
    )


def gather_kernel(clusters, block_ref, out_ref, landing, send_sem, recv_sem):
    me = lax.axis_index("cl")
    mesh_id = pl.DeviceIdType.MESH
    barrier = pltpu.get_barrier_semaphore()

    def greet(step, carry):
        peer = lax.rem(me + step, clusters)
        pl.semaphore_signal(barrier, inc=1, device_id={"cl": peer}, device_id_type=mesh_id)
        return carry

    lax.fori_loop(1, clusters, greet, 0)
    pl.semaphore_wait(barrier, clusters - 1)

    def outgoing(step):
        peer = lax.rem(me + step, clusters)
        return pltpu.make_async_remote_copy(
            src_ref=block_ref,
            dst_ref=landing.at[me],
            send_sem=send_sem.at[step],
            recv_sem=recv_sem.at[me],
            device_id={"cl": peer},
            device_id_type=mesh_id,
        )

    def incoming(step):
        source = lax.rem(me - step + clusters, clusters)
        return pltpu.make_async_remote_copy(
            src_ref=block_ref,
            dst_ref=landing.at[source],
            send_sem=send_sem.at[step],
            recv_sem=recv_sem.at[source],
            device_id={"cl": source},
            device_id_type=mesh_id,
        )

    def send(step, carry):
        outgoing(step).start()
        return carry

    lax.fori_loop(1, clusters, send, 0)
    landing[me] = block_ref[...]

    def finish(step, carry):
        outgoing(step).wait_send()
        incoming(step).wait_recv()
        return carry

    lax.fori_loop(1, clusters, finish, 0)
    out_ref[...] = landing[...]


def cluster_gather_kernel(block):
    clusters = lax.axis_size("cl")
    rows, cols = block.shape
    return pl.pallas_call(
        functools.partial(gather_kernel, clusters),
        out_shape=jax.ShapeDtypeStruct((clusters, rows, cols), jnp.float32),
        in_specs=[pl.BlockSpec(memory_space=pltpu.VMEM)],
        out_specs=pl.BlockSpec(memory_space=pltpu.VMEM),
        scratch_shapes=[
            pltpu.VMEM((clusters, rows, cols), jnp.float32),
            pltpu.SemaphoreType.DMA((clusters,)),
            pltpu.SemaphoreType.DMA((clusters,)),
        ],
        compiler_params=pltpu.CompilerParams(collective_id=0, has_side_effects=True),
    )(block)


def per_device(
    vectors,
    points,
    leaf_basis,
    transfer_leaf,
    transfer_pair,
    transfer_quad,
    skel_leaf,
    skel_pair,
    skel_quad,
    skel_top,
    near_list,
    far_leaf,
    far_pair,
    far_quad,
    far_top,
):
    leaf_points = vectors.shape[1]
    width = vectors.shape[2]
    rank = leaf_basis.shape[2]
    device = lax.axis_index(AX)
    own_points = points[0]
    coef_leaf = transposed_dot(leaf_basis[0], vectors[0])
    pair_matrix = join_rows(transfer_pair, 1, device)
    quad_matrix = join_rows(transfer_quad, 2, device)
    up_pair = transposed_dot(transfer_leaf[0], coef_leaf)
    up_quad = transposed_dot(pair_matrix, up_pair)
    up_top = transposed_dot(quad_matrix, up_quad)
    first = jnp.stack([up_pair, up_quad, up_top])
    first = first + from_partner(first, AX, 0)
    coef_pair = first[0]
    second = first[1:] + from_partner(first[1:], AX, 1)
    coef_quad = second[0]
    coef_top = second[1] + from_partner(second[1], AX, 2)
    top_cluster = device // 8
    top_member = device % 8
    share = width // 8
    top_cols_own = lax.dynamic_slice_in_dim(coef_top.T, top_member * share, share, 0)
    all_top = jnp.swapaxes(cluster_gather_kernel(top_cols_own), 1, 2)
    all_top, coef_leaf, coef_pair, coef_quad, own_points, near_vectors = lax.optimization_barrier(
        (all_top, coef_leaf, coef_pair, coef_quad, points[0], vectors[0])
    )
    shipped = jnp.concatenate(
        [near_vectors, own_points.reshape(3 * leaf_points // width, width)], axis=0
    )
    near_field = near_sum(own_points, near_list[0], shipped, device)
    top_coords = lax.dynamic_index_in_dim(skel_top, top_cluster, 0, keepdims=False)
    top_entries = lax.dynamic_index_in_dim(far_top, top_cluster, 0, keepdims=False)
    top_chosen = jnp.maximum(top_entries, 0)
    top_cols = batched_far(
        top_coords,
        jnp.take(skel_top, top_chosen, axis=0),
        jnp.take(all_top, top_chosen, axis=0),
        top_entries >= 0,
    )
    local_top = lax.all_gather(top_cols, MEMBERS, axis=1, tiled=True)
    local_quad = middle_full(coef_quad, skel_quad, far_quad, quad_matrix, local_top, 4, device)
    local_pair = middle_full(coef_pair, skel_pair, far_pair, pair_matrix, local_quad, 2, device)
    leaf_ship = jnp.concatenate([coef_leaf, skel_leaf[0]], axis=0)
    leaf_rim = window(leaf_ship)
    leaf_entries = far_leaf[0]
    positions = jnp.clip(jnp.maximum(leaf_entries, 0) - device + REACH, 0, 2 * REACH)
    leaf_blocks = jnp.take(leaf_rim, positions, axis=0)
    local_leaf = batched_far(
        skel_leaf[0], leaf_blocks[:, rank:], leaf_blocks[:, :rank], leaf_entries >= 0
    ) + jnp.dot(transfer_leaf[0], local_pair, precision=HIGHEST)
    product = near_field + jnp.dot(leaf_basis[0], local_leaf, precision=HIGHEST)
    return product[None]


def solution(mesh):
    count = mesh.devices.size
    grid = Mesh(mesh.devices.reshape(count // 8, 2, 2, 2), AX)
    spread = P(AX, None, None)
    rows = P(AX, None)
    placed = (
        spread,
        spread,
        spread,
        spread,
        rows,
        rows,
        spread,
        P(),
        P(),
        P(),
        rows,
        rows,
        P(),
        P(),
        P(),
    )
    return jax.shard_map(per_device, mesh=grid, in_specs=placed, out_specs=spread, check_vma=False)
```

```python
import functools

import jax
import jax.numpy as jnp
from jax import lax
from jax.experimental import pallas as pl
from jax.experimental.pallas import tpu as pltpu
from jax.sharding import Mesh
from jax.sharding import PartitionSpec as P

REACH = 8
FAR_REACH = 4


INV_FOUR_PI = 0.07957747154594767
DELTA_SQ = 0.01
HIGHEST = lax.Precision.HIGHEST

AX = ("cl", "q", "p", "c")
MEMBERS = ("q", "p", "c")


def from_partner(value, axis, bit):
    mask = 2**bit
    pairs = [(source, source ^ mask) for source in range(lax.axis_size(axis))]
    return lax.ppermute(value, axis, pairs)


def from_behind(block, axis, distance):
    devices = range(lax.axis_size(axis))
    route = [(i - distance, i) for i in devices if i - distance in devices]
    return lax.ppermute(block, axis, route)


def kernel_block(left_pts, right_pts):
    distance = jnp.zeros((left_pts.shape[1], right_pts.shape[1]), jnp.float32)
    for axis_id in range(3):
        offset_gap = left_pts[axis_id][:, None] - right_pts[axis_id][None, :]
        distance = distance + offset_gap * offset_gap
    return INV_FOUR_PI * lax.rsqrt(distance + DELTA_SQ)


def transposed_dot(matrix, values):
    return lax.dot_general(matrix, values, (((0,), (0,)), ((), ())), precision=HIGHEST)


def listed_sum(own_coords, entries, fetcher, width):

    def advance(running, partner):
        coords, values = fetcher(jnp.maximum(partner, 0))
        contrib = jnp.dot(kernel_block(own_coords, coords), values, precision=HIGHEST)
        return (running + jnp.where(partner >= 0, contrib, 0.0), None)

    start_value = jnp.zeros((own_coords.shape[1], width), jnp.float32)
    result, _ = lax.scan(advance, start_value, entries)
    return result


def batched_far(own_coords, coords, values, valid):
    count, _, span = coords.shape
    right = jnp.transpose(coords, (1, 0, 2)).reshape(3, count * span)
    masked = jnp.where(valid[:, None, None], values, 0.0)
    flat = masked.reshape(count * span, values.shape[2])
    return jnp.dot(kernel_block(own_coords, right), flat, precision=HIGHEST)


def pair_total(partial_value, levels):
    for bit_index in range(levels):
        partial_value = partial_value + from_partner(partial_value, AX, bit_index)
    return partial_value


def join_rows(block, levels, device):
    for bit_index in range(levels):
        other = from_partner(block, AX, bit_index)
        upper = device // 2**bit_index % 2
        block = jnp.where(
            upper == 0, jnp.concatenate([block, other], 0), jnp.concatenate([other, block], 0)
        )
    return block


def window(shipped):
    gathered = []
    for distance in range(-REACH, REACH + 1):
        if distance == 0:
            gathered.append(shipped)
        else:
            gathered.append(from_behind(shipped, AX, -distance))
    return jnp.stack(gathered)


def partner_stack(coefs, stride):
    gathered = []
    for offset in list(range(-FAR_REACH, 0)) + list(range(1, FAR_REACH + 1)):
        gathered.append(from_behind(coefs, AX, -offset * stride))
    stacked = jnp.stack(gathered)

    def slot_of(distance):
        return distance + FAR_REACH - (distance > 0).astype(jnp.int32)

    return (stacked, slot_of)


def middle_level(coefs, skeletons, lists, transfer_rows, above, stride, device):
    rank_rows = coefs.shape[0] // stride
    cluster = device // stride
    member = device % stride
    own_full = lax.dynamic_index_in_dim(skeletons, cluster, 0, keepdims=False)
    own_coords = lax.dynamic_slice_in_dim(own_full, member * rank_rows, rank_rows, 1)
    stacked, slot_of = partner_stack(coefs, stride)
    entries = lax.dynamic_index_in_dim(lists, cluster, 0, keepdims=False)
    chosen = jnp.maximum(entries, 0)
    coords = jnp.take(skeletons, chosen, axis=0)
    slots = jnp.clip(slot_of(chosen - cluster), 0, stacked.shape[0] - 1)
    values = jnp.take(stacked, slots, axis=0)
    rows_here = batched_far(own_coords, coords, values, entries >= 0) + jnp.dot(
        transfer_rows, above, precision=HIGHEST
    )
    return join_rows(rows_here, stride.bit_length() - 1, device)


def cluster_gather(block, device, clusters):
    gathered = block[None]
    for level in range(clusters.bit_length() - 1):
        bit_index = 3 + level
        other = from_partner(gathered, AX, bit_index)
        upper = device // 2**bit_index % 2
        gathered = jnp.where(
            upper == 0,
            jnp.concatenate([gathered, other], 0),
            jnp.concatenate([other, gathered], 0),
        )
    return gathered


def near_sum(own_points, near_entries, shipped, device):
    leaf_points = own_points.shape[1]
    point_rows = leaf_points + 3 * leaf_points // shipped.shape[1]

    def contribution(block, distance):
        listed = jnp.any(near_entries == device + distance)
        coords = block[leaf_points:point_rows].reshape(3, leaf_points)
        contrib = jnp.dot(kernel_block(own_points, coords), block[:leaf_points], precision=HIGHEST)
        return jnp.where(listed, contrib, 0.0)

    total = contribution(shipped, 0)
    ahead = shipped
    behind = shipped
    rim = [None] * (2 * REACH + 1)
    rim[REACH] = shipped[point_rows:]
    for step in range(1, REACH + 1):
        ahead = from_behind(ahead, AX, 1)
        behind = from_behind(behind, AX, -1)
        rim[REACH - step] = ahead[point_rows:]
        rim[REACH + step] = behind[point_rows:]
        total = total + contribution(ahead, -step) + contribution(behind, step)
    return total, jnp.stack(rim)


def middle_full(coefs, skeletons, lists, transfer, above, stride, device):
    cluster = device // stride
    own_coords = lax.dynamic_index_in_dim(skeletons, cluster, 0, keepdims=False)
    stacked, slot_of = partner_stack(coefs, stride)
    entries = lax.dynamic_index_in_dim(lists, cluster, 0, keepdims=False)
    chosen = jnp.maximum(entries, 0)
    coords = jnp.take(skeletons, chosen, axis=0)
    slots = jnp.clip(slot_of(chosen - cluster), 0, stacked.shape[0] - 1)
    values = jnp.take(stacked, slots, axis=0)
    return batched_far(own_coords, coords, values, entries >= 0) + jnp.dot(
        transfer, above, precision=HIGHEST
    )


def gather_kernel(clusters, block_ref, out_ref, landing, send_sem, recv_sem):
    me = lax.axis_index("cl")
    mesh_id = pl.DeviceIdType.MESH
    barrier = pltpu.get_barrier_semaphore()

    def greet(step, carry):
        peer = lax.rem(me + step, clusters)
        pl.semaphore_signal(barrier, inc=1, device_id={"cl": peer}, device_id_type=mesh_id)
        return carry

    lax.fori_loop(1, clusters, greet, 0)
    pl.semaphore_wait(barrier, clusters - 1)

    def outgoing(step):
        peer = lax.rem(me + step, clusters)
        return pltpu.make_async_remote_copy(
            src_ref=block_ref,
            dst_ref=landing.at[me],
            send_sem=send_sem.at[step],
            recv_sem=recv_sem.at[me],
            device_id={"cl": peer},
            device_id_type=mesh_id,
        )

    def incoming(step):
        source = lax.rem(me - step + clusters, clusters)
        return pltpu.make_async_remote_copy(
            src_ref=block_ref,
            dst_ref=landing.at[source],
            send_sem=send_sem.at[step],
            recv_sem=recv_sem.at[source],
            device_id={"cl": source},
            device_id_type=mesh_id,
        )

    def send(step, carry):
        outgoing(step).start()
        return carry

    lax.fori_loop(1, clusters, send, 0)
    landing[me] = block_ref[...]

    def finish(step, carry):
        outgoing(step).wait_send()
        incoming(step).wait_recv()
        return carry

    lax.fori_loop(1, clusters, finish, 0)
    out_ref[...] = landing[...]


def cluster_gather_kernel(block):
    clusters = lax.axis_size("cl")
    rows, cols = block.shape
    return pl.pallas_call(
        functools.partial(gather_kernel, clusters),
        out_shape=jax.ShapeDtypeStruct((clusters, rows, cols), jnp.float32),
        in_specs=[pl.BlockSpec(memory_space=pltpu.VMEM)],
        out_specs=pl.BlockSpec(memory_space=pltpu.VMEM),
        scratch_shapes=[
            pltpu.VMEM((clusters, rows, cols), jnp.float32),
            pltpu.SemaphoreType.DMA((clusters,)),
            pltpu.SemaphoreType.DMA((clusters,)),
        ],
        compiler_params=pltpu.CompilerParams(collective_id=0, has_side_effects=True),
    )(block)


def per_device(
    vectors,
    points,
    leaf_basis,
    transfer_leaf,
    transfer_pair,
    transfer_quad,
    skel_leaf,
    skel_pair,
    skel_quad,
    skel_top,
    near_list,
    far_leaf,
    far_pair,
    far_quad,
    far_top,
):
    leaf_points = vectors.shape[1]
    width = vectors.shape[2]
    rank = leaf_basis.shape[2]
    device = lax.axis_index(AX)
    own_points = points[0]
    coef_leaf = transposed_dot(leaf_basis[0], vectors[0])
    pair_matrix = join_rows(transfer_pair, 1, device)
    quad_matrix = join_rows(transfer_quad, 2, device)
    up_pair = transposed_dot(transfer_leaf[0], coef_leaf)
    up_quad = transposed_dot(pair_matrix, up_pair)
    up_top = transposed_dot(quad_matrix, up_quad)
    first = jnp.stack([up_pair, up_quad, up_top])
    first = first + from_partner(first, AX, 0)
    coef_pair = first[0]
    second = first[1:] + from_partner(first[1:], AX, 1)
    coef_quad = second[0]
    coef_top = second[1] + from_partner(second[1], AX, 2)
    shipped = jnp.concatenate(
        [vectors[0], own_points.reshape(3 * leaf_points // width, width), coef_leaf, skel_leaf[0]],
        axis=0,
    )
    near_field, leaf_rim = near_sum(own_points, near_list[0], shipped, device)
    coef_top, coef_pair, coef_quad = lax.optimization_barrier((coef_top, coef_pair, coef_quad))
    top_cluster = device // 8
    top_member = device % 8
    share = width // 8
    top_cols_own = lax.dynamic_slice_in_dim(coef_top.T, top_member * share, share, 0)
    all_top = jnp.swapaxes(cluster_gather_kernel(top_cols_own), 1, 2)
    top_coords = lax.dynamic_index_in_dim(skel_top, top_cluster, 0, keepdims=False)
    top_entries = lax.dynamic_index_in_dim(far_top, top_cluster, 0, keepdims=False)
    top_chosen = jnp.maximum(top_entries, 0)
    top_cols = batched_far(
        top_coords,
        jnp.take(skel_top, top_chosen, axis=0),
        jnp.take(all_top, top_chosen, axis=0),
        top_entries >= 0,
    )
    local_top = lax.all_gather(top_cols, MEMBERS, axis=1, tiled=True)
    local_quad = middle_full(coef_quad, skel_quad, far_quad, quad_matrix, local_top, 4, device)
    local_pair = middle_full(coef_pair, skel_pair, far_pair, pair_matrix, local_quad, 2, device)
    leaf_entries = far_leaf[0]
    positions = jnp.clip(jnp.maximum(leaf_entries, 0) - device + REACH, 0, 2 * REACH)
    leaf_blocks = jnp.take(leaf_rim, positions, axis=0)
    local_leaf = batched_far(
        skel_leaf[0], leaf_blocks[:, rank:], leaf_blocks[:, :rank], leaf_entries >= 0
    ) + jnp.dot(transfer_leaf[0], local_pair, precision=HIGHEST)
    product = near_field + jnp.dot(leaf_basis[0], local_leaf, precision=HIGHEST)
    return product[None]


def solution(mesh):
    count = mesh.devices.size
    grid = Mesh(mesh.devices.reshape(count // 8, 2, 2, 2), AX)
    spread = P(AX, None, None)
    rows = P(AX, None)
    placed = (
        spread,
        spread,
        spread,
        spread,
        rows,
        rows,
        spread,
        P(),
        P(),
        P(),
        rows,
        rows,
        P(),
        P(),
        P(),
    )
    return jax.shard_map(per_device, mesh=grid, in_specs=placed, out_specs=spread, check_vma=False)
```

```python
import functools

import jax
import jax.numpy as jnp
from jax import lax
from jax.experimental import pallas as pl
from jax.experimental.pallas import tpu as pltpu
from jax.sharding import Mesh
from jax.sharding import PartitionSpec as P

REACH = 8
FAR_REACH = 4


INV_FOUR_PI = 0.07957747154594767
DELTA_SQ = 0.01
HIGHEST = lax.Precision.HIGHEST

AX = ("cl", "q", "p", "c")
MEMBERS = ("q", "p", "c")


def from_partner(value, axis, bit):
    mask = 2**bit
    pairs = [(source, source ^ mask) for source in range(lax.axis_size(axis))]
    return lax.ppermute(value, axis, pairs)


def from_behind(block, axis, distance):
    devices = range(lax.axis_size(axis))
    route = [(i - distance, i) for i in devices if i - distance in devices]
    return lax.ppermute(block, axis, route)


def kernel_block(left_pts, right_pts):
    distance = jnp.zeros((left_pts.shape[1], right_pts.shape[1]), jnp.float32)
    for axis_id in range(3):
        offset_gap = left_pts[axis_id][:, None] - right_pts[axis_id][None, :]
        distance = distance + offset_gap * offset_gap
    return INV_FOUR_PI * lax.rsqrt(distance + DELTA_SQ)


def transposed_dot(matrix, values):
    return lax.dot_general(matrix, values, (((0,), (0,)), ((), ())), precision=HIGHEST)


def listed_sum(own_coords, entries, fetcher, width):

    def advance(running, partner):
        coords, values = fetcher(jnp.maximum(partner, 0))
        contrib = jnp.dot(kernel_block(own_coords, coords), values, precision=HIGHEST)
        return (running + jnp.where(partner >= 0, contrib, 0.0), None)

    start_value = jnp.zeros((own_coords.shape[1], width), jnp.float32)
    result, _ = lax.scan(advance, start_value, entries)
    return result


def batched_far(own_coords, coords, values, valid):
    count, _, span = coords.shape
    right = jnp.transpose(coords, (1, 0, 2)).reshape(3, count * span)
    masked = jnp.where(valid[:, None, None], values, 0.0)
    flat = masked.reshape(count * span, values.shape[2])
    return jnp.dot(kernel_block(own_coords, right), flat, precision=HIGHEST)


def pair_total(partial_value, levels):
    for bit_index in range(levels):
        partial_value = partial_value + from_partner(partial_value, AX, bit_index)
    return partial_value


def join_rows(block, levels, device):
    for bit_index in range(levels):
        other = from_partner(block, AX, bit_index)
        upper = device // 2**bit_index % 2
        block = jnp.where(
            upper == 0, jnp.concatenate([block, other], 0), jnp.concatenate([other, block], 0)
        )
    return block


def window(shipped):
    gathered = []
    for distance in range(-REACH, REACH + 1):
        if distance == 0:
            gathered.append(shipped)
        else:
            gathered.append(from_behind(shipped, AX, -distance))
    return jnp.stack(gathered)


def partner_stack(coefs, stride):
    gathered = []
    for offset in list(range(-FAR_REACH, 0)) + list(range(1, FAR_REACH + 1)):
        gathered.append(from_behind(coefs, AX, -offset * stride))
    stacked = jnp.stack(gathered)

    def slot_of(distance):
        return distance + FAR_REACH - (distance > 0).astype(jnp.int32)

    return (stacked, slot_of)


def middle_level(coefs, skeletons, lists, transfer_rows, above, stride, device):
    rank_rows = coefs.shape[0] // stride
    cluster = device // stride
    member = device % stride
    own_full = lax.dynamic_index_in_dim(skeletons, cluster, 0, keepdims=False)
    own_coords = lax.dynamic_slice_in_dim(own_full, member * rank_rows, rank_rows, 1)
    stacked, slot_of = partner_stack(coefs, stride)
    entries = lax.dynamic_index_in_dim(lists, cluster, 0, keepdims=False)
    chosen = jnp.maximum(entries, 0)
    coords = jnp.take(skeletons, chosen, axis=0)
    slots = jnp.clip(slot_of(chosen - cluster), 0, stacked.shape[0] - 1)
    values = jnp.take(stacked, slots, axis=0)
    rows_here = batched_far(own_coords, coords, values, entries >= 0) + jnp.dot(
        transfer_rows, above, precision=HIGHEST
    )
    return join_rows(rows_here, stride.bit_length() - 1, device)


def cluster_gather(block, device, clusters):
    gathered = block[None]
    for level in range(clusters.bit_length() - 1):
        bit_index = 3 + level
        other = from_partner(gathered, AX, bit_index)
        upper = device // 2**bit_index % 2
        gathered = jnp.where(
            upper == 0,
            jnp.concatenate([gathered, other], 0),
            jnp.concatenate([other, gathered], 0),
        )
    return gathered


def near_sum(own_points, near_entries, shipped, device):
    leaf_points = own_points.shape[1]
    point_rows = leaf_points + 3 * leaf_points // shipped.shape[1]

    def contribution(block, distance):
        listed = jnp.any(near_entries == device + distance)
        coords = block[leaf_points:point_rows].reshape(3, leaf_points)
        contrib = jnp.dot(
            kernel_block(own_points, coords), block[:leaf_points], precision=lax.Precision.HIGH
        )
        return jnp.where(listed, contrib, 0.0)

    total = contribution(shipped, 0)
    ahead = shipped
    behind = shipped
    rim = [None] * (2 * REACH + 1)
    rim[REACH] = shipped[point_rows:]
    for step in range(1, REACH + 1):
        ahead = from_behind(ahead, AX, 1)
        behind = from_behind(behind, AX, -1)
        rim[REACH - step] = ahead[point_rows:]
        rim[REACH + step] = behind[point_rows:]
        total = total + contribution(ahead, -step) + contribution(behind, step)
    return total, jnp.stack(rim)


def middle_full(coefs, skeletons, lists, transfer, above, stride, device):
    cluster = device // stride
    own_coords = lax.dynamic_index_in_dim(skeletons, cluster, 0, keepdims=False)
    stacked, slot_of = partner_stack(coefs, stride)
    entries = lax.dynamic_index_in_dim(lists, cluster, 0, keepdims=False)
    chosen = jnp.maximum(entries, 0)
    coords = jnp.take(skeletons, chosen, axis=0)
    slots = jnp.clip(slot_of(chosen - cluster), 0, stacked.shape[0] - 1)
    values = jnp.take(stacked, slots, axis=0)
    return batched_far(own_coords, coords, values, entries >= 0) + jnp.dot(
        transfer, above, precision=HIGHEST
    )


def gather_kernel(clusters, block_ref, out_ref, landing, send_sem, recv_sem):
    me = lax.axis_index("cl")
    mesh_id = pl.DeviceIdType.MESH
    barrier = pltpu.get_barrier_semaphore()

    def greet(step, carry):
        peer = lax.rem(me + step, clusters)
        pl.semaphore_signal(barrier, inc=1, device_id={"cl": peer}, device_id_type=mesh_id)
        return carry

    lax.fori_loop(1, clusters, greet, 0)
    pl.semaphore_wait(barrier, clusters - 1)

    def outgoing(step):
        peer = lax.rem(me + step, clusters)
        return pltpu.make_async_remote_copy(
            src_ref=block_ref,
            dst_ref=landing.at[me],
            send_sem=send_sem.at[step],
            recv_sem=recv_sem.at[me],
            device_id={"cl": peer},
            device_id_type=mesh_id,
        )

    def incoming(step):
        source = lax.rem(me - step + clusters, clusters)
        return pltpu.make_async_remote_copy(
            src_ref=block_ref,
            dst_ref=landing.at[source],
            send_sem=send_sem.at[step],
            recv_sem=recv_sem.at[source],
            device_id={"cl": source},
            device_id_type=mesh_id,
        )

    def send(step, carry):
        outgoing(step).start()
        return carry

    lax.fori_loop(1, clusters, send, 0)
    landing[me] = block_ref[...]

    def finish(step, carry):
        outgoing(step).wait_send()
        incoming(step).wait_recv()
        return carry

    lax.fori_loop(1, clusters, finish, 0)
    out_ref[...] = landing[...]


def cluster_gather_kernel(block):
    clusters = lax.axis_size("cl")
    rows, cols = block.shape
    return pl.pallas_call(
        functools.partial(gather_kernel, clusters),
        out_shape=jax.ShapeDtypeStruct((clusters, rows, cols), jnp.float32),
        in_specs=[pl.BlockSpec(memory_space=pltpu.VMEM)],
        out_specs=pl.BlockSpec(memory_space=pltpu.VMEM),
        scratch_shapes=[
            pltpu.VMEM((clusters, rows, cols), jnp.float32),
            pltpu.SemaphoreType.DMA((clusters,)),
            pltpu.SemaphoreType.DMA((clusters,)),
        ],
        compiler_params=pltpu.CompilerParams(collective_id=0, has_side_effects=True),
    )(block)


def per_device(
    vectors,
    points,
    leaf_basis,
    transfer_leaf,
    transfer_pair,
    transfer_quad,
    skel_leaf,
    skel_pair,
    skel_quad,
    skel_top,
    near_list,
    far_leaf,
    far_pair,
    far_quad,
    far_top,
):
    leaf_points = vectors.shape[1]
    width = vectors.shape[2]
    rank = leaf_basis.shape[2]
    device = lax.axis_index(AX)
    own_points = points[0]
    coef_leaf = transposed_dot(leaf_basis[0], vectors[0])
    pair_matrix = join_rows(transfer_pair, 1, device)
    quad_matrix = join_rows(transfer_quad, 2, device)
    up_pair = transposed_dot(transfer_leaf[0], coef_leaf)
    up_quad = transposed_dot(pair_matrix, up_pair)
    up_top = transposed_dot(quad_matrix, up_quad)
    first = jnp.stack([up_pair, up_quad, up_top])
    first = first + from_partner(first, AX, 0)
    coef_pair = first[0]
    second = first[1:] + from_partner(first[1:], AX, 1)
    coef_quad = second[0]
    coef_top = second[1] + from_partner(second[1], AX, 2)
    shipped = jnp.concatenate(
        [vectors[0], own_points.reshape(3 * leaf_points // width, width), coef_leaf, skel_leaf[0]],
        axis=0,
    )
    near_field, leaf_rim = near_sum(own_points, near_list[0], shipped, device)
    coef_top, coef_pair, coef_quad = lax.optimization_barrier((coef_top, coef_pair, coef_quad))
    top_cluster = device // 8
    top_member = device % 8
    share = width // 8
    top_cols_own = lax.dynamic_slice_in_dim(coef_top.T, top_member * share, share, 0)
    all_top = jnp.swapaxes(cluster_gather_kernel(top_cols_own), 1, 2)
    top_coords = lax.dynamic_index_in_dim(skel_top, top_cluster, 0, keepdims=False)
    top_entries = lax.dynamic_index_in_dim(far_top, top_cluster, 0, keepdims=False)
    top_chosen = jnp.maximum(top_entries, 0)
    top_cols = batched_far(
        top_coords,
        jnp.take(skel_top, top_chosen, axis=0),
        jnp.take(all_top, top_chosen, axis=0),
        top_entries >= 0,
    )
    local_top = lax.all_gather(top_cols, MEMBERS, axis=1, tiled=True)
    local_quad = middle_full(coef_quad, skel_quad, far_quad, quad_matrix, local_top, 4, device)
    local_pair = middle_full(coef_pair, skel_pair, far_pair, pair_matrix, local_quad, 2, device)
    leaf_entries = far_leaf[0]
    positions = jnp.clip(jnp.maximum(leaf_entries, 0) - device + REACH, 0, 2 * REACH)
    leaf_blocks = jnp.take(leaf_rim, positions, axis=0)
    local_leaf = batched_far(
        skel_leaf[0], leaf_blocks[:, rank:], leaf_blocks[:, :rank], leaf_entries >= 0
    ) + jnp.dot(transfer_leaf[0], local_pair, precision=HIGHEST)
    product = near_field + jnp.dot(leaf_basis[0], local_leaf, precision=HIGHEST)
    return product[None]


def solution(mesh):
    count = mesh.devices.size
    grid = Mesh(mesh.devices.reshape(count // 8, 2, 2, 2), AX)
    spread = P(AX, None, None)
    rows = P(AX, None)
    placed = (
        spread,
        spread,
        spread,
        spread,
        rows,
        rows,
        spread,
        P(),
        P(),
        P(),
        rows,
        rows,
        P(),
        P(),
        P(),
    )
    return jax.shard_map(per_device, mesh=grid, in_specs=placed, out_specs=spread, check_vma=False)
```

```python
import functools

import jax
import jax.numpy as jnp
from jax import lax
from jax.experimental import pallas as pl
from jax.experimental.pallas import tpu as pltpu
from jax.sharding import Mesh
from jax.sharding import PartitionSpec as P

REACH = 8
FAR_REACH = 4


INV_FOUR_PI = 0.07957747154594767
DELTA_SQ = 0.01
HIGHEST = lax.Precision.HIGHEST

AX = ("cl", "q", "p", "c")
MEMBERS = ("q", "p", "c")


def from_partner(value, axis, bit):
    mask = 2**bit
    pairs = [(source, source ^ mask) for source in range(lax.axis_size(axis))]
    return lax.ppermute(value, axis, pairs)


def from_behind(block, axis, distance):
    devices = range(lax.axis_size(axis))
    route = [(i - distance, i) for i in devices if i - distance in devices]
    return lax.ppermute(block, axis, route)


def kernel_block(left_pts, right_pts):
    distance = jnp.zeros((left_pts.shape[1], right_pts.shape[1]), jnp.float32)
    for axis_id in range(3):
        offset_gap = left_pts[axis_id][:, None] - right_pts[axis_id][None, :]
        distance = distance + offset_gap * offset_gap
    return INV_FOUR_PI * lax.rsqrt(distance + DELTA_SQ)


def transposed_dot(matrix, values):
    return lax.dot_general(matrix, values, (((0,), (0,)), ((), ())), precision=HIGHEST)


def listed_sum(own_coords, entries, fetcher, width):

    def advance(running, partner):
        coords, values = fetcher(jnp.maximum(partner, 0))
        contrib = jnp.dot(kernel_block(own_coords, coords), values, precision=HIGHEST)
        return (running + jnp.where(partner >= 0, contrib, 0.0), None)

    start_value = jnp.zeros((own_coords.shape[1], width), jnp.float32)
    result, _ = lax.scan(advance, start_value, entries)
    return result


def batched_far(own_coords, coords, values, valid):
    count, _, span = coords.shape
    right = jnp.transpose(coords, (1, 0, 2)).reshape(3, count * span)
    masked = jnp.where(valid[:, None, None], values, 0.0)
    flat = masked.reshape(count * span, values.shape[2])
    return jnp.dot(kernel_block(own_coords, right), flat, precision=HIGHEST)


def pair_total(partial_value, levels):
    for bit_index in range(levels):
        partial_value = partial_value + from_partner(partial_value, AX, bit_index)
    return partial_value


def join_rows(block, levels, device):
    for bit_index in range(levels):
        other = from_partner(block, AX, bit_index)
        upper = device // 2**bit_index % 2
        block = jnp.where(
            upper == 0, jnp.concatenate([block, other], 0), jnp.concatenate([other, block], 0)
        )
    return block


def window(shipped):
    gathered = []
    for distance in range(-REACH, REACH + 1):
        if distance == 0:
            gathered.append(shipped)
        else:
            gathered.append(from_behind(shipped, AX, -distance))
    return jnp.stack(gathered)


def partner_stack(coefs, stride):
    gathered = []
    for offset in list(range(-FAR_REACH, 0)) + list(range(1, FAR_REACH + 1)):
        gathered.append(from_behind(coefs, AX, -offset * stride))
    stacked = jnp.stack(gathered)

    def slot_of(distance):
        return distance + FAR_REACH - (distance > 0).astype(jnp.int32)

    return (stacked, slot_of)


def middle_level(coefs, skeletons, lists, transfer_rows, above, stride, device):
    rank_rows = coefs.shape[0] // stride
    cluster = device // stride
    member = device % stride
    own_full = lax.dynamic_index_in_dim(skeletons, cluster, 0, keepdims=False)
    own_coords = lax.dynamic_slice_in_dim(own_full, member * rank_rows, rank_rows, 1)
    stacked, slot_of = partner_stack(coefs, stride)
    entries = lax.dynamic_index_in_dim(lists, cluster, 0, keepdims=False)
    chosen = jnp.maximum(entries, 0)
    coords = jnp.take(skeletons, chosen, axis=0)
    slots = jnp.clip(slot_of(chosen - cluster), 0, stacked.shape[0] - 1)
    values = jnp.take(stacked, slots, axis=0)
    rows_here = batched_far(own_coords, coords, values, entries >= 0) + jnp.dot(
        transfer_rows, above, precision=HIGHEST
    )
    return join_rows(rows_here, stride.bit_length() - 1, device)


def cluster_gather(block, device, clusters):
    gathered = block[None]
    for level in range(clusters.bit_length() - 1):
        bit_index = 3 + level
        other = from_partner(gathered, AX, bit_index)
        upper = device // 2**bit_index % 2
        gathered = jnp.where(
            upper == 0,
            jnp.concatenate([gathered, other], 0),
            jnp.concatenate([other, gathered], 0),
        )
    return gathered


def near_sum(own_points, near_entries, shipped, device):
    leaf_points = own_points.shape[1]
    point_rows = leaf_points + 3 * leaf_points // shipped.shape[1]

    def contribution(block, distance):
        listed = jnp.any(near_entries == device + distance)
        coords = block[leaf_points:point_rows].reshape(3, leaf_points)
        contrib = jnp.dot(
            kernel_block(own_points, coords), block[:leaf_points], precision=lax.Precision.HIGH
        )
        return jnp.where(listed, contrib, 0.0)

    total = contribution(shipped, 0)
    ahead = shipped
    behind = shipped
    rim = [None] * (2 * REACH + 1)
    rim[REACH] = shipped[point_rows:]
    for step in range(1, REACH + 1):
        ahead = from_behind(ahead, AX, 1)
        behind = from_behind(behind, AX, -1)
        rim[REACH - step] = ahead[point_rows:]
        rim[REACH + step] = behind[point_rows:]
        total = total + contribution(ahead, -step) + contribution(behind, step)
    return total, jnp.stack(rim)


def slot_of(distance):
    return distance + FAR_REACH - (distance > 0).astype(jnp.int32)


def middle_full(stacked, skeletons, lists, transfer, above, stride, device):
    cluster = device // stride
    own_coords = lax.dynamic_index_in_dim(skeletons, cluster, 0, keepdims=False)
    entries = lax.dynamic_index_in_dim(lists, cluster, 0, keepdims=False)
    chosen = jnp.maximum(entries, 0)
    coords = jnp.take(skeletons, chosen, axis=0)
    slots = jnp.clip(slot_of(chosen - cluster), 0, stacked.shape[0] - 1)
    values = jnp.take(stacked, slots, axis=0)
    return batched_far(own_coords, coords, values, entries >= 0) + jnp.dot(
        transfer, above, precision=HIGHEST
    )


OFFSETS = tuple(range(-FAR_REACH, 0)) + tuple(range(1, FAR_REACH + 1))


def device_coords(linear):
    return (linear // 8, linear // 4 % 2, linear // 2 % 2, linear % 2)


def exchange_kernel(
    clusters,
    top_ref,
    pair_ref,
    quad_ref,
    top_out,
    pair_out,
    quad_out,
    top_land,
    pair_land,
    quad_land,
    top_send,
    top_recv,
    pair_send,
    pair_recv,
    quad_send,
    quad_recv,
):
    me = lax.axis_index("cl")
    dev = lax.axis_index(AX)
    count = clusters * 8
    mesh_id = pl.DeviceIdType.MESH
    pair_land[...] = jnp.zeros(pair_land.shape, jnp.float32)
    quad_land[...] = jnp.zeros(quad_land.shape, jnp.float32)
    barrier = pltpu.get_barrier_semaphore()
    extra = (-12, -6, -4, -2, 2, 4, 6, 12)

    def inside(delta):
        return jnp.logical_and(dev + delta >= 0, dev + delta < count)

    def greet(step, carry):
        peer = lax.rem(me + step, clusters)
        pl.semaphore_signal(barrier, inc=1, device_id={"cl": peer}, device_id_type=mesh_id)
        return carry

    lax.fori_loop(1, clusters, greet, 0)
    for delta in extra:
        pl.semaphore_signal(
            barrier,
            inc=1,
            device_id=device_coords(lax.rem(dev + delta + count, count)),
            device_id_type=mesh_id,
        )
    pl.semaphore_wait(barrier, clusters - 1 + len(extra))

    def outgoing(step):
        peer = lax.rem(me + step, clusters)
        return pltpu.make_async_remote_copy(
            src_ref=top_ref,
            dst_ref=top_land.at[me],
            send_sem=top_send.at[step],
            recv_sem=top_recv.at[me],
            device_id={"cl": peer},
            device_id_type=mesh_id,
        )

    def incoming(step):
        source = lax.rem(me - step + clusters, clusters)
        return pltpu.make_async_remote_copy(
            src_ref=top_ref,
            dst_ref=top_land.at[source],
            send_sem=top_send.at[step],
            recv_sem=top_recv.at[source],
            device_id={"cl": source},
            device_id_type=mesh_id,
        )

    def partner_copy(src, land, send_sem, recv_sem, slot, target):
        return pltpu.make_async_remote_copy(
            src_ref=src,
            dst_ref=land.at[slot],
            send_sem=send_sem.at[slot],
            recv_sem=recv_sem.at[slot],
            device_id=device_coords(target),
            device_id_type=mesh_id,
        )

    partners = (
        (pair_ref, pair_land, pair_send, pair_recv, 2),
        (quad_ref, quad_land, quad_send, quad_recv, 4),
    )
    for src, land, send_sem, recv_sem, stride in partners:
        for slot, offset in enumerate(OFFSETS):

            @pl.when(inside(-offset * stride))
            def _():
                partner_copy(src, land, send_sem, recv_sem, slot, dev - offset * stride).start()

    def send(step, carry):
        outgoing(step).start()
        return carry

    lax.fori_loop(1, clusters, send, 0)
    top_land[me] = top_ref[...]

    def finish(step, carry):
        outgoing(step).wait_send()
        incoming(step).wait_recv()
        return carry

    lax.fori_loop(1, clusters, finish, 0)
    for src, land, send_sem, recv_sem, stride in partners:
        for slot, offset in enumerate(OFFSETS):

            @pl.when(inside(-offset * stride))
            def _():
                partner_copy(src, land, send_sem, recv_sem, slot, dev - offset * stride).wait_send()

            @pl.when(inside(offset * stride))
            def _():
                partner_copy(src, land, send_sem, recv_sem, slot, dev + offset * stride).wait_recv()

    top_out[...] = top_land[...]
    pair_out[...] = pair_land[...]
    quad_out[...] = quad_land[...]


def exchange(top_block, coef_pair, coef_quad):
    clusters = lax.axis_size("cl")
    rows, cols = top_block.shape
    stack = (len(OFFSETS),) + coef_pair.shape
    vmem = pl.BlockSpec(memory_space=pltpu.VMEM)
    return pl.pallas_call(
        functools.partial(exchange_kernel, clusters),
        out_shape=(
            jax.ShapeDtypeStruct((clusters, rows, cols), jnp.float32),
            jax.ShapeDtypeStruct(stack, jnp.float32),
            jax.ShapeDtypeStruct(stack, jnp.float32),
        ),
        in_specs=[vmem] * 3,
        out_specs=(vmem, vmem, vmem),
        scratch_shapes=[
            pltpu.VMEM((clusters, rows, cols), jnp.float32),
            pltpu.VMEM(stack, jnp.float32),
            pltpu.VMEM(stack, jnp.float32),
            pltpu.SemaphoreType.DMA((clusters,)),
            pltpu.SemaphoreType.DMA((clusters,)),
            pltpu.SemaphoreType.DMA((len(OFFSETS),)),
            pltpu.SemaphoreType.DMA((len(OFFSETS),)),
            pltpu.SemaphoreType.DMA((len(OFFSETS),)),
            pltpu.SemaphoreType.DMA((len(OFFSETS),)),
        ],
        compiler_params=pltpu.CompilerParams(collective_id=0, has_side_effects=True),
    )(top_block, coef_pair, coef_quad)


def per_device(
    vectors,
    points,
    leaf_basis,
    transfer_leaf,
    transfer_pair,
    transfer_quad,
    skel_leaf,
    skel_pair,
    skel_quad,
    skel_top,
    near_list,
    far_leaf,
    far_pair,
    far_quad,
    far_top,
):
    leaf_points = vectors.shape[1]
    width = vectors.shape[2]
    rank = leaf_basis.shape[2]
    device = lax.axis_index(AX)
    own_points = points[0]
    coef_leaf = transposed_dot(leaf_basis[0], vectors[0])
    pair_matrix = join_rows(transfer_pair, 1, device)
    quad_matrix = join_rows(transfer_quad, 2, device)
    up_pair = transposed_dot(transfer_leaf[0], coef_leaf)
    up_quad = transposed_dot(pair_matrix, up_pair)
    up_top = transposed_dot(quad_matrix, up_quad)
    first = jnp.stack([up_pair, up_quad, up_top])
    first = first + from_partner(first, AX, 0)
    coef_pair = first[0]
    second = first[1:] + from_partner(first[1:], AX, 1)
    coef_quad = second[0]
    coef_top = second[1] + from_partner(second[1], AX, 2)
    shipped = jnp.concatenate(
        [vectors[0], own_points.reshape(3 * leaf_points // width, width), coef_leaf, skel_leaf[0]],
        axis=0,
    )
    near_field, leaf_rim = near_sum(own_points, near_list[0], shipped, device)
    top_cluster = device // 8
    top_member = device % 8
    share = width // 8
    top_cols_own = lax.dynamic_slice_in_dim(coef_top.T, top_member * share, share, 0)
    top_t, pair_stack, quad_stack = exchange(top_cols_own, coef_pair, coef_quad)
    all_top = jnp.swapaxes(top_t, 1, 2)
    top_coords = lax.dynamic_index_in_dim(skel_top, top_cluster, 0, keepdims=False)
    top_entries = lax.dynamic_index_in_dim(far_top, top_cluster, 0, keepdims=False)
    top_chosen = jnp.maximum(top_entries, 0)
    top_cols = batched_far(
        top_coords,
        jnp.take(skel_top, top_chosen, axis=0),
        jnp.take(all_top, top_chosen, axis=0),
        top_entries >= 0,
    )
    local_top = lax.all_gather(top_cols, MEMBERS, axis=1, tiled=True)
    local_quad = middle_full(quad_stack, skel_quad, far_quad, quad_matrix, local_top, 4, device)
    local_pair = middle_full(pair_stack, skel_pair, far_pair, pair_matrix, local_quad, 2, device)
    leaf_entries = far_leaf[0]
    positions = jnp.clip(jnp.maximum(leaf_entries, 0) - device + REACH, 0, 2 * REACH)
    leaf_blocks = jnp.take(leaf_rim, positions, axis=0)
    local_leaf = batched_far(
        skel_leaf[0], leaf_blocks[:, rank:], leaf_blocks[:, :rank], leaf_entries >= 0
    ) + jnp.dot(transfer_leaf[0], local_pair, precision=HIGHEST)
    product = near_field + jnp.dot(leaf_basis[0], local_leaf, precision=HIGHEST)
    return product[None]


def solution(mesh):
    count = mesh.devices.size
    grid = Mesh(mesh.devices.reshape(count // 8, 2, 2, 2), AX)
    spread = P(AX, None, None)
    rows = P(AX, None)
    placed = (
        spread,
        spread,
        spread,
        spread,
        rows,
        rows,
        spread,
        P(),
        P(),
        P(),
        rows,
        rows,
        P(),
        P(),
        P(),
    )
    return jax.shard_map(per_device, mesh=grid, in_specs=placed, out_specs=spread, check_vma=False)
```

```python
import functools

import jax
import jax.numpy as jnp
from jax import lax
from jax.experimental import pallas as pl
from jax.experimental.pallas import tpu as pltpu
from jax.sharding import Mesh
from jax.sharding import PartitionSpec as P

REACH = 8
FAR_REACH = 4


INV_FOUR_PI = 0.07957747154594767
DELTA_SQ = 0.01
HIGHEST = lax.Precision.HIGHEST

AX = ("cl", "q", "p", "c")
MEMBERS = ("q", "p", "c")


def from_partner(value, axis, bit):
    mask = 2**bit
    pairs = [(source, source ^ mask) for source in range(lax.axis_size(axis))]
    return lax.ppermute(value, axis, pairs)


def from_behind(block, axis, distance):
    devices = range(lax.axis_size(axis))
    route = [(i - distance, i) for i in devices if i - distance in devices]
    return lax.ppermute(block, axis, route)


def kernel_block(left_pts, right_pts):
    distance = jnp.zeros((left_pts.shape[1], right_pts.shape[1]), jnp.float32)
    for axis_id in range(3):
        offset_gap = left_pts[axis_id][:, None] - right_pts[axis_id][None, :]
        distance = distance + offset_gap * offset_gap
    return INV_FOUR_PI * lax.rsqrt(distance + DELTA_SQ)


def transposed_dot(matrix, values):
    return lax.dot_general(matrix, values, (((0,), (0,)), ((), ())), precision=HIGHEST)


def listed_sum(own_coords, entries, fetcher, width):

    def advance(running, partner):
        coords, values = fetcher(jnp.maximum(partner, 0))
        contrib = jnp.dot(kernel_block(own_coords, coords), values, precision=HIGHEST)
        return (running + jnp.where(partner >= 0, contrib, 0.0), None)

    start_value = jnp.zeros((own_coords.shape[1], width), jnp.float32)
    result, _ = lax.scan(advance, start_value, entries)
    return result


def batched_far(own_coords, coords, values, valid):
    count, _, span = coords.shape
    right = jnp.transpose(coords, (1, 0, 2)).reshape(3, count * span)
    masked = jnp.where(valid[:, None, None], values, 0.0)
    flat = masked.reshape(count * span, values.shape[2])
    return jnp.dot(kernel_block(own_coords, right), flat, precision=HIGHEST)


def pair_total(partial_value, levels):
    for bit_index in range(levels):
        partial_value = partial_value + from_partner(partial_value, AX, bit_index)
    return partial_value


def join_rows(block, levels, device):
    for bit_index in range(levels):
        other = from_partner(block, AX, bit_index)
        upper = device // 2**bit_index % 2
        block = jnp.where(
            upper == 0, jnp.concatenate([block, other], 0), jnp.concatenate([other, block], 0)
        )
    return block


def window(shipped):
    gathered = []
    for distance in range(-REACH, REACH + 1):
        if distance == 0:
            gathered.append(shipped)
        else:
            gathered.append(from_behind(shipped, AX, -distance))
    return jnp.stack(gathered)


def partner_stack(coefs, stride):
    gathered = []
    for offset in list(range(-FAR_REACH, 0)) + list(range(1, FAR_REACH + 1)):
        gathered.append(from_behind(coefs, AX, -offset * stride))
    stacked = jnp.stack(gathered)

    def slot_of(distance):
        return distance + FAR_REACH - (distance > 0).astype(jnp.int32)

    return (stacked, slot_of)


def middle_level(coefs, skeletons, lists, transfer_rows, above, stride, device):
    rank_rows = coefs.shape[0] // stride
    cluster = device // stride
    member = device % stride
    own_full = lax.dynamic_index_in_dim(skeletons, cluster, 0, keepdims=False)
    own_coords = lax.dynamic_slice_in_dim(own_full, member * rank_rows, rank_rows, 1)
    stacked, slot_of = partner_stack(coefs, stride)
    entries = lax.dynamic_index_in_dim(lists, cluster, 0, keepdims=False)
    chosen = jnp.maximum(entries, 0)
    coords = jnp.take(skeletons, chosen, axis=0)
    slots = jnp.clip(slot_of(chosen - cluster), 0, stacked.shape[0] - 1)
    values = jnp.take(stacked, slots, axis=0)
    rows_here = batched_far(own_coords, coords, values, entries >= 0) + jnp.dot(
        transfer_rows, above, precision=HIGHEST
    )
    return join_rows(rows_here, stride.bit_length() - 1, device)


def cluster_gather(block, device, clusters):
    gathered = block[None]
    for level in range(clusters.bit_length() - 1):
        bit_index = 3 + level
        other = from_partner(gathered, AX, bit_index)
        upper = device // 2**bit_index % 2
        gathered = jnp.where(
            upper == 0,
            jnp.concatenate([gathered, other], 0),
            jnp.concatenate([other, gathered], 0),
        )
    return gathered


def near_sum(own_points, near_entries, shipped, device):
    leaf_points = own_points.shape[1]
    point_rows = leaf_points + 3 * leaf_points // shipped.shape[1]

    def contribution(block, distance):
        listed = jnp.any(near_entries == device + distance)
        coords = block[leaf_points:point_rows].reshape(3, leaf_points)
        contrib = jnp.dot(
            kernel_block(own_points, coords), block[:leaf_points], precision=lax.Precision.HIGH
        )
        return jnp.where(listed, contrib, 0.0)

    total = contribution(shipped, 0)
    ahead = shipped
    behind = shipped
    rim = [None] * (2 * REACH + 1)
    rim[REACH] = shipped[point_rows:]
    for step in range(1, REACH + 1):
        ahead = from_behind(ahead, AX, 1)
        behind = from_behind(behind, AX, -1)
        rim[REACH - step] = ahead[point_rows:]
        rim[REACH + step] = behind[point_rows:]
        total = total + contribution(ahead, -step) + contribution(behind, step)
    return total, jnp.stack(rim)


def slot_of(distance):
    return distance + FAR_REACH - (distance > 0).astype(jnp.int32)


def middle_full(stacked, skeletons, lists, transfer, above, stride, device):
    cluster = device // stride
    own_coords = lax.dynamic_index_in_dim(skeletons, cluster, 0, keepdims=False)
    entries = lax.dynamic_index_in_dim(lists, cluster, 0, keepdims=False)
    chosen = jnp.maximum(entries, 0)
    coords = jnp.take(skeletons, chosen, axis=0)
    slots = jnp.clip(slot_of(chosen - cluster), 0, stacked.shape[0] - 1)
    values = jnp.take(stacked, slots, axis=0)
    return batched_far(own_coords, coords, values, entries >= 0) + jnp.dot(
        transfer, above, precision=HIGHEST
    )


OFFSETS = tuple(range(-FAR_REACH, 0)) + tuple(range(1, FAR_REACH + 1))


def device_coords(linear):
    return (linear // 8, linear // 4 % 2, linear // 2 % 2, linear % 2)


def exchange_kernel(
    clusters,
    top_ref,
    pair_ref,
    top_out,
    pair_out,
    top_land,
    pair_land,
    top_send,
    top_recv,
    pair_send,
    pair_recv,
):
    me = lax.axis_index("cl")
    dev = lax.axis_index(AX)
    count = clusters * 8
    mesh_id = pl.DeviceIdType.MESH
    pair_land[...] = jnp.zeros(pair_land.shape, jnp.float32)
    barrier = pltpu.get_barrier_semaphore()
    extra = (-6, -4, -2, 2, 4, 6)

    def inside(delta):
        return jnp.logical_and(dev + delta >= 0, dev + delta < count)

    def greet(step, carry):
        peer = lax.rem(me + step, clusters)
        pl.semaphore_signal(barrier, inc=1, device_id={"cl": peer}, device_id_type=mesh_id)
        return carry

    lax.fori_loop(1, clusters, greet, 0)
    for delta in extra:
        pl.semaphore_signal(
            barrier,
            inc=1,
            device_id=device_coords(lax.rem(dev + delta + count, count)),
            device_id_type=mesh_id,
        )
    pl.semaphore_wait(barrier, clusters - 1 + len(extra))

    def outgoing(step):
        peer = lax.rem(me + step, clusters)
        return pltpu.make_async_remote_copy(
            src_ref=top_ref,
            dst_ref=top_land.at[me],
            send_sem=top_send.at[step],
            recv_sem=top_recv.at[me],
            device_id={"cl": peer},
            device_id_type=mesh_id,
        )

    def incoming(step):
        source = lax.rem(me - step + clusters, clusters)
        return pltpu.make_async_remote_copy(
            src_ref=top_ref,
            dst_ref=top_land.at[source],
            send_sem=top_send.at[step],
            recv_sem=top_recv.at[source],
            device_id={"cl": source},
            device_id_type=mesh_id,
        )

    def partner_copy(src, land, send_sem, recv_sem, slot, target):
        return pltpu.make_async_remote_copy(
            src_ref=src,
            dst_ref=land.at[slot],
            send_sem=send_sem.at[slot],
            recv_sem=recv_sem.at[slot],
            device_id=device_coords(target),
            device_id_type=mesh_id,
        )

    partners = ((pair_ref, pair_land, pair_send, pair_recv, 2),)
    for src, land, send_sem, recv_sem, stride in partners:
        for slot, offset in enumerate(OFFSETS):

            @pl.when(inside(-offset * stride))
            def _():
                partner_copy(src, land, send_sem, recv_sem, slot, dev - offset * stride).start()

    def send(step, carry):
        outgoing(step).start()
        return carry

    lax.fori_loop(1, clusters, send, 0)
    top_land[me] = top_ref[...]

    def finish(step, carry):
        outgoing(step).wait_send()
        incoming(step).wait_recv()
        return carry

    lax.fori_loop(1, clusters, finish, 0)
    for src, land, send_sem, recv_sem, stride in partners:
        for slot, offset in enumerate(OFFSETS):

            @pl.when(inside(-offset * stride))
            def _():
                partner_copy(src, land, send_sem, recv_sem, slot, dev - offset * stride).wait_send()

            @pl.when(inside(offset * stride))
            def _():
                partner_copy(src, land, send_sem, recv_sem, slot, dev + offset * stride).wait_recv()

    top_out[...] = top_land[...]
    pair_out[...] = pair_land[...]


def exchange(top_block, coef_pair):
    clusters = lax.axis_size("cl")
    rows, cols = top_block.shape
    stack = (len(OFFSETS),) + coef_pair.shape
    vmem = pl.BlockSpec(memory_space=pltpu.VMEM)
    return pl.pallas_call(
        functools.partial(exchange_kernel, clusters),
        out_shape=(
            jax.ShapeDtypeStruct((clusters, rows, cols), jnp.float32),
            jax.ShapeDtypeStruct(stack, jnp.float32),
        ),
        in_specs=[vmem] * 2,
        out_specs=(vmem, vmem),
        scratch_shapes=[
            pltpu.VMEM((clusters, rows, cols), jnp.float32),
            pltpu.VMEM(stack, jnp.float32),
            pltpu.SemaphoreType.DMA((clusters,)),
            pltpu.SemaphoreType.DMA((clusters,)),
            pltpu.SemaphoreType.DMA((len(OFFSETS),)),
            pltpu.SemaphoreType.DMA((len(OFFSETS),)),
        ],
        compiler_params=pltpu.CompilerParams(collective_id=0, has_side_effects=True),
    )(top_block, coef_pair)


def per_device(
    vectors,
    points,
    leaf_basis,
    transfer_leaf,
    transfer_pair,
    transfer_quad,
    skel_leaf,
    skel_pair,
    skel_quad,
    skel_top,
    near_list,
    far_leaf,
    far_pair,
    far_quad,
    far_top,
):
    leaf_points = vectors.shape[1]
    width = vectors.shape[2]
    rank = leaf_basis.shape[2]
    device = lax.axis_index(AX)
    own_points = points[0]
    coef_leaf = transposed_dot(leaf_basis[0], vectors[0])
    pair_matrix = join_rows(transfer_pair, 1, device)
    quad_matrix = join_rows(transfer_quad, 2, device)
    up_pair = transposed_dot(transfer_leaf[0], coef_leaf)
    up_quad = transposed_dot(pair_matrix, up_pair)
    up_top = transposed_dot(quad_matrix, up_quad)
    first = jnp.stack([up_pair, up_quad, up_top])
    first = first + from_partner(first, AX, 0)
    coef_pair = first[0]
    second = first[1:] + from_partner(first[1:], AX, 1)
    coef_quad = second[0]
    coef_top = second[1] + from_partner(second[1], AX, 2)
    shipped = jnp.concatenate(
        [vectors[0], own_points.reshape(3 * leaf_points // width, width), coef_leaf, skel_leaf[0]],
        axis=0,
    )
    near_field, leaf_rim = near_sum(own_points, near_list[0], shipped, device)
    top_cluster = device // 8
    top_member = device % 8
    share = width // 8
    top_cols_own = lax.dynamic_slice_in_dim(coef_top.T, top_member * share, share, 0)
    quad_stack, _ = partner_stack(coef_quad, 4)
    top_t, pair_stack = exchange(top_cols_own, coef_pair)
    all_top = jnp.swapaxes(top_t, 1, 2)
    top_coords = lax.dynamic_index_in_dim(skel_top, top_cluster, 0, keepdims=False)
    top_entries = lax.dynamic_index_in_dim(far_top, top_cluster, 0, keepdims=False)
    top_chosen = jnp.maximum(top_entries, 0)
    top_cols = batched_far(
        top_coords,
        jnp.take(skel_top, top_chosen, axis=0),
        jnp.take(all_top, top_chosen, axis=0),
        top_entries >= 0,
    )
    local_top = lax.all_gather(top_cols, MEMBERS, axis=1, tiled=True)
    local_quad = middle_full(quad_stack, skel_quad, far_quad, quad_matrix, local_top, 4, device)
    local_pair = middle_full(pair_stack, skel_pair, far_pair, pair_matrix, local_quad, 2, device)
    leaf_entries = far_leaf[0]
    positions = jnp.clip(jnp.maximum(leaf_entries, 0) - device + REACH, 0, 2 * REACH)
    leaf_blocks = jnp.take(leaf_rim, positions, axis=0)
    local_leaf = batched_far(
        skel_leaf[0], leaf_blocks[:, rank:], leaf_blocks[:, :rank], leaf_entries >= 0
    ) + jnp.dot(transfer_leaf[0], local_pair, precision=HIGHEST)
    product = near_field + jnp.dot(leaf_basis[0], local_leaf, precision=HIGHEST)
    return product[None]


def solution(mesh):
    count = mesh.devices.size
    grid = Mesh(mesh.devices.reshape(count // 8, 2, 2, 2), AX)
    spread = P(AX, None, None)
    rows = P(AX, None)
    placed = (
        spread,
        spread,
        spread,
        spread,
        rows,
        rows,
        spread,
        P(),
        P(),
        P(),
        rows,
        rows,
        P(),
        P(),
        P(),
    )
    return jax.shard_map(per_device, mesh=grid, in_specs=placed, out_specs=spread, check_vma=False)
```

```python
import functools

import jax
import jax.numpy as jnp
from jax import lax
from jax.experimental import pallas as pl
from jax.experimental.pallas import tpu as pltpu
from jax.sharding import Mesh
from jax.sharding import PartitionSpec as P

REACH = 8
FAR_REACH = 4


INV_FOUR_PI = 0.07957747154594767
DELTA_SQ = 0.01
HIGHEST = lax.Precision.HIGHEST

AX = ("cl", "q", "p", "c")
MEMBERS = ("q", "p", "c")


def from_partner(value, axis, bit):
    mask = 2**bit
    pairs = [(source, source ^ mask) for source in range(lax.axis_size(axis))]
    return lax.ppermute(value, axis, pairs)


def from_behind(block, axis, distance):
    devices = range(lax.axis_size(axis))
    route = [(i - distance, i) for i in devices if i - distance in devices]
    return lax.ppermute(block, axis, route)


def kernel_block(left_pts, right_pts):
    distance = jnp.zeros((left_pts.shape[1], right_pts.shape[1]), jnp.float32)
    for axis_id in range(3):
        offset_gap = left_pts[axis_id][:, None] - right_pts[axis_id][None, :]
        distance = distance + offset_gap * offset_gap
    return INV_FOUR_PI * lax.rsqrt(distance + DELTA_SQ)


def transposed_dot(matrix, values):
    return lax.dot_general(matrix, values, (((0,), (0,)), ((), ())), precision=HIGHEST)


def listed_sum(own_coords, entries, fetcher, width):

    def advance(running, partner):
        coords, values = fetcher(jnp.maximum(partner, 0))
        contrib = jnp.dot(kernel_block(own_coords, coords), values, precision=HIGHEST)
        return (running + jnp.where(partner >= 0, contrib, 0.0), None)

    start_value = jnp.zeros((own_coords.shape[1], width), jnp.float32)
    result, _ = lax.scan(advance, start_value, entries)
    return result


def batched_far(own_coords, coords, values, valid):
    count, _, span = coords.shape
    right = jnp.transpose(coords, (1, 0, 2)).reshape(3, count * span)
    masked = jnp.where(valid[:, None, None], values, 0.0)
    flat = masked.reshape(count * span, values.shape[2])
    return jnp.dot(kernel_block(own_coords, right), flat, precision=HIGHEST)


def pair_total(partial_value, levels):
    for bit_index in range(levels):
        partial_value = partial_value + from_partner(partial_value, AX, bit_index)
    return partial_value


def join_rows(block, levels, device):
    for bit_index in range(levels):
        other = from_partner(block, AX, bit_index)
        upper = device // 2**bit_index % 2
        block = jnp.where(
            upper == 0, jnp.concatenate([block, other], 0), jnp.concatenate([other, block], 0)
        )
    return block


def window(shipped):
    gathered = []
    for distance in range(-REACH, REACH + 1):
        if distance == 0:
            gathered.append(shipped)
        else:
            gathered.append(from_behind(shipped, AX, -distance))
    return jnp.stack(gathered)


def partner_stack(coefs, stride):
    gathered = []
    for offset in list(range(-FAR_REACH, 0)) + list(range(1, FAR_REACH + 1)):
        gathered.append(from_behind(coefs, AX, -offset * stride))
    stacked = jnp.stack(gathered)

    def slot_of(distance):
        return distance + FAR_REACH - (distance > 0).astype(jnp.int32)

    return (stacked, slot_of)


def middle_level(coefs, skeletons, lists, transfer_rows, above, stride, device):
    rank_rows = coefs.shape[0] // stride
    cluster = device // stride
    member = device % stride
    own_full = lax.dynamic_index_in_dim(skeletons, cluster, 0, keepdims=False)
    own_coords = lax.dynamic_slice_in_dim(own_full, member * rank_rows, rank_rows, 1)
    stacked, slot_of = partner_stack(coefs, stride)
    entries = lax.dynamic_index_in_dim(lists, cluster, 0, keepdims=False)
    chosen = jnp.maximum(entries, 0)
    coords = jnp.take(skeletons, chosen, axis=0)
    slots = jnp.clip(slot_of(chosen - cluster), 0, stacked.shape[0] - 1)
    values = jnp.take(stacked, slots, axis=0)
    rows_here = batched_far(own_coords, coords, values, entries >= 0) + jnp.dot(
        transfer_rows, above, precision=HIGHEST
    )
    return join_rows(rows_here, stride.bit_length() - 1, device)


def cluster_gather(block, device, clusters):
    gathered = block[None]
    for level in range(clusters.bit_length() - 1):
        bit_index = 3 + level
        other = from_partner(gathered, AX, bit_index)
        upper = device // 2**bit_index % 2
        gathered = jnp.where(
            upper == 0,
            jnp.concatenate([gathered, other], 0),
            jnp.concatenate([other, gathered], 0),
        )
    return gathered


def near_sum(own_points, near_entries, shipped, device):
    leaf_points = own_points.shape[1]
    point_rows = leaf_points + 3 * leaf_points // shipped.shape[1]

    def contribution(block, distance):
        listed = jnp.any(near_entries == device + distance)
        coords = block[leaf_points:point_rows].reshape(3, leaf_points)
        contrib = jnp.dot(
            kernel_block(own_points, coords), block[:leaf_points], precision=lax.Precision.HIGH
        )
        return jnp.where(listed, contrib, 0.0)

    total = contribution(shipped, 0)
    ahead = shipped
    behind = shipped
    rim = [None] * (2 * REACH + 1)
    rim[REACH] = shipped[point_rows:]
    for step in range(1, REACH + 1):
        ahead = from_behind(ahead, AX, 1)
        behind = from_behind(behind, AX, -1)
        rim[REACH - step] = ahead[point_rows:]
        rim[REACH + step] = behind[point_rows:]
        total = total + contribution(ahead, -step) + contribution(behind, step)
    return total, jnp.stack(rim)


def slot_of(distance):
    return distance + FAR_REACH - (distance > 0).astype(jnp.int32)


def middle_full(stacked, skeletons, lists, transfer, above, stride, device):
    cluster = device // stride
    own_coords = lax.dynamic_index_in_dim(skeletons, cluster, 0, keepdims=False)
    entries = lax.dynamic_index_in_dim(lists, cluster, 0, keepdims=False)
    chosen = jnp.maximum(entries, 0)
    coords = jnp.take(skeletons, chosen, axis=0)
    slots = jnp.clip(slot_of(chosen - cluster), 0, stacked.shape[0] - 1)
    values = jnp.take(stacked, slots, axis=0)
    return batched_far(own_coords, coords, values, entries >= 0) + jnp.dot(
        transfer, above, precision=HIGHEST
    )


OFFSETS = tuple(range(-FAR_REACH, 0)) + tuple(range(1, FAR_REACH + 1))


def device_coords(linear):
    return (linear // 8, linear // 4 % 2, linear // 2 % 2, linear % 2)


def exchange_kernel(
    clusters,
    top_ref,
    pair_ref,
    quad_ref,
    top_out,
    pair_out,
    quad_out,
    top_land,
    pair_land,
    quad_land,
    top_send,
    top_recv,
    pair_send,
    pair_recv,
    quad_send,
    quad_recv,
):
    me = lax.axis_index("cl")
    dev = lax.axis_index(AX)
    count = clusters * 8
    mesh_id = pl.DeviceIdType.MESH
    pair_land[...] = jnp.zeros(pair_land.shape, jnp.float32)
    quad_land[...] = jnp.zeros(quad_land.shape, jnp.float32)
    barrier = pltpu.get_barrier_semaphore()
    extra = (-12, -6, -4, -2, 2, 4, 6, 12)

    def inside(delta):
        return jnp.logical_and(dev + delta >= 0, dev + delta < count)

    def greet(step, carry):
        peer = lax.rem(me + step, clusters)
        pl.semaphore_signal(barrier, inc=1, device_id={"cl": peer}, device_id_type=mesh_id)
        return carry

    lax.fori_loop(1, clusters, greet, 0)
    for delta in extra:
        pl.semaphore_signal(
            barrier,
            inc=1,
            device_id=device_coords(lax.rem(dev + delta + count, count)),
            device_id_type=mesh_id,
        )
    pl.semaphore_wait(barrier, clusters - 1 + len(extra))

    def outgoing(step):
        peer = lax.rem(me + step, clusters)
        return pltpu.make_async_remote_copy(
            src_ref=top_ref,
            dst_ref=top_land.at[me],
            send_sem=top_send.at[step],
            recv_sem=top_recv.at[me],
            device_id={"cl": peer},
            device_id_type=mesh_id,
        )

    def incoming(step):
        source = lax.rem(me - step + clusters, clusters)
        return pltpu.make_async_remote_copy(
            src_ref=top_ref,
            dst_ref=top_land.at[source],
            send_sem=top_send.at[step],
            recv_sem=top_recv.at[source],
            device_id={"cl": source},
            device_id_type=mesh_id,
        )

    def partner_copy(src, land, send_sem, recv_sem, slot, target):
        return pltpu.make_async_remote_copy(
            src_ref=src,
            dst_ref=land.at[slot],
            send_sem=send_sem.at[slot],
            recv_sem=recv_sem.at[slot],
            device_id=device_coords(target),
            device_id_type=mesh_id,
        )

    partners = (
        (pair_ref, pair_land, pair_send, pair_recv, 2),
        (quad_ref, quad_land, quad_send, quad_recv, 4),
    )
    for src, land, send_sem, recv_sem, stride in partners:
        for slot, offset in enumerate(OFFSETS):

            @pl.when(inside(-offset * stride))
            def _():
                partner_copy(src, land, send_sem, recv_sem, slot, dev - offset * stride).start()

    def send(step, carry):
        outgoing(step).start()
        return carry

    lax.fori_loop(1, clusters, send, 0)
    top_land[me] = top_ref[...]

    def finish(step, carry):
        outgoing(step).wait_send()
        incoming(step).wait_recv()
        return carry

    lax.fori_loop(1, clusters, finish, 0)
    for src, land, send_sem, recv_sem, stride in partners:
        for slot, offset in enumerate(OFFSETS):

            @pl.when(inside(-offset * stride))
            def _():
                partner_copy(src, land, send_sem, recv_sem, slot, dev - offset * stride).wait_send()

            @pl.when(inside(offset * stride))
            def _():
                partner_copy(src, land, send_sem, recv_sem, slot, dev + offset * stride).wait_recv()

    top_out[...] = top_land[...]
    pair_out[...] = pair_land[...]
    quad_out[...] = quad_land[...]


def exchange(top_block, coef_pair, coef_quad):
    clusters = lax.axis_size("cl")
    rows, cols = top_block.shape
    stack = (len(OFFSETS),) + coef_pair.shape
    vmem = pl.BlockSpec(memory_space=pltpu.VMEM)
    return pl.pallas_call(
        functools.partial(exchange_kernel, clusters),
        out_shape=(
            jax.ShapeDtypeStruct((clusters, rows, cols), jnp.float32),
            jax.ShapeDtypeStruct(stack, jnp.float32),
            jax.ShapeDtypeStruct(stack, jnp.float32),
        ),
        in_specs=[vmem] * 3,
        out_specs=(vmem, vmem, vmem),
        scratch_shapes=[
            pltpu.VMEM((clusters, rows, cols), jnp.float32),
            pltpu.VMEM(stack, jnp.float32),
            pltpu.VMEM(stack, jnp.float32),
            pltpu.SemaphoreType.DMA((clusters,)),
            pltpu.SemaphoreType.DMA((clusters,)),
            pltpu.SemaphoreType.DMA((len(OFFSETS),)),
            pltpu.SemaphoreType.DMA((len(OFFSETS),)),
            pltpu.SemaphoreType.DMA((len(OFFSETS),)),
            pltpu.SemaphoreType.DMA((len(OFFSETS),)),
        ],
        compiler_params=pltpu.CompilerParams(collective_id=0, has_side_effects=True),
    )(top_block, coef_pair, coef_quad)


def per_device(
    vectors,
    points,
    leaf_basis,
    transfer_leaf,
    transfer_pair,
    transfer_quad,
    skel_leaf,
    skel_pair,
    skel_quad,
    skel_top,
    near_list,
    far_leaf,
    far_pair,
    far_quad,
    far_top,
):
    leaf_points = vectors.shape[1]
    width = vectors.shape[2]
    rank = leaf_basis.shape[2]
    device = lax.axis_index(AX)
    own_points = points[0]
    coef_leaf = transposed_dot(leaf_basis[0], vectors[0])
    pair_matrix = join_rows(transfer_pair, 1, device)
    quad_matrix = join_rows(transfer_quad, 2, device)
    up_pair = transposed_dot(transfer_leaf[0], coef_leaf)
    up_quad = transposed_dot(pair_matrix, up_pair)
    up_top = transposed_dot(quad_matrix, up_quad)
    first = jnp.stack([up_pair, up_quad, up_top])
    first = first + from_partner(first, AX, 0)
    coef_pair = first[0]
    second = first[1:] + from_partner(first[1:], AX, 1)
    coef_quad = second[0]
    coef_top = second[1] + from_partner(second[1], AX, 2)
    shipped = jnp.concatenate(
        [vectors[0], own_points.reshape(3 * leaf_points // width, width), coef_leaf, skel_leaf[0]],
        axis=0,
    )
    near_field, leaf_rim = near_sum(own_points, near_list[0], shipped, device)
    top_cluster = device // 8
    top_member = device % 8
    share = width // 8
    top_cols_own = lax.dynamic_slice_in_dim(coef_top.T, top_member * share, share, 0)
    top_cols_own, near_field = lax.optimization_barrier((top_cols_own, near_field))
    top_t, pair_stack, quad_stack = exchange(top_cols_own, coef_pair, coef_quad)
    all_top = jnp.swapaxes(top_t, 1, 2)
    top_coords = lax.dynamic_index_in_dim(skel_top, top_cluster, 0, keepdims=False)
    top_entries = lax.dynamic_index_in_dim(far_top, top_cluster, 0, keepdims=False)
    top_chosen = jnp.maximum(top_entries, 0)
    top_cols = batched_far(
        top_coords,
        jnp.take(skel_top, top_chosen, axis=0),
        jnp.take(all_top, top_chosen, axis=0),
        top_entries >= 0,
    )
    local_top = lax.all_gather(top_cols, MEMBERS, axis=1, tiled=True)
    local_quad = middle_full(quad_stack, skel_quad, far_quad, quad_matrix, local_top, 4, device)
    local_pair = middle_full(pair_stack, skel_pair, far_pair, pair_matrix, local_quad, 2, device)
    leaf_entries = far_leaf[0]
    positions = jnp.clip(jnp.maximum(leaf_entries, 0) - device + REACH, 0, 2 * REACH)
    leaf_blocks = jnp.take(leaf_rim, positions, axis=0)
    local_leaf = batched_far(
        skel_leaf[0], leaf_blocks[:, rank:], leaf_blocks[:, :rank], leaf_entries >= 0
    ) + jnp.dot(transfer_leaf[0], local_pair, precision=HIGHEST)
    product = near_field + jnp.dot(leaf_basis[0], local_leaf, precision=HIGHEST)
    return product[None]


def solution(mesh):
    count = mesh.devices.size
    grid = Mesh(mesh.devices.reshape(count // 8, 2, 2, 2), AX)
    spread = P(AX, None, None)
    rows = P(AX, None)
    placed = (
        spread,
        spread,
        spread,
        spread,
        rows,
        rows,
        spread,
        P(),
        P(),
        P(),
        rows,
        rows,
        P(),
        P(),
        P(),
    )
    return jax.shard_map(per_device, mesh=grid, in_specs=placed, out_specs=spread, check_vma=False)
```

```python
import functools

import jax
import jax.numpy as jnp
from jax import lax
from jax.experimental import pallas as pl
from jax.experimental.pallas import tpu as pltpu
from jax.sharding import Mesh
from jax.sharding import PartitionSpec as P

REACH = 8
FAR_REACH = 4


INV_FOUR_PI = 0.07957747154594767
DELTA_SQ = 0.01
HIGHEST = lax.Precision.HIGHEST

AX = ("cl", "q", "p", "c")
MEMBERS = ("q", "p", "c")


def from_partner(value, axis, bit):
    mask = 2**bit
    pairs = [(source, source ^ mask) for source in range(lax.axis_size(axis))]
    return lax.ppermute(value, axis, pairs)


def from_behind(block, axis, distance):
    devices = range(lax.axis_size(axis))
    route = [(i - distance, i) for i in devices if i - distance in devices]
    return lax.ppermute(block, axis, route)


def kernel_block(left_pts, right_pts):
    distance = jnp.zeros((left_pts.shape[1], right_pts.shape[1]), jnp.float32)
    for axis_id in range(3):
        offset_gap = left_pts[axis_id][:, None] - right_pts[axis_id][None, :]
        distance = distance + offset_gap * offset_gap
    return INV_FOUR_PI * lax.rsqrt(distance + DELTA_SQ)


def transposed_dot(matrix, values):
    return lax.dot_general(matrix, values, (((0,), (0,)), ((), ())), precision=HIGHEST)


def listed_sum(own_coords, entries, fetcher, width):

    def advance(running, partner):
        coords, values = fetcher(jnp.maximum(partner, 0))
        contrib = jnp.dot(kernel_block(own_coords, coords), values, precision=HIGHEST)
        return (running + jnp.where(partner >= 0, contrib, 0.0), None)

    start_value = jnp.zeros((own_coords.shape[1], width), jnp.float32)
    result, _ = lax.scan(advance, start_value, entries)
    return result


def batched_far(own_coords, coords, values, valid):
    count, _, span = coords.shape
    right = jnp.transpose(coords, (1, 0, 2)).reshape(3, count * span)
    masked = jnp.where(valid[:, None, None], values, 0.0)
    flat = masked.reshape(count * span, values.shape[2])
    return jnp.dot(kernel_block(own_coords, right), flat, precision=HIGHEST)


def pair_total(partial_value, levels):
    for bit_index in range(levels):
        partial_value = partial_value + from_partner(partial_value, AX, bit_index)
    return partial_value


def join_rows(block, levels, device):
    for bit_index in range(levels):
        other = from_partner(block, AX, bit_index)
        upper = device // 2**bit_index % 2
        block = jnp.where(
            upper == 0, jnp.concatenate([block, other], 0), jnp.concatenate([other, block], 0)
        )
    return block


def window(shipped):
    gathered = []
    for distance in range(-REACH, REACH + 1):
        if distance == 0:
            gathered.append(shipped)
        else:
            gathered.append(from_behind(shipped, AX, -distance))
    return jnp.stack(gathered)


def partner_stack(coefs, stride):
    gathered = []
    for offset in list(range(-FAR_REACH, 0)) + list(range(1, FAR_REACH + 1)):
        gathered.append(from_behind(coefs, AX, -offset * stride))
    stacked = jnp.stack(gathered)

    def slot_of(distance):
        return distance + FAR_REACH - (distance > 0).astype(jnp.int32)

    return (stacked, slot_of)


def middle_level(coefs, skeletons, lists, transfer_rows, above, stride, device):
    rank_rows = coefs.shape[0] // stride
    cluster = device // stride
    member = device % stride
    own_full = lax.dynamic_index_in_dim(skeletons, cluster, 0, keepdims=False)
    own_coords = lax.dynamic_slice_in_dim(own_full, member * rank_rows, rank_rows, 1)
    stacked, slot_of = partner_stack(coefs, stride)
    entries = lax.dynamic_index_in_dim(lists, cluster, 0, keepdims=False)
    chosen = jnp.maximum(entries, 0)
    coords = jnp.take(skeletons, chosen, axis=0)
    slots = jnp.clip(slot_of(chosen - cluster), 0, stacked.shape[0] - 1)
    values = jnp.take(stacked, slots, axis=0)
    rows_here = batched_far(own_coords, coords, values, entries >= 0) + jnp.dot(
        transfer_rows, above, precision=HIGHEST
    )
    return join_rows(rows_here, stride.bit_length() - 1, device)


def cluster_gather(block, device, clusters):
    gathered = block[None]
    for level in range(clusters.bit_length() - 1):
        bit_index = 3 + level
        other = from_partner(gathered, AX, bit_index)
        upper = device // 2**bit_index % 2
        gathered = jnp.where(
            upper == 0,
            jnp.concatenate([gathered, other], 0),
            jnp.concatenate([other, gathered], 0),
        )
    return gathered


def near_sum(own_points, near_entries, shipped, device):
    leaf_points = own_points.shape[1]
    point_rows = leaf_points + 3 * leaf_points // shipped.shape[1]

    def contribution(block, distance):
        listed = jnp.any(near_entries == device + distance)
        coords = block[leaf_points:point_rows].reshape(3, leaf_points)
        contrib = jnp.dot(
            kernel_block(own_points, coords), block[:leaf_points], precision=lax.Precision.HIGH
        )
        return jnp.where(listed, contrib, 0.0)

    total = contribution(shipped, 0)
    ahead = shipped
    behind = shipped
    rim = [None] * (2 * REACH + 1)
    rim[REACH] = shipped[point_rows:]
    for step in range(1, REACH + 1):
        ahead = from_behind(ahead, AX, 1)
        behind = from_behind(behind, AX, -1)
        rim[REACH - step] = ahead[point_rows:]
        rim[REACH + step] = behind[point_rows:]
        total = total + contribution(ahead, -step) + contribution(behind, step)
    return total, jnp.stack(rim)


def slot_of(distance):
    return distance + FAR_REACH - (distance > 0).astype(jnp.int32)


def middle_full(stacked, skeletons, lists, transfer, above, stride, device):
    cluster = device // stride
    own_coords = lax.dynamic_index_in_dim(skeletons, cluster, 0, keepdims=False)
    entries = lax.dynamic_index_in_dim(lists, cluster, 0, keepdims=False)
    chosen = jnp.maximum(entries, 0)
    coords = jnp.take(skeletons, chosen, axis=0)
    slots = jnp.clip(slot_of(chosen - cluster), 0, stacked.shape[0] - 1)
    values = jnp.take(stacked, slots, axis=0)
    return batched_far(own_coords, coords, values, entries >= 0) + jnp.dot(
        transfer, above, precision=HIGHEST
    )


OFFSETS = tuple(range(-FAR_REACH, 0)) + tuple(range(1, FAR_REACH + 1))


def device_coords(linear):
    return (linear // 8, linear // 4 % 2, linear // 2 % 2, linear % 2)


def exchange_kernel(
    clusters,
    top_ref,
    pair_ref,
    quad_ref,
    top_out,
    pair_out,
    quad_out,
    top_land,
    pair_land,
    quad_land,
    top_send,
    top_recv,
    pair_send,
    pair_recv,
    quad_send,
    quad_recv,
):
    me = lax.axis_index("cl")
    dev = lax.axis_index(AX)
    count = clusters * 8
    mesh_id = pl.DeviceIdType.MESH
    pair_land[...] = jnp.zeros(pair_land.shape, jnp.float32)
    quad_land[...] = jnp.zeros(quad_land.shape, jnp.float32)
    barrier = pltpu.get_barrier_semaphore()
    extra = (-16, -12, -8, -6, -4, -2, 2, 4, 6, 8, 12, 16)

    def inside(delta):
        return jnp.logical_and(dev + delta >= 0, dev + delta < count)

    rounds = clusters.bit_length() - 1

    def partner_of(level):
        bit = 2**level
        return me + bit - 2 * (me // bit % 2) * bit

    for level in range(rounds):
        pl.semaphore_signal(
            barrier, inc=1, device_id={"cl": partner_of(level)}, device_id_type=mesh_id
        )
    for delta in extra:
        pl.semaphore_signal(
            barrier,
            inc=1,
            device_id=device_coords(lax.rem(dev + delta + count, count)),
            device_id_type=mesh_id,
        )
    pl.semaphore_wait(barrier, rounds + len(extra))

    def doubling(level):
        width = 2**level
        base = me // width * width
        return pltpu.make_async_remote_copy(
            src_ref=top_land.at[pl.ds(base, width)],
            dst_ref=top_land.at[pl.ds(base, width)],
            send_sem=top_send.at[level],
            recv_sem=top_recv.at[level],
            device_id={"cl": partner_of(level)},
            device_id_type=mesh_id,
        )

    def partner_copy(src, land, send_sem, recv_sem, slot, target):
        return pltpu.make_async_remote_copy(
            src_ref=src,
            dst_ref=land.at[slot],
            send_sem=send_sem.at[slot],
            recv_sem=recv_sem.at[slot],
            device_id=device_coords(target),
            device_id_type=mesh_id,
        )

    partners = (
        (pair_ref, pair_land, pair_send, pair_recv, 2),
        (quad_ref, quad_land, quad_send, quad_recv, 4),
    )
    for src, land, send_sem, recv_sem, stride in partners:
        for slot, offset in enumerate(OFFSETS):

            @pl.when(inside(-offset * stride))
            def _():
                partner_copy(src, land, send_sem, recv_sem, slot, dev - offset * stride).start()

    own = pltpu.make_async_copy(top_ref, top_land.at[me], top_send.at[rounds])
    own.start()
    own.wait()
    for level in range(rounds):
        doubling(level).start()
        doubling(level).wait_send()
        doubling(level).wait_recv()
    for src, land, send_sem, recv_sem, stride in partners:
        for slot, offset in enumerate(OFFSETS):

            @pl.when(inside(-offset * stride))
            def _():
                partner_copy(src, land, send_sem, recv_sem, slot, dev - offset * stride).wait_send()

            @pl.when(inside(offset * stride))
            def _():
                partner_copy(src, land, send_sem, recv_sem, slot, dev + offset * stride).wait_recv()

    top_out[...] = top_land[...]
    pair_out[...] = pair_land[...]
    quad_out[...] = quad_land[...]


def exchange(top_block, coef_pair, coef_quad):
    clusters = lax.axis_size("cl")
    rows, cols = top_block.shape
    stack = (len(OFFSETS),) + coef_pair.shape
    vmem = pl.BlockSpec(memory_space=pltpu.VMEM)
    return pl.pallas_call(
        functools.partial(exchange_kernel, clusters),
        out_shape=(
            jax.ShapeDtypeStruct((clusters, rows, cols), jnp.float32),
            jax.ShapeDtypeStruct(stack, jnp.float32),
            jax.ShapeDtypeStruct(stack, jnp.float32),
        ),
        in_specs=[vmem] * 3,
        out_specs=(vmem, vmem, vmem),
        scratch_shapes=[
            pltpu.VMEM((clusters, rows, cols), jnp.float32),
            pltpu.VMEM(stack, jnp.float32),
            pltpu.VMEM(stack, jnp.float32),
            pltpu.SemaphoreType.DMA((clusters,)),
            pltpu.SemaphoreType.DMA((clusters,)),
            pltpu.SemaphoreType.DMA((len(OFFSETS),)),
            pltpu.SemaphoreType.DMA((len(OFFSETS),)),
            pltpu.SemaphoreType.DMA((len(OFFSETS),)),
            pltpu.SemaphoreType.DMA((len(OFFSETS),)),
        ],
        compiler_params=pltpu.CompilerParams(collective_id=0, has_side_effects=True),
    )(top_block, coef_pair, coef_quad)


def per_device(
    vectors,
    points,
    leaf_basis,
    transfer_leaf,
    transfer_pair,
    transfer_quad,
    skel_leaf,
    skel_pair,
    skel_quad,
    skel_top,
    near_list,
    far_leaf,
    far_pair,
    far_quad,
    far_top,
):
    leaf_points = vectors.shape[1]
    width = vectors.shape[2]
    rank = leaf_basis.shape[2]
    device = lax.axis_index(AX)
    own_points = points[0]
    coef_leaf = transposed_dot(leaf_basis[0], vectors[0])
    pair_matrix = join_rows(transfer_pair, 1, device)
    quad_matrix = join_rows(transfer_quad, 2, device)
    up_pair = transposed_dot(transfer_leaf[0], coef_leaf)
    up_quad = transposed_dot(pair_matrix, up_pair)
    up_top = transposed_dot(quad_matrix, up_quad)
    first = jnp.stack([up_pair, up_quad, up_top])
    first = first + from_partner(first, AX, 0)
    coef_pair = first[0]
    second = first[1:] + from_partner(first[1:], AX, 1)
    coef_quad = second[0]
    coef_top = second[1] + from_partner(second[1], AX, 2)
    shipped = jnp.concatenate(
        [vectors[0], own_points.reshape(3 * leaf_points // width, width), coef_leaf, skel_leaf[0]],
        axis=0,
    )
    near_field, leaf_rim = near_sum(own_points, near_list[0], shipped, device)
    top_cluster = device // 8
    top_member = device % 8
    share = width // 8
    top_cols_own = lax.dynamic_slice_in_dim(coef_top.T, top_member * share, share, 0)
    top_cols_own, near_field = lax.optimization_barrier((top_cols_own, near_field))
    top_t, pair_stack, quad_stack = exchange(top_cols_own, coef_pair, coef_quad)
    all_top = jnp.swapaxes(top_t, 1, 2)
    top_coords = lax.dynamic_index_in_dim(skel_top, top_cluster, 0, keepdims=False)
    top_entries = lax.dynamic_index_in_dim(far_top, top_cluster, 0, keepdims=False)
    top_chosen = jnp.maximum(top_entries, 0)
    top_cols = batched_far(
        top_coords,
        jnp.take(skel_top, top_chosen, axis=0),
        jnp.take(all_top, top_chosen, axis=0),
        top_entries >= 0,
    )
    local_top = lax.all_gather(top_cols, MEMBERS, axis=1, tiled=True)
    local_quad = middle_full(quad_stack, skel_quad, far_quad, quad_matrix, local_top, 4, device)
    local_pair = middle_full(pair_stack, skel_pair, far_pair, pair_matrix, local_quad, 2, device)
    leaf_entries = far_leaf[0]
    positions = jnp.clip(jnp.maximum(leaf_entries, 0) - device + REACH, 0, 2 * REACH)
    leaf_blocks = jnp.take(leaf_rim, positions, axis=0)
    local_leaf = batched_far(
        skel_leaf[0], leaf_blocks[:, rank:], leaf_blocks[:, :rank], leaf_entries >= 0
    ) + jnp.dot(transfer_leaf[0], local_pair, precision=HIGHEST)
    product = near_field + jnp.dot(leaf_basis[0], local_leaf, precision=HIGHEST)
    return product[None]


def solution(mesh):
    count = mesh.devices.size
    grid = Mesh(mesh.devices.reshape(count // 8, 2, 2, 2), AX)
    spread = P(AX, None, None)
    rows = P(AX, None)
    placed = (
        spread,
        spread,
        spread,
        spread,
        rows,
        rows,
        spread,
        P(),
        P(),
        P(),
        rows,
        rows,
        P(),
        P(),
        P(),
    )
    return jax.shard_map(per_device, mesh=grid, in_specs=placed, out_specs=spread, check_vma=False)
```

```python
import functools

import jax
import jax.numpy as jnp
from jax import lax
from jax.experimental import pallas as pl
from jax.experimental.pallas import tpu as pltpu
from jax.sharding import Mesh
from jax.sharding import PartitionSpec as P

REACH = 8
FAR_REACH = 4


INV_FOUR_PI = 0.07957747154594767
DELTA_SQ = 0.01
HIGHEST = lax.Precision.HIGHEST

AX = ("cl", "q", "p", "c")
MEMBERS = ("q", "p", "c")


def from_partner(value, axis, bit):
    mask = 2**bit
    pairs = [(source, source ^ mask) for source in range(lax.axis_size(axis))]
    return lax.ppermute(value, axis, pairs)


def from_behind(block, axis, distance):
    devices = range(lax.axis_size(axis))
    route = [(i - distance, i) for i in devices if i - distance in devices]
    return lax.ppermute(block, axis, route)


def kernel_block(left_pts, right_pts):
    distance = jnp.zeros((left_pts.shape[1], right_pts.shape[1]), jnp.float32)
    for axis_id in range(3):
        offset_gap = left_pts[axis_id][:, None] - right_pts[axis_id][None, :]
        distance = distance + offset_gap * offset_gap
    return INV_FOUR_PI * lax.rsqrt(distance + DELTA_SQ)


def transposed_dot(matrix, values):
    return lax.dot_general(matrix, values, (((0,), (0,)), ((), ())), precision=HIGHEST)


def listed_sum(own_coords, entries, fetcher, width):

    def advance(running, partner):
        coords, values = fetcher(jnp.maximum(partner, 0))
        contrib = jnp.dot(kernel_block(own_coords, coords), values, precision=HIGHEST)
        return (running + jnp.where(partner >= 0, contrib, 0.0), None)

    start_value = jnp.zeros((own_coords.shape[1], width), jnp.float32)
    result, _ = lax.scan(advance, start_value, entries)
    return result


def batched_far(own_coords, coords, values, valid):
    count, _, span = coords.shape
    right = jnp.transpose(coords, (1, 0, 2)).reshape(3, count * span)
    masked = jnp.where(valid[:, None, None], values, 0.0)
    flat = masked.reshape(count * span, values.shape[2])
    return jnp.dot(kernel_block(own_coords, right), flat, precision=lax.Precision.HIGH)


def pair_total(partial_value, levels):
    for bit_index in range(levels):
        partial_value = partial_value + from_partner(partial_value, AX, bit_index)
    return partial_value


def join_rows(block, levels, device):
    for bit_index in range(levels):
        other = from_partner(block, AX, bit_index)
        upper = device // 2**bit_index % 2
        block = jnp.where(
            upper == 0, jnp.concatenate([block, other], 0), jnp.concatenate([other, block], 0)
        )
    return block


def window(shipped):
    gathered = []
    for distance in range(-REACH, REACH + 1):
        if distance == 0:
            gathered.append(shipped)
        else:
            gathered.append(from_behind(shipped, AX, -distance))
    return jnp.stack(gathered)


def partner_stack(coefs, stride):
    gathered = []
    for offset in list(range(-FAR_REACH, 0)) + list(range(1, FAR_REACH + 1)):
        gathered.append(from_behind(coefs, AX, -offset * stride))
    stacked = jnp.stack(gathered)

    def slot_of(distance):
        return distance + FAR_REACH - (distance > 0).astype(jnp.int32)

    return (stacked, slot_of)


def middle_level(coefs, skeletons, lists, transfer_rows, above, stride, device):
    rank_rows = coefs.shape[0] // stride
    cluster = device // stride
    member = device % stride
    own_full = lax.dynamic_index_in_dim(skeletons, cluster, 0, keepdims=False)
    own_coords = lax.dynamic_slice_in_dim(own_full, member * rank_rows, rank_rows, 1)
    stacked, slot_of = partner_stack(coefs, stride)
    entries = lax.dynamic_index_in_dim(lists, cluster, 0, keepdims=False)
    chosen = jnp.maximum(entries, 0)
    coords = jnp.take(skeletons, chosen, axis=0)
    slots = jnp.clip(slot_of(chosen - cluster), 0, stacked.shape[0] - 1)
    values = jnp.take(stacked, slots, axis=0)
    rows_here = batched_far(own_coords, coords, values, entries >= 0) + jnp.dot(
        transfer_rows, above, precision=HIGHEST
    )
    return join_rows(rows_here, stride.bit_length() - 1, device)


def cluster_gather(block, device, clusters):
    gathered = block[None]
    for level in range(clusters.bit_length() - 1):
        bit_index = 3 + level
        other = from_partner(gathered, AX, bit_index)
        upper = device // 2**bit_index % 2
        gathered = jnp.where(
            upper == 0,
            jnp.concatenate([gathered, other], 0),
            jnp.concatenate([other, gathered], 0),
        )
    return gathered


def near_sum(own_points, near_entries, shipped, device):
    leaf_points = own_points.shape[1]
    point_rows = leaf_points + 3 * leaf_points // shipped.shape[1]

    def contribution(block, distance):
        listed = jnp.any(near_entries == device + distance)
        coords = block[leaf_points:point_rows].reshape(3, leaf_points)
        contrib = jnp.dot(
            kernel_block(own_points, coords), block[:leaf_points], precision=lax.Precision.HIGH
        )
        return jnp.where(listed, contrib, 0.0)

    total = contribution(shipped, 0)
    ahead = shipped
    behind = shipped
    rim = [None] * (2 * REACH + 1)
    rim[REACH] = shipped[point_rows:]
    for step in range(1, REACH + 1):
        ahead = from_behind(ahead, AX, 1)
        behind = from_behind(behind, AX, -1)
        rim[REACH - step] = ahead[point_rows:]
        rim[REACH + step] = behind[point_rows:]
        total = total + contribution(ahead, -step) + contribution(behind, step)
    return total, jnp.stack(rim)


def slot_of(distance):
    return distance + FAR_REACH - (distance > 0).astype(jnp.int32)


def middle_full(stacked, skeletons, lists, transfer, above, stride, device):
    cluster = device // stride
    own_coords = lax.dynamic_index_in_dim(skeletons, cluster, 0, keepdims=False)
    entries = lax.dynamic_index_in_dim(lists, cluster, 0, keepdims=False)
    chosen = jnp.maximum(entries, 0)
    coords = jnp.take(skeletons, chosen, axis=0)
    slots = jnp.clip(slot_of(chosen - cluster), 0, stacked.shape[0] - 1)
    values = jnp.take(stacked, slots, axis=0)
    return batched_far(own_coords, coords, values, entries >= 0) + jnp.dot(
        transfer, above, precision=HIGHEST
    )


OFFSETS = tuple(range(-FAR_REACH, 0)) + tuple(range(1, FAR_REACH + 1))


def device_coords(linear):
    return (linear // 8, linear // 4 % 2, linear // 2 % 2, linear % 2)


def exchange_kernel(
    clusters,
    top_ref,
    pair_ref,
    quad_ref,
    top_out,
    pair_out,
    quad_out,
    top_land,
    pair_land,
    quad_land,
    top_send,
    top_recv,
    pair_send,
    pair_recv,
    quad_send,
    quad_recv,
):
    me = lax.axis_index("cl")
    dev = lax.axis_index(AX)
    count = clusters * 8
    mesh_id = pl.DeviceIdType.MESH
    pair_land[...] = jnp.zeros(pair_land.shape, jnp.float32)
    quad_land[...] = jnp.zeros(quad_land.shape, jnp.float32)
    barrier = pltpu.get_barrier_semaphore()
    extra = (-12, -6, -4, -2, 2, 4, 6, 12)

    def inside(delta):
        return jnp.logical_and(dev + delta >= 0, dev + delta < count)

    def greet(step, carry):
        peer = lax.rem(me + step, clusters)
        pl.semaphore_signal(barrier, inc=1, device_id={"cl": peer}, device_id_type=mesh_id)
        return carry

    lax.fori_loop(1, clusters, greet, 0)
    for delta in extra:
        pl.semaphore_signal(
            barrier,
            inc=1,
            device_id=device_coords(lax.rem(dev + delta + count, count)),
            device_id_type=mesh_id,
        )
    pl.semaphore_wait(barrier, clusters - 1 + len(extra))

    def outgoing(step):
        peer = lax.rem(me + step, clusters)
        return pltpu.make_async_remote_copy(
            src_ref=top_ref,
            dst_ref=top_land.at[me],
            send_sem=top_send.at[step],
            recv_sem=top_recv.at[me],
            device_id={"cl": peer},
            device_id_type=mesh_id,
        )

    def incoming(step):
        source = lax.rem(me - step + clusters, clusters)
        return pltpu.make_async_remote_copy(
            src_ref=top_ref,
            dst_ref=top_land.at[source],
            send_sem=top_send.at[step],
            recv_sem=top_recv.at[source],
            device_id={"cl": source},
            device_id_type=mesh_id,
        )

    def partner_copy(src, land, send_sem, recv_sem, slot, target):
        return pltpu.make_async_remote_copy(
            src_ref=src,
            dst_ref=land.at[slot],
            send_sem=send_sem.at[slot],
            recv_sem=recv_sem.at[slot],
            device_id=device_coords(target),
            device_id_type=mesh_id,
        )

    partners = (
        (pair_ref, pair_land, pair_send, pair_recv, 2),
        (quad_ref, quad_land, quad_send, quad_recv, 4),
    )
    for src, land, send_sem, recv_sem, stride in partners:
        for slot, offset in enumerate(OFFSETS):

            @pl.when(inside(-offset * stride))
            def _():
                partner_copy(src, land, send_sem, recv_sem, slot, dev - offset * stride).start()

    def send(step, carry):
        outgoing(step).start()
        return carry

    lax.fori_loop(1, clusters, send, 0)
    top_land[me] = top_ref[...]

    def finish(step, carry):
        outgoing(step).wait_send()
        incoming(step).wait_recv()
        return carry

    lax.fori_loop(1, clusters, finish, 0)
    for src, land, send_sem, recv_sem, stride in partners:
        for slot, offset in enumerate(OFFSETS):

            @pl.when(inside(-offset * stride))
            def _():
                partner_copy(src, land, send_sem, recv_sem, slot, dev - offset * stride).wait_send()

            @pl.when(inside(offset * stride))
            def _():
                partner_copy(src, land, send_sem, recv_sem, slot, dev + offset * stride).wait_recv()

    top_out[...] = top_land[...]
    pair_out[...] = pair_land[...]
    quad_out[...] = quad_land[...]


def exchange(top_block, coef_pair, coef_quad):
    clusters = lax.axis_size("cl")
    rows, cols = top_block.shape
    stack = (len(OFFSETS),) + coef_pair.shape
    vmem = pl.BlockSpec(memory_space=pltpu.VMEM)
    return pl.pallas_call(
        functools.partial(exchange_kernel, clusters),
        out_shape=(
            jax.ShapeDtypeStruct((clusters, rows, cols), jnp.float32),
            jax.ShapeDtypeStruct(stack, jnp.float32),
            jax.ShapeDtypeStruct(stack, jnp.float32),
        ),
        in_specs=[vmem] * 3,
        out_specs=(vmem, vmem, vmem),
        scratch_shapes=[
            pltpu.VMEM((clusters, rows, cols), jnp.float32),
            pltpu.VMEM(stack, jnp.float32),
            pltpu.VMEM(stack, jnp.float32),
            pltpu.SemaphoreType.DMA((clusters,)),
            pltpu.SemaphoreType.DMA((clusters,)),
            pltpu.SemaphoreType.DMA((len(OFFSETS),)),
            pltpu.SemaphoreType.DMA((len(OFFSETS),)),
            pltpu.SemaphoreType.DMA((len(OFFSETS),)),
            pltpu.SemaphoreType.DMA((len(OFFSETS),)),
        ],
        compiler_params=pltpu.CompilerParams(collective_id=0, has_side_effects=True),
    )(top_block, coef_pair, coef_quad)


def per_device(
    vectors,
    points,
    leaf_basis,
    transfer_leaf,
    transfer_pair,
    transfer_quad,
    skel_leaf,
    skel_pair,
    skel_quad,
    skel_top,
    near_list,
    far_leaf,
    far_pair,
    far_quad,
    far_top,
):
    leaf_points = vectors.shape[1]
    width = vectors.shape[2]
    rank = leaf_basis.shape[2]
    device = lax.axis_index(AX)
    own_points = points[0]
    coef_leaf = transposed_dot(leaf_basis[0], vectors[0])
    pair_matrix = join_rows(transfer_pair, 1, device)
    quad_matrix = join_rows(transfer_quad, 2, device)
    up_pair = transposed_dot(transfer_leaf[0], coef_leaf)
    up_quad = transposed_dot(pair_matrix, up_pair)
    up_top = transposed_dot(quad_matrix, up_quad)
    first = jnp.stack([up_pair, up_quad, up_top])
    first = first + from_partner(first, AX, 0)
    coef_pair = first[0]
    second = first[1:] + from_partner(first[1:], AX, 1)
    coef_quad = second[0]
    coef_top = second[1] + from_partner(second[1], AX, 2)
    shipped = jnp.concatenate(
        [vectors[0], own_points.reshape(3 * leaf_points // width, width), coef_leaf, skel_leaf[0]],
        axis=0,
    )
    near_field, leaf_rim = near_sum(own_points, near_list[0], shipped, device)
    top_cluster = device // 8
    top_member = device % 8
    share = width // 8
    top_cols_own = lax.dynamic_slice_in_dim(coef_top.T, top_member * share, share, 0)
    top_cols_own, near_field = lax.optimization_barrier((top_cols_own, near_field))
    top_t, pair_stack, quad_stack = exchange(top_cols_own, coef_pair, coef_quad)
    all_top = jnp.swapaxes(top_t, 1, 2)
    top_coords = lax.dynamic_index_in_dim(skel_top, top_cluster, 0, keepdims=False)
    top_entries = lax.dynamic_index_in_dim(far_top, top_cluster, 0, keepdims=False)
    top_chosen = jnp.maximum(top_entries, 0)
    top_cols = batched_far(
        top_coords,
        jnp.take(skel_top, top_chosen, axis=0),
        jnp.take(all_top, top_chosen, axis=0),
        top_entries >= 0,
    )
    local_top = lax.all_gather(top_cols, MEMBERS, axis=1, tiled=True)
    local_quad = middle_full(quad_stack, skel_quad, far_quad, quad_matrix, local_top, 4, device)
    local_pair = middle_full(pair_stack, skel_pair, far_pair, pair_matrix, local_quad, 2, device)
    leaf_entries = far_leaf[0]
    positions = jnp.clip(jnp.maximum(leaf_entries, 0) - device + REACH, 0, 2 * REACH)
    leaf_blocks = jnp.take(leaf_rim, positions, axis=0)
    local_leaf = batched_far(
        skel_leaf[0], leaf_blocks[:, rank:], leaf_blocks[:, :rank], leaf_entries >= 0
    ) + jnp.dot(transfer_leaf[0], local_pair, precision=HIGHEST)
    product = near_field + jnp.dot(leaf_basis[0], local_leaf, precision=lax.Precision.HIGH)
    return product[None]


def solution(mesh):
    count = mesh.devices.size
    grid = Mesh(mesh.devices.reshape(count // 8, 2, 2, 2), AX)
    spread = P(AX, None, None)
    rows = P(AX, None)
    placed = (
        spread,
        spread,
        spread,
        spread,
        rows,
        rows,
        spread,
        P(),
        P(),
        P(),
        rows,
        rows,
        P(),
        P(),
        P(),
    )
    return jax.shard_map(per_device, mesh=grid, in_specs=placed, out_specs=spread, check_vma=False)
```

```python
import functools

import jax
import jax.numpy as jnp
from jax import lax
from jax.experimental import pallas as pl
from jax.experimental.pallas import tpu as pltpu
from jax.sharding import Mesh
from jax.sharding import PartitionSpec as P

REACH = 8
FAR_REACH = 4


INV_FOUR_PI = 0.07957747154594767
DELTA_SQ = 0.01
HIGHEST = lax.Precision.HIGHEST

AX = ("cl", "q", "p", "c")
MEMBERS = ("q", "p", "c")


def from_partner(value, axis, bit):
    mask = 2**bit
    pairs = [(source, source ^ mask) for source in range(lax.axis_size(axis))]
    return lax.ppermute(value, axis, pairs)


def from_behind(block, axis, distance):
    devices = range(lax.axis_size(axis))
    route = [(i - distance, i) for i in devices if i - distance in devices]
    return lax.ppermute(block, axis, route)


def kernel_block(left_pts, right_pts):
    distance = jnp.zeros((left_pts.shape[1], right_pts.shape[1]), jnp.float32)
    for axis_id in range(3):
        offset_gap = left_pts[axis_id][:, None] - right_pts[axis_id][None, :]
        distance = distance + offset_gap * offset_gap
    return INV_FOUR_PI * lax.rsqrt(distance + DELTA_SQ)


def transposed_dot(matrix, values):
    return lax.dot_general(matrix, values, (((0,), (0,)), ((), ())), precision=HIGHEST)


def listed_sum(own_coords, entries, fetcher, width):

    def advance(running, partner):
        coords, values = fetcher(jnp.maximum(partner, 0))
        contrib = jnp.dot(kernel_block(own_coords, coords), values, precision=HIGHEST)
        return (running + jnp.where(partner >= 0, contrib, 0.0), None)

    start_value = jnp.zeros((own_coords.shape[1], width), jnp.float32)
    result, _ = lax.scan(advance, start_value, entries)
    return result


def batched_far(own_coords, coords, values, valid):
    count, _, span = coords.shape
    right = jnp.transpose(coords, (1, 0, 2)).reshape(3, count * span)
    masked = jnp.where(valid[:, None, None], values, 0.0)
    flat = masked.reshape(count * span, values.shape[2])
    return jnp.dot(kernel_block(own_coords, right), flat, precision=lax.Precision.HIGH)


def pair_total(partial_value, levels):
    for bit_index in range(levels):
        partial_value = partial_value + from_partner(partial_value, AX, bit_index)
    return partial_value


def join_rows(block, levels, device):
    for bit_index in range(levels):
        other = from_partner(block, AX, bit_index)
        upper = device // 2**bit_index % 2
        block = jnp.where(
            upper == 0, jnp.concatenate([block, other], 0), jnp.concatenate([other, block], 0)
        )
    return block


def window(shipped):
    gathered = []
    for distance in range(-REACH, REACH + 1):
        if distance == 0:
            gathered.append(shipped)
        else:
            gathered.append(from_behind(shipped, AX, -distance))
    return jnp.stack(gathered)


def partner_stack(coefs, stride):
    gathered = []
    for offset in list(range(-FAR_REACH, 0)) + list(range(1, FAR_REACH + 1)):
        gathered.append(from_behind(coefs, AX, -offset * stride))
    stacked = jnp.stack(gathered)

    def slot_of(distance):
        return distance + FAR_REACH - (distance > 0).astype(jnp.int32)

    return (stacked, slot_of)


def middle_level(coefs, skeletons, lists, transfer_rows, above, stride, device):
    rank_rows = coefs.shape[0] // stride
    cluster = device // stride
    member = device % stride
    own_full = lax.dynamic_index_in_dim(skeletons, cluster, 0, keepdims=False)
    own_coords = lax.dynamic_slice_in_dim(own_full, member * rank_rows, rank_rows, 1)
    stacked, slot_of = partner_stack(coefs, stride)
    entries = lax.dynamic_index_in_dim(lists, cluster, 0, keepdims=False)
    chosen = jnp.maximum(entries, 0)
    coords = jnp.take(skeletons, chosen, axis=0)
    slots = jnp.clip(slot_of(chosen - cluster), 0, stacked.shape[0] - 1)
    values = jnp.take(stacked, slots, axis=0)
    rows_here = batched_far(own_coords, coords, values, entries >= 0) + jnp.dot(
        transfer_rows, above, precision=HIGHEST
    )
    return join_rows(rows_here, stride.bit_length() - 1, device)


def cluster_gather(block, device, clusters):
    gathered = block[None]
    for level in range(clusters.bit_length() - 1):
        bit_index = 3 + level
        other = from_partner(gathered, AX, bit_index)
        upper = device // 2**bit_index % 2
        gathered = jnp.where(
            upper == 0,
            jnp.concatenate([gathered, other], 0),
            jnp.concatenate([other, gathered], 0),
        )
    return gathered


def near_sum(own_points, near_entries, shipped, device):
    leaf_points = own_points.shape[1]
    point_rows = leaf_points + 3 * leaf_points // shipped.shape[1]

    def contribution(block, distance):
        listed = jnp.any(near_entries == device + distance)
        coords = block[leaf_points:point_rows].reshape(3, leaf_points)
        contrib = jnp.dot(
            kernel_block(own_points, coords), block[:leaf_points], precision=lax.Precision.HIGH
        )
        return jnp.where(listed, contrib, 0.0)

    total = contribution(shipped, 0)
    ahead = shipped
    behind = shipped
    rim = [None] * (2 * REACH + 1)
    rim[REACH] = shipped[point_rows:]
    for step in range(1, REACH + 1):
        ahead = from_behind(ahead, AX, 1)
        behind = from_behind(behind, AX, -1)
        rim[REACH - step] = ahead[point_rows:]
        rim[REACH + step] = behind[point_rows:]
        total = total + contribution(ahead, -step) + contribution(behind, step)
    return total, jnp.stack(rim)


def slot_of(distance):
    return distance + FAR_REACH - (distance > 0).astype(jnp.int32)


def middle_full(stacked, skeletons, lists, transfer, above, stride, device):
    cluster = device // stride
    own_coords = lax.dynamic_index_in_dim(skeletons, cluster, 0, keepdims=False)
    entries = lax.dynamic_index_in_dim(lists, cluster, 0, keepdims=False)
    chosen = jnp.maximum(entries, 0)
    coords = jnp.take(skeletons, chosen, axis=0)
    slots = jnp.clip(slot_of(chosen - cluster), 0, stacked.shape[0] - 1)
    values = jnp.take(stacked, slots, axis=0)
    return batched_far(own_coords, coords, values, entries >= 0) + jnp.dot(
        transfer, above, precision=lax.Precision.HIGH
    )


OFFSETS = tuple(range(-FAR_REACH, 0)) + tuple(range(1, FAR_REACH + 1))


def device_coords(linear):
    return (linear // 8, linear // 4 % 2, linear // 2 % 2, linear % 2)


def exchange_kernel(
    clusters,
    top_ref,
    pair_ref,
    quad_ref,
    top_out,
    pair_out,
    quad_out,
    top_land,
    pair_land,
    quad_land,
    top_send,
    top_recv,
    pair_send,
    pair_recv,
    quad_send,
    quad_recv,
):
    me = lax.axis_index("cl")
    dev = lax.axis_index(AX)
    count = clusters * 8
    mesh_id = pl.DeviceIdType.MESH
    pair_land[...] = jnp.zeros(pair_land.shape, jnp.float32)
    quad_land[...] = jnp.zeros(quad_land.shape, jnp.float32)
    barrier = pltpu.get_barrier_semaphore()
    extra = (-12, -6, -4, -2, 2, 4, 6, 12)

    def inside(delta):
        return jnp.logical_and(dev + delta >= 0, dev + delta < count)

    def greet(step, carry):
        peer = lax.rem(me + step, clusters)
        pl.semaphore_signal(barrier, inc=1, device_id={"cl": peer}, device_id_type=mesh_id)
        return carry

    lax.fori_loop(1, clusters, greet, 0)
    for delta in extra:
        pl.semaphore_signal(
            barrier,
            inc=1,
            device_id=device_coords(lax.rem(dev + delta + count, count)),
            device_id_type=mesh_id,
        )
    pl.semaphore_wait(barrier, clusters - 1 + len(extra))

    def outgoing(step):
        peer = lax.rem(me + step, clusters)
        return pltpu.make_async_remote_copy(
            src_ref=top_ref,
            dst_ref=top_land.at[me],
            send_sem=top_send.at[step],
            recv_sem=top_recv.at[me],
            device_id={"cl": peer},
            device_id_type=mesh_id,
        )

    def incoming(step):
        source = lax.rem(me - step + clusters, clusters)
        return pltpu.make_async_remote_copy(
            src_ref=top_ref,
            dst_ref=top_land.at[source],
            send_sem=top_send.at[step],
            recv_sem=top_recv.at[source],
            device_id={"cl": source},
            device_id_type=mesh_id,
        )

    def partner_copy(src, land, send_sem, recv_sem, slot, target):
        return pltpu.make_async_remote_copy(
            src_ref=src,
            dst_ref=land.at[slot],
            send_sem=send_sem.at[slot],
            recv_sem=recv_sem.at[slot],
            device_id=device_coords(target),
            device_id_type=mesh_id,
        )

    partners = (
        (pair_ref, pair_land, pair_send, pair_recv, 2),
        (quad_ref, quad_land, quad_send, quad_recv, 4),
    )
    for src, land, send_sem, recv_sem, stride in partners:
        for slot, offset in enumerate(OFFSETS):

            @pl.when(inside(-offset * stride))
            def _():
                partner_copy(src, land, send_sem, recv_sem, slot, dev - offset * stride).start()

    def send(step, carry):
        outgoing(step).start()
        return carry

    lax.fori_loop(1, clusters, send, 0)
    top_land[me] = top_ref[...]

    def finish(step, carry):
        outgoing(step).wait_send()
        incoming(step).wait_recv()
        return carry

    lax.fori_loop(1, clusters, finish, 0)
    for src, land, send_sem, recv_sem, stride in partners:
        for slot, offset in enumerate(OFFSETS):

            @pl.when(inside(-offset * stride))
            def _():
                partner_copy(src, land, send_sem, recv_sem, slot, dev - offset * stride).wait_send()

            @pl.when(inside(offset * stride))
            def _():
                partner_copy(src, land, send_sem, recv_sem, slot, dev + offset * stride).wait_recv()

    top_out[...] = top_land[...]
    pair_out[...] = pair_land[...]
    quad_out[...] = quad_land[...]


def exchange(top_block, coef_pair, coef_quad):
    clusters = lax.axis_size("cl")
    rows, cols = top_block.shape
    stack = (len(OFFSETS),) + coef_pair.shape
    vmem = pl.BlockSpec(memory_space=pltpu.VMEM)
    return pl.pallas_call(
        functools.partial(exchange_kernel, clusters),
        out_shape=(
            jax.ShapeDtypeStruct((clusters, rows, cols), jnp.float32),
            jax.ShapeDtypeStruct(stack, jnp.float32),
            jax.ShapeDtypeStruct(stack, jnp.float32),
        ),
        in_specs=[vmem] * 3,
        out_specs=(vmem, vmem, vmem),
        scratch_shapes=[
            pltpu.VMEM((clusters, rows, cols), jnp.float32),
            pltpu.VMEM(stack, jnp.float32),
            pltpu.VMEM(stack, jnp.float32),
            pltpu.SemaphoreType.DMA((clusters,)),
            pltpu.SemaphoreType.DMA((clusters,)),
            pltpu.SemaphoreType.DMA((len(OFFSETS),)),
            pltpu.SemaphoreType.DMA((len(OFFSETS),)),
            pltpu.SemaphoreType.DMA((len(OFFSETS),)),
            pltpu.SemaphoreType.DMA((len(OFFSETS),)),
        ],
        compiler_params=pltpu.CompilerParams(collective_id=0, has_side_effects=True),
    )(top_block, coef_pair, coef_quad)


def per_device(
    vectors,
    points,
    leaf_basis,
    transfer_leaf,
    transfer_pair,
    transfer_quad,
    skel_leaf,
    skel_pair,
    skel_quad,
    skel_top,
    near_list,
    far_leaf,
    far_pair,
    far_quad,
    far_top,
):
    leaf_points = vectors.shape[1]
    width = vectors.shape[2]
    rank = leaf_basis.shape[2]
    device = lax.axis_index(AX)
    own_points = points[0]
    coef_leaf = transposed_dot(leaf_basis[0], vectors[0])
    pair_matrix = join_rows(transfer_pair, 1, device)
    quad_matrix = join_rows(transfer_quad, 2, device)
    up_pair = transposed_dot(transfer_leaf[0], coef_leaf)
    up_quad = transposed_dot(pair_matrix, up_pair)
    up_top = transposed_dot(quad_matrix, up_quad)
    first = jnp.stack([up_pair, up_quad, up_top])
    first = first + from_partner(first, AX, 0)
    coef_pair = first[0]
    second = first[1:] + from_partner(first[1:], AX, 1)
    coef_quad = second[0]
    coef_top = second[1] + from_partner(second[1], AX, 2)
    shipped = jnp.concatenate(
        [vectors[0], own_points.reshape(3 * leaf_points // width, width), coef_leaf, skel_leaf[0]],
        axis=0,
    )
    near_field, leaf_rim = near_sum(own_points, near_list[0], shipped, device)
    top_cluster = device // 8
    top_member = device % 8
    share = width // 8
    top_cols_own = lax.dynamic_slice_in_dim(coef_top.T, top_member * share, share, 0)
    top_cols_own, near_field = lax.optimization_barrier((top_cols_own, near_field))
    top_t, pair_stack, quad_stack = exchange(top_cols_own, coef_pair, coef_quad)
    all_top = jnp.swapaxes(top_t, 1, 2)
    top_coords = lax.dynamic_index_in_dim(skel_top, top_cluster, 0, keepdims=False)
    top_entries = lax.dynamic_index_in_dim(far_top, top_cluster, 0, keepdims=False)
    top_chosen = jnp.maximum(top_entries, 0)
    top_cols = batched_far(
        top_coords,
        jnp.take(skel_top, top_chosen, axis=0),
        jnp.take(all_top, top_chosen, axis=0),
        top_entries >= 0,
    )
    local_top = lax.all_gather(top_cols, MEMBERS, axis=1, tiled=True)
    local_quad = middle_full(quad_stack, skel_quad, far_quad, quad_matrix, local_top, 4, device)
    local_pair = middle_full(pair_stack, skel_pair, far_pair, pair_matrix, local_quad, 2, device)
    leaf_entries = far_leaf[0]
    positions = jnp.clip(jnp.maximum(leaf_entries, 0) - device + REACH, 0, 2 * REACH)
    leaf_blocks = jnp.take(leaf_rim, positions, axis=0)
    local_leaf = batched_far(
        skel_leaf[0], leaf_blocks[:, rank:], leaf_blocks[:, :rank], leaf_entries >= 0
    ) + jnp.dot(transfer_leaf[0], local_pair, precision=lax.Precision.HIGH)
    product = near_field + jnp.dot(leaf_basis[0], local_leaf, precision=lax.Precision.HIGH)
    return product[None]


def solution(mesh):
    count = mesh.devices.size
    grid = Mesh(mesh.devices.reshape(count // 8, 2, 2, 2), AX)
    spread = P(AX, None, None)
    rows = P(AX, None)
    placed = (
        spread,
        spread,
        spread,
        spread,
        rows,
        rows,
        spread,
        P(),
        P(),
        P(),
        rows,
        rows,
        P(),
        P(),
        P(),
    )
    return jax.shard_map(per_device, mesh=grid, in_specs=placed, out_specs=spread, check_vma=False)
```

```python
import functools

import jax
import jax.numpy as jnp
from jax import lax
from jax.experimental import pallas as pl
from jax.experimental.pallas import tpu as pltpu
from jax.sharding import Mesh
from jax.sharding import PartitionSpec as P

REACH = 8
FAR_REACH = 4


INV_FOUR_PI = 0.07957747154594767
DELTA_SQ = 0.01
HIGHEST = lax.Precision.HIGHEST

AX = ("cl", "q", "p", "c")
MEMBERS = ("q", "p", "c")


def from_partner(value, axis, bit):
    mask = 2**bit
    pairs = [(source, source ^ mask) for source in range(lax.axis_size(axis))]
    return lax.ppermute(value, axis, pairs)


def from_behind(block, axis, distance):
    devices = range(lax.axis_size(axis))
    route = [(i - distance, i) for i in devices if i - distance in devices]
    return lax.ppermute(block, axis, route)


def kernel_block(left_pts, right_pts):
    distance = jnp.zeros((left_pts.shape[1], right_pts.shape[1]), jnp.float32)
    for axis_id in range(3):
        offset_gap = left_pts[axis_id][:, None] - right_pts[axis_id][None, :]
        distance = distance + offset_gap * offset_gap
    return INV_FOUR_PI * lax.rsqrt(distance + DELTA_SQ)


def transposed_dot(matrix, values):
    return lax.dot_general(matrix, values, (((0,), (0,)), ((), ())), precision=HIGHEST)


def listed_sum(own_coords, entries, fetcher, width):

    def advance(running, partner):
        coords, values = fetcher(jnp.maximum(partner, 0))
        contrib = jnp.dot(kernel_block(own_coords, coords), values, precision=HIGHEST)
        return (running + jnp.where(partner >= 0, contrib, 0.0), None)

    start_value = jnp.zeros((own_coords.shape[1], width), jnp.float32)
    result, _ = lax.scan(advance, start_value, entries)
    return result


def batched_far(own_coords, coords, values, valid):
    count, _, span = coords.shape
    right = jnp.transpose(coords, (1, 0, 2)).reshape(3, count * span)
    masked = jnp.where(valid[:, None, None], values, 0.0)
    flat = masked.reshape(count * span, values.shape[2])
    return jnp.dot(kernel_block(own_coords, right), flat, precision=lax.Precision.HIGH)


def pair_total(partial_value, levels):
    for bit_index in range(levels):
        partial_value = partial_value + from_partner(partial_value, AX, bit_index)
    return partial_value


def join_rows(block, levels, device):
    for bit_index in range(levels):
        other = from_partner(block, AX, bit_index)
        upper = device // 2**bit_index % 2
        block = jnp.where(
            upper == 0, jnp.concatenate([block, other], 0), jnp.concatenate([other, block], 0)
        )
    return block


def window(shipped):
    gathered = []
    for distance in range(-REACH, REACH + 1):
        if distance == 0:
            gathered.append(shipped)
        else:
            gathered.append(from_behind(shipped, AX, -distance))
    return jnp.stack(gathered)


def partner_stack(coefs, stride):
    gathered = []
    for offset in list(range(-FAR_REACH, 0)) + list(range(1, FAR_REACH + 1)):
        gathered.append(from_behind(coefs, AX, -offset * stride))
    stacked = jnp.stack(gathered)

    def slot_of(distance):
        return distance + FAR_REACH - (distance > 0).astype(jnp.int32)

    return (stacked, slot_of)


def middle_level(coefs, skeletons, lists, transfer_rows, above, stride, device):
    rank_rows = coefs.shape[0] // stride
    cluster = device // stride
    member = device % stride
    own_full = lax.dynamic_index_in_dim(skeletons, cluster, 0, keepdims=False)
    own_coords = lax.dynamic_slice_in_dim(own_full, member * rank_rows, rank_rows, 1)
    stacked, slot_of = partner_stack(coefs, stride)
    entries = lax.dynamic_index_in_dim(lists, cluster, 0, keepdims=False)
    chosen = jnp.maximum(entries, 0)
    coords = jnp.take(skeletons, chosen, axis=0)
    slots = jnp.clip(slot_of(chosen - cluster), 0, stacked.shape[0] - 1)
    values = jnp.take(stacked, slots, axis=0)
    rows_here = batched_far(own_coords, coords, values, entries >= 0) + jnp.dot(
        transfer_rows, above, precision=HIGHEST
    )
    return join_rows(rows_here, stride.bit_length() - 1, device)


def cluster_gather(block, device, clusters):
    gathered = block[None]
    for level in range(clusters.bit_length() - 1):
        bit_index = 3 + level
        other = from_partner(gathered, AX, bit_index)
        upper = device // 2**bit_index % 2
        gathered = jnp.where(
            upper == 0,
            jnp.concatenate([gathered, other], 0),
            jnp.concatenate([other, gathered], 0),
        )
    return gathered


def near_sum(own_points, near_entries, shipped, device):
    leaf_points = own_points.shape[1]
    point_rows = leaf_points + 3 * leaf_points // shipped.shape[1]

    def contribution(block, distance):
        listed = jnp.any(near_entries == device + distance)
        coords = block[leaf_points:point_rows].reshape(3, leaf_points)
        contrib = jnp.dot(
            kernel_block(own_points, coords), block[:leaf_points], precision=lax.Precision.HIGH
        )
        return jnp.where(listed, contrib, 0.0)

    total = contribution(shipped, 0)
    ahead = shipped
    behind = shipped
    rim = [None] * (2 * REACH + 1)
    rim[REACH] = shipped[point_rows:]
    for step in range(1, REACH + 1):
        ahead = from_behind(ahead, AX, 1)
        behind = from_behind(behind, AX, -1)
        rim[REACH - step] = ahead[point_rows:]
        rim[REACH + step] = behind[point_rows:]
        total = total + contribution(ahead, -step) + contribution(behind, step)
    return total, jnp.stack(rim)


def slot_of(distance):
    return distance + FAR_REACH - (distance > 0).astype(jnp.int32)


def middle_full(stacked, skeletons, lists, transfer, above, stride, device):
    cluster = device // stride
    own_coords = lax.dynamic_index_in_dim(skeletons, cluster, 0, keepdims=False)
    entries = lax.dynamic_index_in_dim(lists, cluster, 0, keepdims=False)
    chosen = jnp.maximum(entries, 0)
    coords = jnp.take(skeletons, chosen, axis=0)
    slots = jnp.clip(slot_of(chosen - cluster), 0, stacked.shape[0] - 1)
    values = jnp.take(stacked, slots, axis=0)
    return batched_far(own_coords, coords, values, entries >= 0) + jnp.dot(
        transfer, above, precision=HIGHEST
    )


OFFSETS = tuple(range(-FAR_REACH, 0)) + tuple(range(1, FAR_REACH + 1))


def device_coords(linear):
    return (linear // 8, linear // 4 % 2, linear // 2 % 2, linear % 2)


def exchange_kernel(
    clusters,
    top_ref,
    pair_ref,
    quad_ref,
    top_out,
    pair_out,
    quad_out,
    top_land,
    pair_land,
    quad_land,
    top_send,
    top_recv,
    pair_send,
    pair_recv,
    quad_send,
    quad_recv,
):
    me = lax.axis_index("cl")
    dev = lax.axis_index(AX)
    count = clusters * 8
    mesh_id = pl.DeviceIdType.MESH
    pair_land[...] = jnp.zeros(pair_land.shape, jnp.float32)
    quad_land[...] = jnp.zeros(quad_land.shape, jnp.float32)
    barrier = pltpu.get_barrier_semaphore()
    extra = (-12, -6, -4, -2, 2, 4, 6, 12)

    def inside(delta):
        return jnp.logical_and(dev + delta >= 0, dev + delta < count)

    def greet(step, carry):
        peer = lax.rem(me + step, clusters)
        pl.semaphore_signal(barrier, inc=1, device_id={"cl": peer}, device_id_type=mesh_id)
        return carry

    lax.fori_loop(1, clusters, greet, 0)
    for delta in extra:
        pl.semaphore_signal(
            barrier,
            inc=1,
            device_id=device_coords(lax.rem(dev + delta + count, count)),
            device_id_type=mesh_id,
        )
    pl.semaphore_wait(barrier, clusters - 1 + len(extra))

    def outgoing(step):
        peer = lax.rem(me + step, clusters)
        return pltpu.make_async_remote_copy(
            src_ref=top_ref,
            dst_ref=top_land.at[me],
            send_sem=top_send.at[step],
            recv_sem=top_recv.at[me],
            device_id={"cl": peer},
            device_id_type=mesh_id,
        )

    def incoming(step):
        source = lax.rem(me - step + clusters, clusters)
        return pltpu.make_async_remote_copy(
            src_ref=top_ref,
            dst_ref=top_land.at[source],
            send_sem=top_send.at[step],
            recv_sem=top_recv.at[source],
            device_id={"cl": source},
            device_id_type=mesh_id,
        )

    def partner_copy(src, land, send_sem, recv_sem, slot, target):
        return pltpu.make_async_remote_copy(
            src_ref=src,
            dst_ref=land.at[slot],
            send_sem=send_sem.at[slot],
            recv_sem=recv_sem.at[slot],
            device_id=device_coords(target),
            device_id_type=mesh_id,
        )

    partners = (
        (pair_ref, pair_land, pair_send, pair_recv, 2),
        (quad_ref, quad_land, quad_send, quad_recv, 4),
    )
    for src, land, send_sem, recv_sem, stride in partners:
        for slot, offset in enumerate(OFFSETS):

            @pl.when(inside(-offset * stride))
            def _():
                partner_copy(src, land, send_sem, recv_sem, slot, dev - offset * stride).start()

    def send(step, carry):
        outgoing(step).start()
        return carry

    lax.fori_loop(1, clusters, send, 0)
    top_land[me] = top_ref[...]

    def finish(step, carry):
        outgoing(step).wait_send()
        incoming(step).wait_recv()
        return carry

    lax.fori_loop(1, clusters, finish, 0)
    for src, land, send_sem, recv_sem, stride in partners:
        for slot, offset in enumerate(OFFSETS):

            @pl.when(inside(-offset * stride))
            def _():
                partner_copy(src, land, send_sem, recv_sem, slot, dev - offset * stride).wait_send()

            @pl.when(inside(offset * stride))
            def _():
                partner_copy(src, land, send_sem, recv_sem, slot, dev + offset * stride).wait_recv()

    top_out[...] = top_land[...]
    pair_out[...] = pair_land[...]
    quad_out[...] = quad_land[...]


def mates_kernel(block_ref, out_ref, landing, send_sem, recv_sem):
    dev = lax.axis_index(AX)
    member = dev % 8
    base = dev - member
    mesh_id = pl.DeviceIdType.MESH
    barrier = pltpu.get_barrier_semaphore()
    for step in range(1, 8):
        pl.semaphore_signal(
            barrier,
            inc=1,
            device_id=device_coords(base + lax.rem(member + step, 8)),
            device_id_type=mesh_id,
        )
    pl.semaphore_wait(barrier, 7)

    def outgoing(step):
        return pltpu.make_async_remote_copy(
            src_ref=block_ref,
            dst_ref=landing.at[member],
            send_sem=send_sem.at[step],
            recv_sem=recv_sem.at[member],
            device_id=device_coords(base + lax.rem(member + step, 8)),
            device_id_type=mesh_id,
        )

    def incoming(step):
        source = lax.rem(member - step + 8, 8)
        return pltpu.make_async_remote_copy(
            src_ref=block_ref,
            dst_ref=landing.at[source],
            send_sem=send_sem.at[step],
            recv_sem=recv_sem.at[source],
            device_id=device_coords(base + source),
            device_id_type=mesh_id,
        )

    for step in range(1, 8):
        outgoing(step).start()
    own = pltpu.make_async_copy(block_ref, landing.at[member], send_sem.at[0])
    own.start()
    own.wait()
    for step in range(1, 8):
        outgoing(step).wait_send()
        incoming(step).wait_recv()
    out_ref[...] = landing[...]


def mates_gather(block):
    rows, cols = block.shape
    vmem = pl.BlockSpec(memory_space=pltpu.VMEM)
    return pl.pallas_call(
        mates_kernel,
        out_shape=jax.ShapeDtypeStruct((8, rows, cols), jnp.float32),
        in_specs=[vmem],
        out_specs=vmem,
        scratch_shapes=[
            pltpu.VMEM((8, rows, cols), jnp.float32),
            pltpu.SemaphoreType.DMA((8,)),
            pltpu.SemaphoreType.DMA((8,)),
        ],
        compiler_params=pltpu.CompilerParams(collective_id=1, has_side_effects=True),
    )(block)


def exchange(top_block, coef_pair, coef_quad):
    clusters = lax.axis_size("cl")
    rows, cols = top_block.shape
    stack = (len(OFFSETS),) + coef_pair.shape
    vmem = pl.BlockSpec(memory_space=pltpu.VMEM)
    return pl.pallas_call(
        functools.partial(exchange_kernel, clusters),
        out_shape=(
            jax.ShapeDtypeStruct((clusters, rows, cols), jnp.float32),
            jax.ShapeDtypeStruct(stack, jnp.float32),
            jax.ShapeDtypeStruct(stack, jnp.float32),
        ),
        in_specs=[vmem] * 3,
        out_specs=(vmem, vmem, vmem),
        scratch_shapes=[
            pltpu.VMEM((clusters, rows, cols), jnp.float32),
            pltpu.VMEM(stack, jnp.float32),
            pltpu.VMEM(stack, jnp.float32),
            pltpu.SemaphoreType.DMA((clusters,)),
            pltpu.SemaphoreType.DMA((clusters,)),
            pltpu.SemaphoreType.DMA((len(OFFSETS),)),
            pltpu.SemaphoreType.DMA((len(OFFSETS),)),
            pltpu.SemaphoreType.DMA((len(OFFSETS),)),
            pltpu.SemaphoreType.DMA((len(OFFSETS),)),
        ],
        compiler_params=pltpu.CompilerParams(collective_id=0, has_side_effects=True),
    )(top_block, coef_pair, coef_quad)


def per_device(
    vectors,
    points,
    leaf_basis,
    transfer_leaf,
    transfer_pair,
    transfer_quad,
    skel_leaf,
    skel_pair,
    skel_quad,
    skel_top,
    near_list,
    far_leaf,
    far_pair,
    far_quad,
    far_top,
):
    leaf_points = vectors.shape[1]
    width = vectors.shape[2]
    rank = leaf_basis.shape[2]
    device = lax.axis_index(AX)
    own_points = points[0]
    coef_leaf = transposed_dot(leaf_basis[0], vectors[0])
    pair_matrix = join_rows(transfer_pair, 1, device)
    quad_matrix = join_rows(transfer_quad, 2, device)
    up_pair = transposed_dot(transfer_leaf[0], coef_leaf)
    up_quad = transposed_dot(pair_matrix, up_pair)
    up_top = transposed_dot(quad_matrix, up_quad)
    first = jnp.stack([up_pair, up_quad, up_top])
    first = first + from_partner(first, AX, 0)
    coef_pair = first[0]
    second = first[1:] + from_partner(first[1:], AX, 1)
    coef_quad = second[0]
    coef_top = second[1] + from_partner(second[1], AX, 2)
    shipped = jnp.concatenate(
        [vectors[0], own_points.reshape(3 * leaf_points // width, width), coef_leaf, skel_leaf[0]],
        axis=0,
    )
    near_field, leaf_rim = near_sum(own_points, near_list[0], shipped, device)
    top_cluster = device // 8
    top_member = device % 8
    share = width // 8
    top_cols_own = lax.dynamic_slice_in_dim(coef_top.T, top_member * share, share, 0)
    top_cols_own, near_field = lax.optimization_barrier((top_cols_own, near_field))
    top_t, pair_stack, quad_stack = exchange(top_cols_own, coef_pair, coef_quad)
    all_top = jnp.swapaxes(top_t, 1, 2)
    top_coords = lax.dynamic_index_in_dim(skel_top, top_cluster, 0, keepdims=False)
    top_entries = lax.dynamic_index_in_dim(far_top, top_cluster, 0, keepdims=False)
    top_chosen = jnp.maximum(top_entries, 0)
    top_cols = batched_far(
        top_coords,
        jnp.take(skel_top, top_chosen, axis=0),
        jnp.take(all_top, top_chosen, axis=0),
        top_entries >= 0,
    )
    local_top = mates_gather(top_cols.T).reshape(rank, width).T
    local_quad = middle_full(quad_stack, skel_quad, far_quad, quad_matrix, local_top, 4, device)
    local_pair = middle_full(pair_stack, skel_pair, far_pair, pair_matrix, local_quad, 2, device)
    leaf_entries = far_leaf[0]
    positions = jnp.clip(jnp.maximum(leaf_entries, 0) - device + REACH, 0, 2 * REACH)
    leaf_blocks = jnp.take(leaf_rim, positions, axis=0)
    local_leaf = batched_far(
        skel_leaf[0], leaf_blocks[:, rank:], leaf_blocks[:, :rank], leaf_entries >= 0
    ) + jnp.dot(transfer_leaf[0], local_pair, precision=HIGHEST)
    product = near_field + jnp.dot(leaf_basis[0], local_leaf, precision=lax.Precision.HIGH)
    return product[None]


def solution(mesh):
    count = mesh.devices.size
    grid = Mesh(mesh.devices.reshape(count // 8, 2, 2, 2), AX)
    spread = P(AX, None, None)
    rows = P(AX, None)
    placed = (
        spread,
        spread,
        spread,
        spread,
        rows,
        rows,
        spread,
        P(),
        P(),
        P(),
        rows,
        rows,
        P(),
        P(),
        P(),
    )
    return jax.shard_map(per_device, mesh=grid, in_specs=placed, out_specs=spread, check_vma=False)
```

```python
import functools

import jax
import jax.numpy as jnp
from jax import lax
from jax.experimental import pallas as pl
from jax.experimental.pallas import tpu as pltpu
from jax.sharding import Mesh
from jax.sharding import PartitionSpec as P

REACH = 8
FAR_REACH = 4


INV_FOUR_PI = 0.07957747154594767
DELTA_SQ = 0.01
HIGHEST = lax.Precision.HIGHEST

AX = ("cl", "q", "p", "c")
MEMBERS = ("q", "p", "c")


def from_partner(value, axis, bit):
    mask = 2**bit
    pairs = [(source, source ^ mask) for source in range(lax.axis_size(axis))]
    return lax.ppermute(value, axis, pairs)


def from_behind(block, axis, distance):
    devices = range(lax.axis_size(axis))
    route = [(i - distance, i) for i in devices if i - distance in devices]
    return lax.ppermute(block, axis, route)


def kernel_block(left_pts, right_pts):
    distance = jnp.zeros((left_pts.shape[1], right_pts.shape[1]), jnp.float32)
    for axis_id in range(3):
        offset_gap = left_pts[axis_id][:, None] - right_pts[axis_id][None, :]
        distance = distance + offset_gap * offset_gap
    return INV_FOUR_PI * lax.rsqrt(distance + DELTA_SQ)


def transposed_dot(matrix, values):
    return lax.dot_general(
        matrix, values, (((0,), (0,)), ((), ())), precision=lax.Precision.HIGH
    )


def listed_sum(own_coords, entries, fetcher, width):

    def advance(running, partner):
        coords, values = fetcher(jnp.maximum(partner, 0))
        contrib = jnp.dot(kernel_block(own_coords, coords), values, precision=HIGHEST)
        return (running + jnp.where(partner >= 0, contrib, 0.0), None)

    start_value = jnp.zeros((own_coords.shape[1], width), jnp.float32)
    result, _ = lax.scan(advance, start_value, entries)
    return result


def batched_far(own_coords, coords, values, valid):
    count, _, span = coords.shape
    right = jnp.transpose(coords, (1, 0, 2)).reshape(3, count * span)
    masked = jnp.where(valid[:, None, None], values, 0.0)
    flat = masked.reshape(count * span, values.shape[2])
    return jnp.dot(kernel_block(own_coords, right), flat, precision=lax.Precision.HIGH)


def pair_total(partial_value, levels):
    for bit_index in range(levels):
        partial_value = partial_value + from_partner(partial_value, AX, bit_index)
    return partial_value


def join_rows(block, levels, device):
    for bit_index in range(levels):
        other = from_partner(block, AX, bit_index)
        upper = device // 2**bit_index % 2
        block = jnp.where(
            upper == 0, jnp.concatenate([block, other], 0), jnp.concatenate([other, block], 0)
        )
    return block


def window(shipped):
    gathered = []
    for distance in range(-REACH, REACH + 1):
        if distance == 0:
            gathered.append(shipped)
        else:
            gathered.append(from_behind(shipped, AX, -distance))
    return jnp.stack(gathered)


def partner_stack(coefs, stride):
    gathered = []
    for offset in list(range(-FAR_REACH, 0)) + list(range(1, FAR_REACH + 1)):
        gathered.append(from_behind(coefs, AX, -offset * stride))
    stacked = jnp.stack(gathered)

    def slot_of(distance):
        return distance + FAR_REACH - (distance > 0).astype(jnp.int32)

    return (stacked, slot_of)


def middle_level(coefs, skeletons, lists, transfer_rows, above, stride, device):
    rank_rows = coefs.shape[0] // stride
    cluster = device // stride
    member = device % stride
    own_full = lax.dynamic_index_in_dim(skeletons, cluster, 0, keepdims=False)
    own_coords = lax.dynamic_slice_in_dim(own_full, member * rank_rows, rank_rows, 1)
    stacked, slot_of = partner_stack(coefs, stride)
    entries = lax.dynamic_index_in_dim(lists, cluster, 0, keepdims=False)
    chosen = jnp.maximum(entries, 0)
    coords = jnp.take(skeletons, chosen, axis=0)
    slots = jnp.clip(slot_of(chosen - cluster), 0, stacked.shape[0] - 1)
    values = jnp.take(stacked, slots, axis=0)
    rows_here = batched_far(own_coords, coords, values, entries >= 0) + jnp.dot(
        transfer_rows, above, precision=HIGHEST
    )
    return join_rows(rows_here, stride.bit_length() - 1, device)


def cluster_gather(block, device, clusters):
    gathered = block[None]
    for level in range(clusters.bit_length() - 1):
        bit_index = 3 + level
        other = from_partner(gathered, AX, bit_index)
        upper = device // 2**bit_index % 2
        gathered = jnp.where(
            upper == 0,
            jnp.concatenate([gathered, other], 0),
            jnp.concatenate([other, gathered], 0),
        )
    return gathered


def near_sum(own_points, near_entries, shipped, device):
    leaf_points = own_points.shape[1]
    point_rows = leaf_points + 3 * leaf_points // shipped.shape[1]

    def contribution(block, distance):
        listed = jnp.any(near_entries == device + distance)
        coords = block[leaf_points:point_rows].reshape(3, leaf_points)
        contrib = jnp.dot(
            kernel_block(own_points, coords), block[:leaf_points], precision=lax.Precision.HIGH
        )
        return jnp.where(listed, contrib, 0.0)

    total = contribution(shipped, 0)
    ahead = shipped
    behind = shipped
    rim = [None] * (2 * REACH + 1)
    rim[REACH] = shipped[point_rows:]
    for step in range(1, REACH + 1):
        ahead = from_behind(ahead, AX, 1)
        behind = from_behind(behind, AX, -1)
        rim[REACH - step] = ahead[point_rows:]
        rim[REACH + step] = behind[point_rows:]
        total = total + contribution(ahead, -step) + contribution(behind, step)
    return total, jnp.stack(rim)


def slot_of(distance):
    return distance + FAR_REACH - (distance > 0).astype(jnp.int32)


def middle_full(stacked, skeletons, lists, transfer, above, stride, device):
    cluster = device // stride
    own_coords = lax.dynamic_index_in_dim(skeletons, cluster, 0, keepdims=False)
    entries = lax.dynamic_index_in_dim(lists, cluster, 0, keepdims=False)
    chosen = jnp.maximum(entries, 0)
    coords = jnp.take(skeletons, chosen, axis=0)
    slots = jnp.clip(slot_of(chosen - cluster), 0, stacked.shape[0] - 1)
    values = jnp.take(stacked, slots, axis=0)
    return batched_far(own_coords, coords, values, entries >= 0) + jnp.dot(
        transfer, above, precision=HIGHEST
    )


OFFSETS = tuple(range(-FAR_REACH, 0)) + tuple(range(1, FAR_REACH + 1))


def device_coords(linear):
    return (linear // 8, linear // 4 % 2, linear // 2 % 2, linear % 2)


def exchange_kernel(
    clusters,
    top_ref,
    pair_ref,
    quad_ref,
    top_out,
    pair_out,
    quad_out,
    top_land,
    pair_land,
    quad_land,
    top_send,
    top_recv,
    pair_send,
    pair_recv,
    quad_send,
    quad_recv,
):
    me = lax.axis_index("cl")
    dev = lax.axis_index(AX)
    count = clusters * 8
    mesh_id = pl.DeviceIdType.MESH
    pair_land[...] = jnp.zeros(pair_land.shape, jnp.float32)
    quad_land[...] = jnp.zeros(quad_land.shape, jnp.float32)
    barrier = pltpu.get_barrier_semaphore()
    extra = (-12, -6, -4, -2, 2, 4, 6, 12)

    def inside(delta):
        return jnp.logical_and(dev + delta >= 0, dev + delta < count)

    def greet(step, carry):
        peer = lax.rem(me + step, clusters)
        pl.semaphore_signal(barrier, inc=1, device_id={"cl": peer}, device_id_type=mesh_id)
        return carry

    lax.fori_loop(1, clusters, greet, 0)
    for delta in extra:
        pl.semaphore_signal(
            barrier,
            inc=1,
            device_id=device_coords(lax.rem(dev + delta + count, count)),
            device_id_type=mesh_id,
        )
    pl.semaphore_wait(barrier, clusters - 1 + len(extra))

    def outgoing(step):
        peer = lax.rem(me + step, clusters)
        return pltpu.make_async_remote_copy(
            src_ref=top_ref,
            dst_ref=top_land.at[me],
            send_sem=top_send.at[step],
            recv_sem=top_recv.at[me],
            device_id={"cl": peer},
            device_id_type=mesh_id,
        )

    def incoming(step):
        source = lax.rem(me - step + clusters, clusters)
        return pltpu.make_async_remote_copy(
            src_ref=top_ref,
            dst_ref=top_land.at[source],
            send_sem=top_send.at[step],
            recv_sem=top_recv.at[source],
            device_id={"cl": source},
            device_id_type=mesh_id,
        )

    def partner_copy(src, land, send_sem, recv_sem, slot, target):
        return pltpu.make_async_remote_copy(
            src_ref=src,
            dst_ref=land.at[slot],
            send_sem=send_sem.at[slot],
            recv_sem=recv_sem.at[slot],
            device_id=device_coords(target),
            device_id_type=mesh_id,
        )

    partners = (
        (pair_ref, pair_land, pair_send, pair_recv, 2),
        (quad_ref, quad_land, quad_send, quad_recv, 4),
    )
    for src, land, send_sem, recv_sem, stride in partners:
        for slot, offset in enumerate(OFFSETS):

            @pl.when(inside(-offset * stride))
            def _():
                partner_copy(src, land, send_sem, recv_sem, slot, dev - offset * stride).start()

    def send(step, carry):
        outgoing(step).start()
        return carry

    lax.fori_loop(1, clusters, send, 0)
    top_land[me] = top_ref[...]

    def finish(step, carry):
        outgoing(step).wait_send()
        incoming(step).wait_recv()
        return carry

    lax.fori_loop(1, clusters, finish, 0)
    for src, land, send_sem, recv_sem, stride in partners:
        for slot, offset in enumerate(OFFSETS):

            @pl.when(inside(-offset * stride))
            def _():
                partner_copy(src, land, send_sem, recv_sem, slot, dev - offset * stride).wait_send()

            @pl.when(inside(offset * stride))
            def _():
                partner_copy(src, land, send_sem, recv_sem, slot, dev + offset * stride).wait_recv()

    top_out[...] = top_land[...]
    pair_out[...] = pair_land[...]
    quad_out[...] = quad_land[...]


def mates_kernel(block_ref, out_ref, landing, send_sem, recv_sem):
    dev = lax.axis_index(AX)
    member = dev % 8
    base = dev - member
    mesh_id = pl.DeviceIdType.MESH
    barrier = pltpu.get_barrier_semaphore()
    for step in range(1, 8):
        pl.semaphore_signal(
            barrier,
            inc=1,
            device_id=device_coords(base + lax.rem(member + step, 8)),
            device_id_type=mesh_id,
        )
    pl.semaphore_wait(barrier, 7)

    def outgoing(step):
        return pltpu.make_async_remote_copy(
            src_ref=block_ref,
            dst_ref=landing.at[member],
            send_sem=send_sem.at[step],
            recv_sem=recv_sem.at[member],
            device_id=device_coords(base + lax.rem(member + step, 8)),
            device_id_type=mesh_id,
        )

    def incoming(step):
        source = lax.rem(member - step + 8, 8)
        return pltpu.make_async_remote_copy(
            src_ref=block_ref,
            dst_ref=landing.at[source],
            send_sem=send_sem.at[step],
            recv_sem=recv_sem.at[source],
            device_id=device_coords(base + source),
            device_id_type=mesh_id,
        )

    for step in range(1, 8):
        outgoing(step).start()
    own = pltpu.make_async_copy(block_ref, landing.at[member], send_sem.at[0])
    own.start()
    own.wait()
    for step in range(1, 8):
        outgoing(step).wait_send()
        incoming(step).wait_recv()
    out_ref[...] = landing[...]


def mates_gather(block):
    rows, cols = block.shape
    vmem = pl.BlockSpec(memory_space=pltpu.VMEM)
    return pl.pallas_call(
        mates_kernel,
        out_shape=jax.ShapeDtypeStruct((8, rows, cols), jnp.float32),
        in_specs=[vmem],
        out_specs=vmem,
        scratch_shapes=[
            pltpu.VMEM((8, rows, cols), jnp.float32),
            pltpu.SemaphoreType.DMA((8,)),
            pltpu.SemaphoreType.DMA((8,)),
        ],
        compiler_params=pltpu.CompilerParams(collective_id=1, has_side_effects=True),
    )(block)


def exchange(top_block, coef_pair, coef_quad):
    clusters = lax.axis_size("cl")
    rows, cols = top_block.shape
    stack = (len(OFFSETS),) + coef_pair.shape
    vmem = pl.BlockSpec(memory_space=pltpu.VMEM)
    return pl.pallas_call(
        functools.partial(exchange_kernel, clusters),
        out_shape=(
            jax.ShapeDtypeStruct((clusters, rows, cols), jnp.float32),
            jax.ShapeDtypeStruct(stack, jnp.float32),
            jax.ShapeDtypeStruct(stack, jnp.float32),
        ),
        in_specs=[vmem] * 3,
        out_specs=(vmem, vmem, vmem),
        scratch_shapes=[
            pltpu.VMEM((clusters, rows, cols), jnp.float32),
            pltpu.VMEM(stack, jnp.float32),
            pltpu.VMEM(stack, jnp.float32),
            pltpu.SemaphoreType.DMA((clusters,)),
            pltpu.SemaphoreType.DMA((clusters,)),
            pltpu.SemaphoreType.DMA((len(OFFSETS),)),
            pltpu.SemaphoreType.DMA((len(OFFSETS),)),
            pltpu.SemaphoreType.DMA((len(OFFSETS),)),
            pltpu.SemaphoreType.DMA((len(OFFSETS),)),
        ],
        compiler_params=pltpu.CompilerParams(collective_id=0, has_side_effects=True),
    )(top_block, coef_pair, coef_quad)


def per_device(
    vectors,
    points,
    leaf_basis,
    transfer_leaf,
    transfer_pair,
    transfer_quad,
    skel_leaf,
    skel_pair,
    skel_quad,
    skel_top,
    near_list,
    far_leaf,
    far_pair,
    far_quad,
    far_top,
):
    leaf_points = vectors.shape[1]
    width = vectors.shape[2]
    rank = leaf_basis.shape[2]
    device = lax.axis_index(AX)
    own_points = points[0]
    coef_leaf = transposed_dot(leaf_basis[0], vectors[0])
    pair_matrix = join_rows(transfer_pair, 1, device)
    quad_matrix = join_rows(transfer_quad, 2, device)
    up_pair = transposed_dot(transfer_leaf[0], coef_leaf)
    up_quad = transposed_dot(pair_matrix, up_pair)
    up_top = transposed_dot(quad_matrix, up_quad)
    first = jnp.stack([up_pair, up_quad, up_top])
    first = first + from_partner(first, AX, 0)
    coef_pair = first[0]
    second = first[1:] + from_partner(first[1:], AX, 1)
    coef_quad = second[0]
    coef_top = second[1] + from_partner(second[1], AX, 2)
    shipped = jnp.concatenate(
        [vectors[0], own_points.reshape(3 * leaf_points // width, width), coef_leaf, skel_leaf[0]],
        axis=0,
    )
    near_field, leaf_rim = near_sum(own_points, near_list[0], shipped, device)
    top_cluster = device // 8
    top_member = device % 8
    share = width // 8
    top_cols_own = lax.dynamic_slice_in_dim(coef_top.T, top_member * share, share, 0)
    top_cols_own, near_field = lax.optimization_barrier((top_cols_own, near_field))
    top_t, pair_stack, quad_stack = exchange(top_cols_own, coef_pair, coef_quad)
    all_top = jnp.swapaxes(top_t, 1, 2)
    top_coords = lax.dynamic_index_in_dim(skel_top, top_cluster, 0, keepdims=False)
    top_entries = lax.dynamic_index_in_dim(far_top, top_cluster, 0, keepdims=False)
    top_chosen = jnp.maximum(top_entries, 0)
    top_cols = batched_far(
        top_coords,
        jnp.take(skel_top, top_chosen, axis=0),
        jnp.take(all_top, top_chosen, axis=0),
        top_entries >= 0,
    )
    local_top = mates_gather(top_cols.T).reshape(rank, width).T
    local_quad = middle_full(quad_stack, skel_quad, far_quad, quad_matrix, local_top, 4, device)
    local_pair = middle_full(pair_stack, skel_pair, far_pair, pair_matrix, local_quad, 2, device)
    leaf_entries = far_leaf[0]
    positions = jnp.clip(jnp.maximum(leaf_entries, 0) - device + REACH, 0, 2 * REACH)
    leaf_blocks = jnp.take(leaf_rim, positions, axis=0)
    local_leaf = batched_far(
        skel_leaf[0], leaf_blocks[:, rank:], leaf_blocks[:, :rank], leaf_entries >= 0
    ) + jnp.dot(transfer_leaf[0], local_pair, precision=HIGHEST)
    product = near_field + jnp.dot(leaf_basis[0], local_leaf, precision=lax.Precision.HIGH)
    return product[None]


def solution(mesh):
    count = mesh.devices.size
    grid = Mesh(mesh.devices.reshape(count // 8, 2, 2, 2), AX)
    spread = P(AX, None, None)
    rows = P(AX, None)
    placed = (
        spread,
        spread,
        spread,
        spread,
        rows,
        rows,
        spread,
        P(),
        P(),
        P(),
        rows,
        rows,
        P(),
        P(),
        P(),
    )
    return jax.shard_map(per_device, mesh=grid, in_specs=placed, out_specs=spread, check_vma=False)
```

```python
import functools

import jax
import jax.numpy as jnp
from jax import lax
from jax.experimental import pallas as pl
from jax.experimental.pallas import tpu as pltpu
from jax.sharding import Mesh
from jax.sharding import PartitionSpec as P

REACH = 8
FAR_REACH = 4


INV_FOUR_PI = 0.07957747154594767
DELTA_SQ = 0.01
HIGHEST = lax.Precision.HIGHEST

AX = ("cl", "q", "p", "c")
MEMBERS = ("q", "p", "c")


def from_partner(value, axis, bit):
    mask = 2**bit
    pairs = [(source, source ^ mask) for source in range(lax.axis_size(axis))]
    return lax.ppermute(value, axis, pairs)


def from_behind(block, axis, distance):
    devices = range(lax.axis_size(axis))
    route = [(i - distance, i) for i in devices if i - distance in devices]
    return lax.ppermute(block, axis, route)


def kernel_block(left_pts, right_pts):
    distance = jnp.zeros((left_pts.shape[1], right_pts.shape[1]), jnp.float32)
    for axis_id in range(3):
        offset_gap = left_pts[axis_id][:, None] - right_pts[axis_id][None, :]
        distance = distance + offset_gap * offset_gap
    return INV_FOUR_PI * lax.rsqrt(distance + DELTA_SQ)


def transposed_dot(matrix, values):
    return lax.dot_general(matrix, values, (((0,), (0,)), ((), ())), precision=HIGHEST)


def listed_sum(own_coords, entries, fetcher, width):

    def advance(running, partner):
        coords, values = fetcher(jnp.maximum(partner, 0))
        contrib = jnp.dot(kernel_block(own_coords, coords), values, precision=HIGHEST)
        return (running + jnp.where(partner >= 0, contrib, 0.0), None)

    start_value = jnp.zeros((own_coords.shape[1], width), jnp.float32)
    result, _ = lax.scan(advance, start_value, entries)
    return result


def batched_far(own_coords, coords, values, valid):
    count, _, span = coords.shape
    right = jnp.transpose(coords, (1, 0, 2)).reshape(3, count * span)
    masked = jnp.where(valid[:, None, None], values, 0.0)
    flat = masked.reshape(count * span, values.shape[2])
    return jnp.dot(kernel_block(own_coords, right), flat, precision=lax.Precision.HIGH)


def pair_total(partial_value, levels):
    for bit_index in range(levels):
        partial_value = partial_value + from_partner(partial_value, AX, bit_index)
    return partial_value


def join_rows(block, levels, device):
    for bit_index in range(levels):
        other = from_partner(block, AX, bit_index)
        upper = device // 2**bit_index % 2
        block = jnp.where(
            upper == 0, jnp.concatenate([block, other], 0), jnp.concatenate([other, block], 0)
        )
    return block


def window(shipped):
    gathered = []
    for distance in range(-REACH, REACH + 1):
        if distance == 0:
            gathered.append(shipped)
        else:
            gathered.append(from_behind(shipped, AX, -distance))
    return jnp.stack(gathered)


def partner_stack(coefs, stride):
    gathered = []
    for offset in list(range(-FAR_REACH, 0)) + list(range(1, FAR_REACH + 1)):
        gathered.append(from_behind(coefs, AX, -offset * stride))
    stacked = jnp.stack(gathered)

    def slot_of(distance):
        return distance + FAR_REACH - (distance > 0).astype(jnp.int32)

    return (stacked, slot_of)


def middle_level(coefs, skeletons, lists, transfer_rows, above, stride, device):
    rank_rows = coefs.shape[0] // stride
    cluster = device // stride
    member = device % stride
    own_full = lax.dynamic_index_in_dim(skeletons, cluster, 0, keepdims=False)
    own_coords = lax.dynamic_slice_in_dim(own_full, member * rank_rows, rank_rows, 1)
    stacked, slot_of = partner_stack(coefs, stride)
    entries = lax.dynamic_index_in_dim(lists, cluster, 0, keepdims=False)
    chosen = jnp.maximum(entries, 0)
    coords = jnp.take(skeletons, chosen, axis=0)
    slots = jnp.clip(slot_of(chosen - cluster), 0, stacked.shape[0] - 1)
    values = jnp.take(stacked, slots, axis=0)
    rows_here = batched_far(own_coords, coords, values, entries >= 0) + jnp.dot(
        transfer_rows, above, precision=HIGHEST
    )
    return join_rows(rows_here, stride.bit_length() - 1, device)


def cluster_gather(block, device, clusters):
    gathered = block[None]
    for level in range(clusters.bit_length() - 1):
        bit_index = 3 + level
        other = from_partner(gathered, AX, bit_index)
        upper = device // 2**bit_index % 2
        gathered = jnp.where(
            upper == 0,
            jnp.concatenate([gathered, other], 0),
            jnp.concatenate([other, gathered], 0),
        )
    return gathered


def near_sum(own_points, near_entries, shipped, device):
    leaf_points = own_points.shape[1]
    point_rows = leaf_points + 3 * leaf_points // shipped.shape[1]

    def contribution(block, distance):
        listed = jnp.any(near_entries == device + distance)
        coords = block[leaf_points:point_rows].reshape(3, leaf_points)
        def compute(coords, values):
            return jnp.dot(kernel_block(own_points, coords), values, precision=lax.Precision.HIGH)

        def skip(coords, values):
            return jnp.zeros(values.shape, jnp.float32)

        return lax.cond(listed, compute, skip, coords, block[:leaf_points])

    total = contribution(shipped, 0)
    ahead = shipped
    behind = shipped
    rim = [None] * (2 * REACH + 1)
    rim[REACH] = shipped[point_rows:]
    for step in range(1, REACH + 1):
        ahead = from_behind(ahead, AX, 1)
        behind = from_behind(behind, AX, -1)
        rim[REACH - step] = ahead[point_rows:]
        rim[REACH + step] = behind[point_rows:]
        total = total + contribution(ahead, -step) + contribution(behind, step)
    return total, jnp.stack(rim)


def slot_of(distance):
    return distance + FAR_REACH - (distance > 0).astype(jnp.int32)


def middle_full(stacked, skeletons, lists, transfer, above, stride, device):
    cluster = device // stride
    own_coords = lax.dynamic_index_in_dim(skeletons, cluster, 0, keepdims=False)
    entries = lax.dynamic_index_in_dim(lists, cluster, 0, keepdims=False)
    chosen = jnp.maximum(entries, 0)
    coords = jnp.take(skeletons, chosen, axis=0)
    slots = jnp.clip(slot_of(chosen - cluster), 0, stacked.shape[0] - 1)
    values = jnp.take(stacked, slots, axis=0)
    return batched_far(own_coords, coords, values, entries >= 0) + jnp.dot(
        transfer, above, precision=HIGHEST
    )


OFFSETS = tuple(range(-FAR_REACH, 0)) + tuple(range(1, FAR_REACH + 1))


def device_coords(linear):
    return (linear // 8, linear // 4 % 2, linear // 2 % 2, linear % 2)


def exchange_kernel(
    clusters,
    top_ref,
    pair_ref,
    quad_ref,
    top_out,
    pair_out,
    quad_out,
    top_land,
    pair_land,
    quad_land,
    top_send,
    top_recv,
    pair_send,
    pair_recv,
    quad_send,
    quad_recv,
):
    me = lax.axis_index("cl")
    dev = lax.axis_index(AX)
    count = clusters * 8
    mesh_id = pl.DeviceIdType.MESH
    pair_land[...] = jnp.zeros(pair_land.shape, jnp.float32)
    quad_land[...] = jnp.zeros(quad_land.shape, jnp.float32)
    barrier = pltpu.get_barrier_semaphore()
    extra = (-12, -6, -4, -2, 2, 4, 6, 12)

    def inside(delta):
        return jnp.logical_and(dev + delta >= 0, dev + delta < count)

    def greet(step, carry):
        peer = lax.rem(me + step, clusters)
        pl.semaphore_signal(barrier, inc=1, device_id={"cl": peer}, device_id_type=mesh_id)
        return carry

    lax.fori_loop(1, clusters, greet, 0)
    for delta in extra:
        pl.semaphore_signal(
            barrier,
            inc=1,
            device_id=device_coords(lax.rem(dev + delta + count, count)),
            device_id_type=mesh_id,
        )
    pl.semaphore_wait(barrier, clusters - 1 + len(extra))

    def outgoing(step):
        peer = lax.rem(me + step, clusters)
        return pltpu.make_async_remote_copy(
            src_ref=top_ref,
            dst_ref=top_land.at[me],
            send_sem=top_send.at[step],
            recv_sem=top_recv.at[me],
            device_id={"cl": peer},
            device_id_type=mesh_id,
        )

    def incoming(step):
        source = lax.rem(me - step + clusters, clusters)
        return pltpu.make_async_remote_copy(
            src_ref=top_ref,
            dst_ref=top_land.at[source],
            send_sem=top_send.at[step],
            recv_sem=top_recv.at[source],
            device_id={"cl": source},
            device_id_type=mesh_id,
        )

    def partner_copy(src, land, send_sem, recv_sem, slot, target):
        return pltpu.make_async_remote_copy(
            src_ref=src,
            dst_ref=land.at[slot],
            send_sem=send_sem.at[slot],
            recv_sem=recv_sem.at[slot],
            device_id=device_coords(target),
            device_id_type=mesh_id,
        )

    partners = (
        (pair_ref, pair_land, pair_send, pair_recv, 2),
        (quad_ref, quad_land, quad_send, quad_recv, 4),
    )
    for src, land, send_sem, recv_sem, stride in partners:
        for slot, offset in enumerate(OFFSETS):

            @pl.when(inside(-offset * stride))
            def _():
                partner_copy(src, land, send_sem, recv_sem, slot, dev - offset * stride).start()

    def send(step, carry):
        outgoing(step).start()
        return carry

    lax.fori_loop(1, clusters, send, 0)
    top_land[me] = top_ref[...]

    def finish(step, carry):
        outgoing(step).wait_send()
        incoming(step).wait_recv()
        return carry

    lax.fori_loop(1, clusters, finish, 0)
    for src, land, send_sem, recv_sem, stride in partners:
        for slot, offset in enumerate(OFFSETS):

            @pl.when(inside(-offset * stride))
            def _():
                partner_copy(src, land, send_sem, recv_sem, slot, dev - offset * stride).wait_send()

            @pl.when(inside(offset * stride))
            def _():
                partner_copy(src, land, send_sem, recv_sem, slot, dev + offset * stride).wait_recv()

    top_out[...] = top_land[...]
    pair_out[...] = pair_land[...]
    quad_out[...] = quad_land[...]


def mates_kernel(block_ref, out_ref, landing, send_sem, recv_sem):
    dev = lax.axis_index(AX)
    member = dev % 8
    base = dev - member
    mesh_id = pl.DeviceIdType.MESH
    barrier = pltpu.get_barrier_semaphore()
    for step in range(1, 8):
        pl.semaphore_signal(
            barrier,
            inc=1,
            device_id=device_coords(base + lax.rem(member + step, 8)),
            device_id_type=mesh_id,
        )
    pl.semaphore_wait(barrier, 7)

    def outgoing(step):
        return pltpu.make_async_remote_copy(
            src_ref=block_ref,
            dst_ref=landing.at[member],
            send_sem=send_sem.at[step],
            recv_sem=recv_sem.at[member],
            device_id=device_coords(base + lax.rem(member + step, 8)),
            device_id_type=mesh_id,
        )

    def incoming(step):
        source = lax.rem(member - step + 8, 8)
        return pltpu.make_async_remote_copy(
            src_ref=block_ref,
            dst_ref=landing.at[source],
            send_sem=send_sem.at[step],
            recv_sem=recv_sem.at[source],
            device_id=device_coords(base + source),
            device_id_type=mesh_id,
        )

    for step in range(1, 8):
        outgoing(step).start()
    own = pltpu.make_async_copy(block_ref, landing.at[member], send_sem.at[0])
    own.start()
    own.wait()
    for step in range(1, 8):
        outgoing(step).wait_send()
        incoming(step).wait_recv()
    out_ref[...] = landing[...]


def mates_gather(block):
    rows, cols = block.shape
    vmem = pl.BlockSpec(memory_space=pltpu.VMEM)
    return pl.pallas_call(
        mates_kernel,
        out_shape=jax.ShapeDtypeStruct((8, rows, cols), jnp.float32),
        in_specs=[vmem],
        out_specs=vmem,
        scratch_shapes=[
            pltpu.VMEM((8, rows, cols), jnp.float32),
            pltpu.SemaphoreType.DMA((8,)),
            pltpu.SemaphoreType.DMA((8,)),
        ],
        compiler_params=pltpu.CompilerParams(collective_id=1, has_side_effects=True),
    )(block)


def exchange(top_block, coef_pair, coef_quad):
    clusters = lax.axis_size("cl")
    rows, cols = top_block.shape
    stack = (len(OFFSETS),) + coef_pair.shape
    vmem = pl.BlockSpec(memory_space=pltpu.VMEM)
    return pl.pallas_call(
        functools.partial(exchange_kernel, clusters),
        out_shape=(
            jax.ShapeDtypeStruct((clusters, rows, cols), jnp.float32),
            jax.ShapeDtypeStruct(stack, jnp.float32),
            jax.ShapeDtypeStruct(stack, jnp.float32),
        ),
        in_specs=[vmem] * 3,
        out_specs=(vmem, vmem, vmem),
        scratch_shapes=[
            pltpu.VMEM((clusters, rows, cols), jnp.float32),
            pltpu.VMEM(stack, jnp.float32),
            pltpu.VMEM(stack, jnp.float32),
            pltpu.SemaphoreType.DMA((clusters,)),
            pltpu.SemaphoreType.DMA((clusters,)),
            pltpu.SemaphoreType.DMA((len(OFFSETS),)),
            pltpu.SemaphoreType.DMA((len(OFFSETS),)),
            pltpu.SemaphoreType.DMA((len(OFFSETS),)),
            pltpu.SemaphoreType.DMA((len(OFFSETS),)),
        ],
        compiler_params=pltpu.CompilerParams(collective_id=0, has_side_effects=True),
    )(top_block, coef_pair, coef_quad)


def per_device(
    vectors,
    points,
    leaf_basis,
    transfer_leaf,
    transfer_pair,
    transfer_quad,
    skel_leaf,
    skel_pair,
    skel_quad,
    skel_top,
    near_list,
    far_leaf,
    far_pair,
    far_quad,
    far_top,
):
    leaf_points = vectors.shape[1]
    width = vectors.shape[2]
    rank = leaf_basis.shape[2]
    device = lax.axis_index(AX)
    own_points = points[0]
    coef_leaf = transposed_dot(leaf_basis[0], vectors[0])
    pair_matrix = join_rows(transfer_pair, 1, device)
    quad_matrix = join_rows(transfer_quad, 2, device)
    up_pair = transposed_dot(transfer_leaf[0], coef_leaf)
    up_quad = transposed_dot(pair_matrix, up_pair)
    up_top = transposed_dot(quad_matrix, up_quad)
    first = jnp.stack([up_pair, up_quad, up_top])
    first = first + from_partner(first, AX, 0)
    coef_pair = first[0]
    second = first[1:] + from_partner(first[1:], AX, 1)
    coef_quad = second[0]
    coef_top = second[1] + from_partner(second[1], AX, 2)
    shipped = jnp.concatenate(
        [vectors[0], own_points.reshape(3 * leaf_points // width, width), coef_leaf, skel_leaf[0]],
        axis=0,
    )
    near_field, leaf_rim = near_sum(own_points, near_list[0], shipped, device)
    top_cluster = device // 8
    top_member = device % 8
    share = width // 8
    top_cols_own = lax.dynamic_slice_in_dim(coef_top.T, top_member * share, share, 0)
    top_cols_own, near_field = lax.optimization_barrier((top_cols_own, near_field))
    top_t, pair_stack, quad_stack = exchange(top_cols_own, coef_pair, coef_quad)
    all_top = jnp.swapaxes(top_t, 1, 2)
    top_coords = lax.dynamic_index_in_dim(skel_top, top_cluster, 0, keepdims=False)
    top_entries = lax.dynamic_index_in_dim(far_top, top_cluster, 0, keepdims=False)
    top_chosen = jnp.maximum(top_entries, 0)
    top_cols = batched_far(
        top_coords,
        jnp.take(skel_top, top_chosen, axis=0),
        jnp.take(all_top, top_chosen, axis=0),
        top_entries >= 0,
    )
    local_top = mates_gather(top_cols.T).reshape(rank, width).T
    local_quad = middle_full(quad_stack, skel_quad, far_quad, quad_matrix, local_top, 4, device)
    local_pair = middle_full(pair_stack, skel_pair, far_pair, pair_matrix, local_quad, 2, device)
    leaf_entries = far_leaf[0]
    positions = jnp.clip(jnp.maximum(leaf_entries, 0) - device + REACH, 0, 2 * REACH)
    leaf_blocks = jnp.take(leaf_rim, positions, axis=0)
    local_leaf = batched_far(
        skel_leaf[0], leaf_blocks[:, rank:], leaf_blocks[:, :rank], leaf_entries >= 0
    ) + jnp.dot(transfer_leaf[0], local_pair, precision=HIGHEST)
    product = near_field + jnp.dot(leaf_basis[0], local_leaf, precision=lax.Precision.HIGH)
    return product[None]


def solution(mesh):
    count = mesh.devices.size
    grid = Mesh(mesh.devices.reshape(count // 8, 2, 2, 2), AX)
    spread = P(AX, None, None)
    rows = P(AX, None)
    placed = (
        spread,
        spread,
        spread,
        spread,
        rows,
        rows,
        spread,
        P(),
        P(),
        P(),
        rows,
        rows,
        P(),
        P(),
        P(),
    )
    return jax.shard_map(per_device, mesh=grid, in_specs=placed, out_specs=spread, check_vma=False)
```
